256 devices in a mesh: gx: 8 (over y, core), gy: 16 (over x, z_hi), gz: 2 (over z_lo).
Axes of the slice: x: 4, y: 4, z: 8 (z_hi: 4, z_lo: 2; z = z_hi * 2 + z_lo), core: 2. Of those that a mesh axis runs over, the one named last changes fastest.
Arguments:
- force_u: float32 [16, 64, 32, 1024], P('gz', None, 'gy', 'gx'), may hold values from -6 to 6
- force_p: float32 [16, 16, 32, 1024], P('gz', None, 'gy', 'gx'), may hold values from -6 to 6
- cellmask: int32 [16, 32, 1024], P('gz', 'gy', 'gx'), may hold values 0 or 1
- layer_mats: int32 [16], P('gz'), may hold values from 0 to 3
- kblocks: bfloat16 [4, 7, 64, 64], replicated
- bcoup: float32 [4, 16, 64], replicated, may hold values from -0.75 to 0.75
- sinv: float32 [8, 16, 16, 16], replicated, may hold values from -0.75 to 0.75
- band_offsets: int32 [8], replicated, may hold values from -15 to 15, as said below
- spectrum: float32 [2], replicated, may hold values from 0.25 to 1.9, as said below
Outputs:
- displacement: float32 [16, 64, 32, 1024], P('gz', None, 'gy', 'gx')
- pressure: float32 [16, 16, 32, 1024], P('gz', None, 'gy', 'gx')
The draws below stay inside these ranges and needn't reach their ends.
Inputs may be any that keep to these rules, and one draw needn't show every extreme that they name: `band_offsets`: the offsets are distinct; 0, 15 and -(15) are among them. `spectrum`: the lower bound is positive and below the upper bound.
All inputs are finite; a program needn't handle non-finite values. No bound on the sum of `cellmask` on one device may be relied on, other than what follows from the above.
Results may differ from the reference program's by a relative error of at most 0.0028.
The reference program's roundings to bfloat16 on the way count: a program that leaves them out, or rounds other values in their place, can miss the bound.
Values may be sent and summed in bfloat16 or wider, within the bound.
No kernel may reach another device: no remote copies, remote signals or barrier semaphores. Data moves between devices by JAX's collectives and lax.ppermute only.
A program may use at most 64 MiB of HBM per device.

```python
import jax
import jax.numpy as jnp
from jax import lax

BU = 64
PB = 16
MATS = 4
NBAND = 8
SWEEPS = 4
OUTER = 2
NX = 1024
NY = 32
NZ = 16


def draw_kblocks(key, part):
    noise_key = jax.random.fold_in(key, 11)
    diag_key = jax.random.fold_in(key, 12)
    noise = jax.random.normal(noise_key, (MATS, 7, BU, BU), jnp.float32)
    diagonal = jax.random.uniform(diag_key, (MATS, BU), jnp.float32, 0.8, 1.2)
    centre = (jnp.arange(7) == 0).astype(jnp.float32)[None, :, None, None]
    scales = 0.03 * centre + 0.02 * (1.0 - centre)
    identity = jnp.eye(BU, dtype=jnp.float32)[None, None]
    blocks = noise * scales + centre * identity * diagonal[:, None, :, None]
    return blocks.astype(jnp.bfloat16)


def draw_band_offsets(key, part):
    pick_key = jax.random.fold_in(key, 21)
    order_key = jax.random.fold_in(key, 22)
    inner = jnp.arange(1, NZ - 1, dtype=jnp.int32)
    candidates = jnp.concatenate([inner, -inner])
    chosen = jax.random.permutation(pick_key, candidates)[:NBAND - 3]
    fixed = jnp.array([0, NZ - 1, 1 - NZ], dtype=jnp.int32)
    return jax.random.permutation(order_key, jnp.concatenate([fixed, chosen])).astype(jnp.int32)


def draw_spectrum(key, part):
    low_key = jax.random.fold_in(key, 31)
    high_key = jax.random.fold_in(key, 32)
    lower = jax.random.uniform(low_key, (1,), jnp.float32, 0.25, 0.4)
    upper = jax.random.uniform(high_key, (1,), jnp.float32, 1.6, 1.9)
    return jnp.concatenate([lower, upper]).astype(jnp.float32)


def touch_ends(drawn, stream_key, least, high):
    extent = drawn.shape
    spot = [jax.random.randint(jax.random.fold_in(stream_key, axis), (), 0, extent[axis]) for axis in range(len(extent))]
    drawn = drawn.at[tuple(spot)].set(least)
    longest = extent.index(max(extent))
    spot[longest] = (spot[longest] + 1) % extent[longest]
    return drawn.at[tuple(spot)].set(high)


def block_scale(own_key, extent, split, smallest, top_value):
    gain = 1.0
    for axis_at, blocks in split:
        heights = jax.random.uniform(jax.random.fold_in(jax.random.fold_in(own_key, 6), axis_at), (blocks,), jnp.float32, smallest / len(split), top_value / len(split))
        gain = gain * jnp.repeat(jnp.exp(heights), extent[axis_at] // blocks).reshape((-1,) + (1,) * (len(extent) - 1 - axis_at))
    return gain


def normal_values(stream_key, extent, spread, bound, cuts=(), kind=jnp.bfloat16):
    values = jax.random.normal(stream_key, extent, jnp.float32) * spread
    if len(cuts) > 0:
        values = block_scale(stream_key, extent, cuts, -0.22, 0.18) * values
    return jnp.clip(values, min=-bound, max=bound).astype(kind)


def setup_inputs(seed: int = 0) -> dict:
    key_list = jax.random.split(jax.random.key(seed), 10)
    force_u = normal_values(key_list[0], (NZ, BU, NY, NX), 1.0, 6.0, ((0, 2), (2, 16), (3, 8)), jnp.float32)
    force_p = normal_values(key_list[1], (NZ, PB, NY, NX), 1.0, 6.0, ((0, 2), (2, 16), (3, 8)), jnp.float32)
    cellmask = touch_ends((jax.random.randint(key_list[2], (NZ, NY, NX), 0, 4) < 3).astype(jnp.int32), jax.random.fold_in(key_list[2], 1), 0, 1)
    layer_mats = touch_ends(jax.random.randint(key_list[3], (NZ,), 0, MATS), jax.random.fold_in(key_list[3], 1), 0, MATS - 1).astype(jnp.int32)
    kblocks = draw_kblocks(jax.random.fold_in(key_list[9], 71), 0)
    bcoup = normal_values(key_list[5], (MATS, PB, BU), BU ** -0.5, 0.75, (), jnp.float32)
    sinv = normal_values(key_list[6], (NBAND, NZ, PB, PB), (PB * 4) ** -0.5, 0.75, (), jnp.float32)
    band_offsets = draw_band_offsets(jax.random.fold_in(key_list[9], 71), 0)
    spectrum = draw_spectrum(jax.random.fold_in(key_list[9], 71), 0)
    return {"force_u": force_u, "force_p": force_p, "cellmask": cellmask, "layer_mats": layer_mats, "kblocks": kblocks, "bcoup": bcoup, "sinv": sinv, "band_offsets": band_offsets, "spectrum": spectrum}


HIGHEST = lax.Precision.HIGHEST


def stencil(field, tables, weight):
    rounded = lax.optimization_barrier(field.astype(jnp.bfloat16)).astype(jnp.float32)
    padded = jnp.pad(rounded, ((1, 1), (0, 0), (1, 1), (1, 1)))

    def layer(index):
        slab = lax.dynamic_slice_in_dim(padded, index, 3, 0)
        parts = jnp.stack([slab[1, :, 1:-1, 1:-1], slab[0, :, 1:-1, 1:-1], slab[2, :, 1:-1, 1:-1],
                           slab[1, :, :-2, 1:-1], slab[1, :, 2:, 1:-1],
                           slab[1, :, 1:-1, :-2], slab[1, :, 1:-1, 2:]], axis=0)
        table = lax.dynamic_index_in_dim(tables, index, 0, keepdims=False)
        return jnp.einsum('dij,djyx->iyx', table, parts, precision=HIGHEST)

    result = lax.map(layer, jnp.arange(NZ).astype(jnp.int32))
    return result * weight[:, None]


def couple(field, coupling, weight):
    return jnp.einsum('zpj,zjyx->zpyx', coupling, field, precision=HIGHEST) * weight[:, None]


def couple_back(field, coupling, weight):
    return jnp.einsum('zpj,zpyx->zjyx', coupling, field, precision=HIGHEST) * weight[:, None]


def schur(field, sinv, band_offsets, weight):
    depth = field.shape[0]
    padded = jnp.pad(field, ((depth, depth), (0, 0), (0, 0), (0, 0)))
    total = jnp.zeros(field.shape, jnp.float32)
    for band in range(NBAND):
        begin = (band_offsets[band] + depth).astype(jnp.int32)
        shifted = lax.dynamic_slice_in_dim(padded, begin, depth, 0)
        total = total + jnp.einsum('zab,zbyx->zayx', sinv[band], shifted, precision=HIGHEST)
    return total * weight[:, None]


def chebyshev(residue, apply_op, spectrum):
    lower, upper = spectrum[0], spectrum[1]
    theta = (upper + lower) / 2.0
    delta = (upper - lower) / 2.0
    sigma = theta / delta
    rho = 1.0 / sigma
    direction = residue / theta
    solution = jnp.zeros_like(residue)
    for sweep in range(SWEEPS):
        solution = solution + direction
        if sweep + 1 < SWEEPS:
            residue = residue - apply_op(direction)
            rho_next = 1.0 / (2.0 * sigma - rho)
            direction = rho_next * rho * direction + (2.0 * rho_next / delta) * residue
            rho = rho_next
    return solution


def reference(force_u, force_p, cellmask, layer_mats, kblocks, bcoup, sinv, band_offsets, spectrum):
    weight = cellmask.astype(jnp.float32)
    tables = kblocks[layer_mats].astype(jnp.float32)
    coupling = bcoup[layer_mats]
    force_disp = force_u * weight[:, None]
    force_pres = force_p * weight[:, None]

    def apply_op(field):
        return stencil(field, tables, weight)

    displacement = jnp.zeros_like(force_disp)
    pressure = jnp.zeros_like(force_pres)
    for outer in range(OUTER):
        if outer == 0:
            res_disp = force_disp
            res_pres = force_pres
        else:
            res_disp = force_disp - apply_op(displacement) - couple_back(pressure, coupling, weight)
            res_pres = force_pres - couple(displacement, coupling, weight)
        step_disp = chebyshev(res_disp, apply_op, spectrum)
        step_pres = schur(couple(step_disp, coupling, weight) - res_pres, sinv, band_offsets, weight)
        displacement = displacement + step_disp
        pressure = pressure + step_pres
    return displacement, pressure
```

```python
import jax
import jax.numpy as jnp
from jax import lax
from jax.experimental import pallas as pl
from jax.experimental.pallas import tpu as pltpu
from jax.sharding import PartitionSpec as P

SWEEPS = 4
ALL = ("gx", "gy", "gz")
PLANE = ("gy", "gz")
HIGHEST = lax.Precision.HIGHEST
NZ, BU, PB, NY = 16, 64, 16, 32
ZL, YL, XL, CH = 8, 2, 4, 32
RU, RP = NZ * BU, NZ * PB
HU, HP = ZL * BU, ZL * PB
WIDE = HU + HP
LANES = 128
BLOCKS = WIDE // LANES
STEP = 2 * BLOCKS * 8
f32, bf16 = jnp.float32, jnp.bfloat16


def place(variant, k):
    if variant == 0:
        cx, r = k // 8, k % 8
        cz = r if cx % 2 == 0 else 7 - r
    elif variant == 1:
        cz, r = k // 4, k % 4
        cx = 3 - r if cz % 2 == 0 else r
    elif variant == 2:
        q, r = k // 8, k % 8
        cx = 3 - q
        cz = 7 - r if q % 2 == 0 else r
    else:
        q, r = k // 4, k % 4
        cz = 7 - q
        cx = r if q % 2 == 0 else 3 - r
    return cx * 8 + cz


def slot_of(variant, k):
    a, b, c, d = (place(v, k) for v in range(4))
    return jnp.where(
        variant < 2, jnp.where(variant == 0, a, b), jnp.where(variant == 2, c, d)
    )


def chain():
    order = [g * CH + place(g % 4, k) for g in range(8) for k in range(CH)]
    up = [(order[i], order[i + 1]) for i in range(len(order) - 1)]
    return up, [(b, a) for a, b in up]


def pack_kernel(var_ref, fu_ref, fp_ref, mask_ref, out_ref, flip_ref):
    for yl in range(YL):
        pressure = []
        for z in range(ZL):
            live = mask_ref[pl.ds(z * YL + yl, 1), :] != 0
            weight = live.astype(f32)
            fp = fp_ref[pl.ds(z * PB * YL + yl, PB, stride=YL), :] * weight
            last = lax.broadcasted_iota(jnp.int32, (PB, LANES), 0) == PB - 1
            dead = jnp.broadcast_to(weight, (PB, LANES)) == 0.0
            pressure.append(jnp.where(jnp.logical_and(last, dead), jnp.inf, fp))
        for b in range(BLOCKS - 1):
            pair = []
            for z in (2 * b, 2 * b + 1):
                weight = (mask_ref[pl.ds(z * YL + yl, 1), :] != 0).astype(f32)
                pair.append(fu_ref[pl.ds(z * BU * YL + yl, BU, stride=YL), :] * weight)
            flip_ref[yl, b] = jnp.concatenate(pair, axis=0).T
        flip_ref[yl, BLOCKS - 1] = jnp.concatenate(pressure, axis=0).T
    variant = var_ref[0]
    for k in range(CH):
        dest = slot_of(variant, k) * BLOCKS
        for b in range(BLOCKS):
            out_ref[dest + b] = jnp.concatenate(
                [flip_ref[yl, b, pl.ds(XL * k, XL), :] for yl in range(YL)], axis=0
            )


def spread_kernel(coef_ref, got_ref, fu_ref, fp_ref, mask_ref, send_ref, rows_ref):
    theta_inv = coef_ref[0]
    for half in range(2):
        for b in range(BLOCKS):
            for x in range(XL):
                for yl in range(YL):
                    rows_ref[b, pl.ds(x * NY + yl, CH // 2, stride=YL), :] = got_ref[
                        pl.ds((half * BLOCKS + b) * 8 + yl * XL + x, CH // 2, stride=STEP), :
                    ]
            flat = rows_ref[b].T
            if b < BLOCKS - 1:
                at = pl.ds(half * HU + b * LANES, LANES)
                fu_ref[at, :] = flat
                send_ref[at, :] = (flat * theta_inv).astype(bf16)
            else:
                fp_ref[pl.ds(half * HP, HP), :] = flat
    marks = fp_ref[pl.ds(PB - 1, NZ, stride=PB), :]
    weight = jnp.where(marks == jnp.inf, 0.0, 1.0)
    mask_ref[...] = weight
    send_ref[pl.ds(RU, NZ), :] = weight.astype(bf16)
    fp_ref[...] = jnp.where(fp_ref[...] == jnp.inf, 0.0, fp_ref[...])


def lane_iota(rows):
    return lax.broadcasted_iota(jnp.int32, (rows, LANES), 1)


def neighbours(parts, which):
    own = parts[which]
    lane = lane_iota(BU)
    y = lane % NY
    zero = jnp.zeros_like(own)
    below_y = jnp.where(y == 0, zero, pltpu.roll(own, 1, 1))
    above_y = jnp.where(y == NY - 1, zero, pltpu.roll(own, LANES - 1, 1))
    below_x = pltpu.roll(own, NY, 1)
    if which > 0:
        below_x = jnp.where(lane < NY, pltpu.roll(parts[which - 1], NY, 1), below_x)
    above_x = pltpu.roll(own, LANES - NY, 1)
    if which < 2:
        above_x = jnp.where(
            lane >= LANES - NY, pltpu.roll(parts[which + 1], LANES - NY, 1), above_x
        )
    return jnp.concatenate([below_y, above_y, below_x, above_x], axis=0)


def apply_layer(z, lm_ref, table_ref, w_ref, blocks):
    table = table_ref[lm_ref[z]]
    first = blocks[0] * LANES
    width = len(blocks) * LANES
    parts = [
        w_ref[pl.ds(z * BU + BU, BU), pl.ds(b * LANES, LANES)] for b in range(3)
    ]
    side = jnp.concatenate([neighbours(parts, b) for b in blocks], axis=1)
    column = w_ref[pl.ds(z * BU, 3 * BU), pl.ds(first, width)]
    return jnp.dot(table[:, : 3 * BU], column, preferred_element_type=f32) + jnp.dot(
        table[:, 3 * BU :], side, preferred_element_type=f32
    )


def sweeps(coef_ref, lm_ref, table_ref, mask_ref, d_ref, r_ref, s_ref, w_refs, plan):
    for k, blocks in enumerate(plan):
        keep, scale = coef_ref[2 + 2 * k], coef_ref[3 + 2 * k]
        old, new = w_refs[k % 2], w_refs[(k + 1) % 2]
        lanes = pl.ds(blocks[0] * LANES, len(blocks) * LANES)

        def layer(z, carry):
            z64 = pl.multiple_of(z * BU, BU)
            rows = pl.ds(z64, BU)
            product = apply_layer(z, lm_ref, table_ref, old, blocks)
            r = r_ref[rows, lanes] - product * mask_ref[z, pl.ds(0, 1), lanes]
            d = keep * d_ref[rows, lanes] + scale * r
            s = s_ref[rows, lanes] + d
            r_ref[rows, lanes] = r
            d_ref[rows, lanes] = d
            s_ref[rows, lanes] = s
            if k + 1 < len(plan):
                new[pl.ds(z64 + BU, BU), lanes] = d.astype(bf16)
            return carry

        lax.fori_loop(0, NZ, layer, 0)


def widen(wide_ref, mask_ref, low_ref, high_ref):
    low = low_ref[pl.ds(RU, NZ), :].astype(f32)
    high = high_ref[pl.ds(RU, NZ), :].astype(f32)
    whole = jnp.concatenate([low, mask_ref[...], high], axis=1)
    for z in range(NZ):
        wide_ref[z] = jnp.broadcast_to(whole[z : z + 1], (8, 3 * LANES))


def fill(own_r, thetas, own_w, low, high, d_ref, r_ref, s_ref, w_ref):
    theta_inv, theta = thetas
    edge = jnp.zeros((BU, 3 * LANES), bf16)
    w_ref[pl.ds(0, BU), :] = edge
    w_ref[pl.ds(RU + BU, BU), :] = edge
    for at, src in ((0, low), (2, high)):
        w = src[pl.ds(0, RU), :]
        lanes = pl.ds(at * LANES, LANES)
        w_ref[pl.ds(BU, RU), lanes] = w
        d = w.astype(f32)
        d_ref[:, lanes] = d
        s_ref[:, lanes] = d
        r_ref[:, lanes] = d * theta
    lanes = pl.ds(LANES, LANES)
    d = own_r[...] * theta_inv
    r_ref[:, lanes] = own_r[...]
    d_ref[:, lanes] = d
    s_ref[:, lanes] = d
    w_ref[pl.ds(BU, RU), lanes] = own_w[pl.ds(0, RU), :]


def first_kernel(coef_ref, lm_ref, table_ref, coup_ref, coup_t_ref, schur_ref,
                 fu_ref, fp_ref, mask_ref, own_ref, low_ref, high_ref,
                 ru_ref, du_ref, dp_ref, q_ref, send_ref,
                 wide_ref, d_ref, r_ref, s_ref, wa_ref, wb_ref):
    thetas = (coef_ref[0], coef_ref[1])
    widen(wide_ref, mask_ref, low_ref, high_ref)
    fill(fu_ref, thetas, own_ref, low_ref, high_ref, d_ref, r_ref, s_ref, wa_ref)
    wb_ref[pl.ds(0, BU), :] = jnp.zeros((BU, 3 * LANES), bf16)
    wb_ref[pl.ds(RU + BU, BU), :] = jnp.zeros((BU, 3 * LANES), bf16)
    full = (0, 1, 2)
    sweeps(coef_ref, lm_ref, table_ref, wide_ref, d_ref, r_ref, s_ref, (wa_ref, wb_ref),
           (full, full, full))
    own = pl.ds(LANES, LANES)
    wa_ref[pl.ds(BU, RU), :] = s_ref[...].astype(bf16)
    du_ref[...] = s_ref[:, own]

    def gather(z, carry):
        du = du_ref[pl.ds(pl.multiple_of(z * BU, BU), BU), :]
        here = pl.ds(pl.multiple_of(z * PB, PB), PB)
        q = jnp.dot(coup_ref[lm_ref[z]], du, precision=HIGHEST, preferred_element_type=f32)
        q_ref[here, :] = q * mask_ref[pl.ds(z, 1), :] - fp_ref[here, :]
        return carry

    lax.fori_loop(0, NZ, gather, 0)
    dp_ref[...] = jnp.dot(schur_ref[...], q_ref[...], precision=HIGHEST,
                          preferred_element_type=f32)

    def finish(z, carry):
        here = pl.ds(pl.multiple_of(z * PB, PB), PB)
        rows = pl.ds(pl.multiple_of(z * BU, BU), BU)
        weight = mask_ref[pl.ds(z, 1), :]
        dp = dp_ref[here, :] * weight
        dp_ref[here, :] = dp
        back = jnp.dot(coup_t_ref[lm_ref[z]], dp, precision=HIGHEST,
                       preferred_element_type=f32)
        product = apply_layer(z, lm_ref, table_ref, wa_ref, (1,))
        ru = fu_ref[rows, :] - product * weight - back * weight
        ru_ref[rows, :] = ru
        send_ref[rows, :] = (ru * thetas[0]).astype(bf16)
        return carry

    lax.fori_loop(0, NZ, finish, 0)


def second_kernel(coef_ref, lm_ref, table_ref, coup_ref, schur_ref,
                  fu_ref, mask_ref, ru_ref, du_ref, dp_ref, q_ref, own_ref, low_ref,
                  high_ref, mlow_ref, mhigh_ref, out_ref,
                  wide_ref, d_ref, r_ref, s_ref, wa_ref, wb_ref, p_ref, rows_ref, sort_ref):
    thetas = (coef_ref[0], coef_ref[1])
    widen(wide_ref, mask_ref, mlow_ref, mhigh_ref)
    fill(ru_ref, thetas, own_ref, low_ref, high_ref, d_ref, r_ref, s_ref, wa_ref)
    wb_ref[pl.ds(0, BU), :] = jnp.zeros((BU, 3 * LANES), bf16)
    wb_ref[pl.ds(RU + BU, BU), :] = jnp.zeros((BU, 3 * LANES), bf16)
    full = (0, 1, 2)
    sweeps(coef_ref, lm_ref, table_ref, wide_ref, d_ref, r_ref, s_ref, (wa_ref, wb_ref),
           (full, full, (1,)))
    own = pl.ds(LANES, LANES)

    def gather(z, carry):
        rows = pl.ds(pl.multiple_of(z * BU, BU), BU)
        here = pl.ds(pl.multiple_of(z * PB, PB), PB)
        du = s_ref[rows, own]
        q = jnp.dot(coup_ref[lm_ref[z]], du, precision=HIGHEST, preferred_element_type=f32)
        p_ref[here, :] = q * mask_ref[pl.ds(z, 1), :] + q_ref[here, :]
        return carry

    lax.fori_loop(0, NZ, gather, 0)
    p_ref[...] = jnp.dot(schur_ref[...], p_ref[...], precision=HIGHEST,
                         preferred_element_type=f32)
    for half in range(2):
        for b in range(BLOCKS):
            if b < BLOCKS - 1:
                rows = pl.ds(half * HU + b * LANES, LANES)
                flat = s_ref[rows, own] + du_ref[rows, :] - fu_ref[rows, :]
            else:
                pressure = []
                for z in range(half * ZL, half * ZL + ZL):
                    here = pl.ds(z * PB, PB)
                    dp = p_ref[here, :] * mask_ref[pl.ds(z, 1), :]
                    pressure.append(dp + dp_ref[here, :])
                flat = jnp.concatenate(pressure, axis=0)
            rows_ref[b] = flat.T
            for x in range(XL):
                for yl in range(YL):
                    sort_ref[
                        pl.ds((half * BLOCKS + b) * 8 + yl * XL + x, CH // 2, stride=STEP), :
                    ] = rows_ref[b, pl.ds(x * NY + yl, CH // 2, stride=YL), :]
    out_ref[...] = sort_ref[...].astype(bf16)


def unpack_kernel(var_ref, got_ref, fu_ref, mask_ref, disp_ref, pres_ref, rows_ref):
    variant = var_ref[0]
    for k in range(CH):
        src = slot_of(variant, k) * BLOCKS
        for b in range(BLOCKS):
            piece = got_ref[src + b].astype(f32)
            for yl in range(YL):
                rows_ref[yl, b, pl.ds(XL * k, XL), :] = piece[yl * XL : yl * XL + XL]
    for yl in range(YL):
        for b in range(BLOCKS - 1):
            flat = rows_ref[yl, b].T
            for i in range(2):
                z = 2 * b + i
                weight = (mask_ref[pl.ds(z * YL + yl, 1), :] != 0).astype(f32)
                at = pl.ds(z * BU * YL + yl, BU, stride=YL)
                disp_ref[at, :] = flat[i * BU : i * BU + BU] + fu_ref[at, :] * weight
        pres_ref[pl.ds(yl, HP, stride=YL), :] = rows_ref[yl, BLOCKS - 1].T


VM = pl.BlockSpec(memory_space=pltpu.VMEM)
SM = pl.BlockSpec(memory_space=pltpu.SMEM)


def call(kernel, scalars, arrays, outs, scratch):
    return pl.pallas_call(
        kernel,
        out_shape=[jax.ShapeDtypeStruct(*o) for o in outs],
        in_specs=[SM] * len(scalars) + [VM] * len(arrays),
        out_specs=[VM] * len(outs),
        scratch_shapes=[pltpu.VMEM(*s) for s in scratch],
    )(*scalars, *arrays)


def coefficients(spectrum):
    lower, upper = spectrum[0], spectrum[1]
    theta = (upper + lower) / 2.0
    delta = (upper - lower) / 2.0
    sigma = theta / delta
    rho = 1.0 / sigma
    values = [1.0 / theta, theta]
    for _ in range(SWEEPS - 1):
        rho_next = 1.0 / (2.0 * sigma - rho)
        values += [rho_next * rho, 2.0 * rho_next / delta]
        rho = rho_next
    return jnp.stack(values)


def schur_matrix(sinv, band_offsets):
    depth = jnp.arange(NZ, dtype=jnp.int32)
    hit = (depth[None, :, None] + band_offsets[:, None, None] == depth[None, None, :])
    picked = jnp.where(hit[:, :, None, :, None], sinv[:, :, :, None, :], 0.0)
    return jnp.sum(picked, axis=0).reshape(RP, RP)


def body(force_u, force_p, cellmask, layer_mats, kblocks, bcoup, sinv, band_offsets, spectrum):
    up, down = chain()
    other = lax.ppermute(layer_mats, "gz", [(0, 1), (1, 0)])
    gz = lax.axis_index("gz")
    layers = jnp.where(
        gz == 0, jnp.concatenate([layer_mats, other]), jnp.concatenate([other, layer_mats])
    )
    variant = (lax.axis_index("gx") % 4).astype(jnp.int32)[None]
    fu_in = force_u.reshape(ZL * BU * YL, LANES)
    fp_in = force_p.reshape(ZL * PB * YL, LANES)
    mask_in = cellmask.reshape(ZL * YL, LANES)
    coefs = coefficients(spectrum)
    table = jnp.stack([kblocks[:, d] for d in (1, 0, 2, 3, 4, 5, 6)], axis=2).reshape(4, BU, 7 * BU)
    matrix = schur_matrix(sinv, band_offsets)
    coup_t = bcoup.transpose(0, 2, 1)

    (packed,) = call(
        pack_kernel, [variant], [fu_in, fp_in, mask_in],
        [((CH * BLOCKS, 8, LANES), f32)],
        [((YL, BLOCKS, LANES, LANES), f32)],
    )
    got = lax.all_to_all(packed, PLANE, 0, 0, tiled=True)
    fu, fp, mask, send = call(
        spread_kernel, [coefs], [got.reshape(CH * BLOCKS * 8, LANES)],
        [((RU, LANES), f32), ((RP, LANES), f32), ((NZ, LANES), f32), ((RU + NZ, LANES), bf16)],
        [((BLOCKS, LANES, LANES), f32)],
    )
    low = lax.ppermute(send, ALL, up)
    high = lax.ppermute(send, ALL, down)
    wide = [((NZ, 8, 3 * LANES), f32)] + [((RU, 3 * LANES), f32)] * 3 + [
        ((RU + 2 * BU, 3 * LANES), bf16)
    ] * 2
    ru, du, dp, q, send2 = call(
        first_kernel, [coefs, layers],
        [table, bcoup, coup_t, matrix, fu, fp, mask, send, low, high],
        [((RU, LANES), f32), ((RU, LANES), f32), ((RP, LANES), f32), ((RP, LANES), f32),
         ((RU, LANES), bf16)],
        wide,
    )
    low2 = lax.ppermute(send2, ALL, up)
    high2 = lax.ppermute(send2, ALL, down)
    (back,) = call(
        second_kernel, [coefs, layers],
        [table, bcoup, matrix, fu, mask, ru, du, dp, q, send2, low2, high2, low, high],
        [((CH * BLOCKS * 8, LANES), bf16)],
        wide + [((RP, LANES), f32), ((BLOCKS, LANES, LANES), f32),
                ((CH * BLOCKS * 8, LANES), f32)],
    )
    home = lax.all_to_all(back.reshape(CH * BLOCKS, 8, LANES), PLANE, 0, 0, tiled=True)
    disp, pres = call(
        unpack_kernel, [variant], [home, fu_in, mask_in],
        [((ZL * BU * YL, LANES), f32), ((ZL * PB * YL, LANES), f32)],
        [((YL, BLOCKS, LANES, LANES), f32)],
    )
    return (disp.reshape(ZL, BU, YL, LANES), pres.reshape(ZL, PB, YL, LANES))


def solution(mesh):
    in_specs = (
        P("gz", None, "gy", "gx"),
        P("gz", None, "gy", "gx"),
        P("gz", "gy", "gx"),
        P("gz"),
        P(),
        P(),
        P(),
        P(),
        P(),
    )
    out_specs = (P("gz", None, "gy", "gx"), P("gz", None, "gy", "gx"))
    return jax.shard_map(body, mesh=mesh, in_specs=in_specs, out_specs=out_specs, check_vma=False)
```

```python
import jax
import jax.numpy as jnp
from jax import lax
from jax.experimental import pallas as pl
from jax.experimental.pallas import tpu as pltpu
from jax.sharding import PartitionSpec as P

SWEEPS = 4
ALL = ("gx", "gy", "gz")
PLANE = ("gy", "gz")
HIGHEST = lax.Precision.HIGHEST
NZ, BU, PB, NY = 16, 64, 16, 32
ZL, YL, XL, CH = 8, 2, 4, 32
RU, RP = NZ * BU, NZ * PB
HU, HP = ZL * BU, ZL * PB
WIDE = HU + HP
LANES = 128
BLOCKS = WIDE // LANES
STEP = 2 * BLOCKS * 8
UNROLL = 4
f32, bf16 = jnp.float32, jnp.bfloat16


def place(variant, k):
    if variant == 0:
        cx, r = k // 8, k % 8
        cz = r if cx % 2 == 0 else 7 - r
    elif variant == 1:
        cz, r = k // 4, k % 4
        cx = 3 - r if cz % 2 == 0 else r
    elif variant == 2:
        q, r = k // 8, k % 8
        cx = 3 - q
        cz = 7 - r if q % 2 == 0 else r
    else:
        q, r = k // 4, k % 4
        cz = 7 - q
        cx = r if q % 2 == 0 else 3 - r
    return cx * 8 + cz


def slot_of(variant, k):
    a, b, c, d = (place(v, k) for v in range(4))
    return jnp.where(
        variant < 2, jnp.where(variant == 0, a, b), jnp.where(variant == 2, c, d)
    )


def chain():
    order = [g * CH + place(g % 4, k) for g in range(8) for k in range(CH)]
    up = [(order[i], order[i + 1]) for i in range(len(order) - 1)]
    return up, [(b, a) for a, b in up]


def pack_kernel(var_ref, fu_ref, fp_ref, mask_ref, out_ref, flip_ref):
    for yl in range(YL):
        pressure = []
        for z in range(ZL):
            live = mask_ref[pl.ds(z * YL + yl, 1), :] != 0
            weight = live.astype(f32)
            fp = fp_ref[pl.ds(z * PB * YL + yl, PB, stride=YL), :] * weight
            last = lax.broadcasted_iota(jnp.int32, (PB, LANES), 0) == PB - 1
            dead = jnp.broadcast_to(weight, (PB, LANES)) == 0.0
            pressure.append(jnp.where(jnp.logical_and(last, dead), jnp.inf, fp))
        for b in range(BLOCKS - 1):
            pair = []
            for z in (2 * b, 2 * b + 1):
                weight = (mask_ref[pl.ds(z * YL + yl, 1), :] != 0).astype(f32)
                pair.append(fu_ref[pl.ds(z * BU * YL + yl, BU, stride=YL), :] * weight)
            flip_ref[yl, b] = jnp.concatenate(pair, axis=0).T
        flip_ref[yl, BLOCKS - 1] = jnp.concatenate(pressure, axis=0).T
    variant = var_ref[0]
    for k in range(CH):
        dest = slot_of(variant, k) * BLOCKS
        for b in range(BLOCKS):
            out_ref[dest + b] = jnp.concatenate(
                [flip_ref[yl, b, pl.ds(XL * k, XL), :] for yl in range(YL)], axis=0
            )


def spread_kernel(coef_ref, got_ref, fu_ref, fp_ref, mask_ref, send_ref, rows_ref):
    theta_inv = coef_ref[0]
    for half in range(2):
        for b in range(BLOCKS):
            for x in range(XL):
                for yl in range(YL):
                    rows_ref[b, pl.ds(x * NY + yl, CH // 2, stride=YL), :] = got_ref[
                        pl.ds((half * BLOCKS + b) * 8 + yl * XL + x, CH // 2, stride=STEP), :
                    ]
            flat = rows_ref[b].T
            if b < BLOCKS - 1:
                at = pl.ds(half * HU + b * LANES, LANES)
                fu_ref[at, :] = flat
                send_ref[at, :] = (flat * theta_inv).astype(bf16)
            else:
                fp_ref[pl.ds(half * HP, HP), :] = flat
    marks = fp_ref[pl.ds(PB - 1, NZ, stride=PB), :]
    weight = jnp.where(marks == jnp.inf, 0.0, 1.0)
    mask_ref[...] = weight
    send_ref[pl.ds(RU, NZ), :] = weight.astype(bf16)
    fp_ref[...] = jnp.where(fp_ref[...] == jnp.inf, 0.0, fp_ref[...])


def lane_iota(rows):
    return lax.broadcasted_iota(jnp.int32, (rows, LANES), 1)


def neighbours(parts, which):
    own = parts[which]
    lane = lane_iota(BU)
    y = lane % NY
    zero = jnp.zeros_like(own)
    below_y = jnp.where(y == 0, zero, pltpu.roll(own, 1, 1))
    above_y = jnp.where(y == NY - 1, zero, pltpu.roll(own, LANES - 1, 1))
    below_x = pltpu.roll(own, NY, 1)
    if which > 0:
        below_x = jnp.where(lane < NY, pltpu.roll(parts[which - 1], NY, 1), below_x)
    above_x = pltpu.roll(own, LANES - NY, 1)
    if which < 2:
        above_x = jnp.where(
            lane >= LANES - NY, pltpu.roll(parts[which + 1], LANES - NY, 1), above_x
        )
    return jnp.concatenate([below_y, above_y, below_x, above_x], axis=0)


def operands(z64, w_ref, blocks):
    first = blocks[0] * LANES
    width = len(blocks) * LANES
    parts = [
        w_ref[pl.ds(z64 + BU, BU), pl.ds(b * LANES, LANES)] for b in range(3)
    ]
    side = jnp.concatenate([neighbours(parts, b) for b in blocks], axis=1)
    column = w_ref[pl.ds(z64, 3 * BU), pl.ds(first, width)]
    return [side, column]


def layers_of(group):
    return [group * UNROLL + i for i in range(UNROLL)]


def sweep(k, blocks, begin, last, scal, refs, old, new):
    coef_ref, lm_ref, table_ref, mask_ref, d_ref, r_ref, s_ref = refs
    keep, scale = coef_ref[2 + 2 * k], coef_ref[3 + 2 * k]
    lanes = pl.ds(blocks[0] * LANES, len(blocks) * LANES)

    def group(g, carry):
        at = [pl.multiple_of(z * BU, BU) for z in layers_of(g)]
        products = []
        for z, z64 in zip(layers_of(g), at):
            table = table_ref[lm_ref[z]]
            stack = jnp.concatenate(operands(z64, old, blocks), axis=0)
            products.append(
                jnp.dot(table[:, : 7 * BU], stack, preferred_element_type=f32)
            )
        for z, z64, product in zip(layers_of(g), at, products):
            rows = pl.ds(z64, BU)
            if begin is None:
                r, d, s = r_ref[rows, lanes], d_ref[rows, lanes], s_ref[rows, lanes]
            else:
                r, d = begin(rows)
                s = d
            r = r - product * mask_ref[z, pl.ds(0, 1), lanes]
            d = keep * d + scale * r
            s = s + d
            if last is None:
                r_ref[rows, lanes] = r
                d_ref[rows, lanes] = d
                s_ref[rows, lanes] = s
                new[pl.ds(z64 + BU, BU), lanes] = d.astype(bf16)
            else:
                last(z64, s)
        return carry

    lax.fori_loop(0, NZ // UNROLL, group, 0)


def starter(scal, own_ref, low_ref, high_ref):
    theta_inv, theta = scal

    def begin(rows):
        r = own_ref[rows, :]
        low = low_ref[rows, :].astype(f32)
        high = high_ref[rows, :].astype(f32)
        return (
            jnp.concatenate([low * theta, r, high * theta], axis=1),
            jnp.concatenate([low, r * theta_inv, high], axis=1),
        )

    return begin


def widen(wide_ref, mask_ref, low_ref, high_ref):
    low = low_ref[pl.ds(RU, NZ), :].astype(f32)
    high = high_ref[pl.ds(RU, NZ), :].astype(f32)
    whole = jnp.concatenate([low, mask_ref[...], high], axis=1)
    for z in range(NZ):
        wide_ref[z] = jnp.broadcast_to(whole[z : z + 1], (8, 3 * LANES))


def pad_in(w_refs, sources):
    edge = jnp.zeros((BU, 3 * LANES), bf16)
    for w_ref in w_refs:
        w_ref[pl.ds(0, BU), :] = edge
        w_ref[pl.ds(RU + BU, BU), :] = edge
    for at, src in enumerate(sources):
        w_refs[0][pl.ds(BU, RU), pl.ds(at * LANES, LANES)] = src[pl.ds(0, RU), :]


def thirds(v):
    high = v.astype(bf16)
    low = (v - high.astype(f32)).astype(bf16)
    return [high, low, high]


def couple(get, lm_ref, coup_ref, mask_ref, rest_ref, sign, q_ref):
    def group(g, carry):
        for z in layers_of(g):
            here = pl.ds(pl.multiple_of(z * PB, PB), PB)
            du = get(pl.multiple_of(z * BU, BU))
            q = jnp.dot(coup_ref[lm_ref[z]], jnp.concatenate(thirds(du), axis=0),
                        preferred_element_type=f32)
            q_ref[here, :] = q * mask_ref[z, pl.ds(0, 1), pl.ds(LANES, LANES)] + sign * rest_ref[here, :]
        return carry

    lax.fori_loop(0, NZ // UNROLL, group, 0)


def bands(schur_ref, q_ref):
    return jnp.dot(schur_ref[...], jnp.concatenate(thirds(q_ref[...]), axis=0),
                   preferred_element_type=f32)


OWN = pl.ds(LANES, LANES)
FULL = (0, 1, 2)


def prep_kernel(kb_ref, coup_ref, schur_ref, table_ref, pair_ref, band_ref):
    for m in range(4):
        coup = coup_ref[m]
        high = coup.astype(bf16)
        low = (coup - high.astype(f32)).astype(bf16)
        pair_ref[m] = jnp.concatenate([high, high, low], axis=1)
        back = coup.T
        bhigh = back.astype(bf16)
        blow = (back - bhigh.astype(f32)).astype(bf16)
        blocks = [kb_ref[m, d] for d in (3, 4, 5, 6, 1, 0, 2)]
        pad = jnp.zeros((BU, PB), bf16)
        table_ref[m] = jnp.concatenate(blocks + [bhigh, bhigh, blow, pad], axis=1)
    whole = schur_ref[...]
    high = whole.astype(bf16)
    low = (whole - high.astype(f32)).astype(bf16)
    band_ref[...] = jnp.concatenate([high, high, low], axis=1)


def first_kernel(coef_ref, lm_ref, table_ref, coup_ref, schur_ref,
                 fu_ref, fp_ref, mask_ref, own_ref, low_ref, high_ref,
                 ru_ref, du_ref, dp_ref, q_ref, send_ref,
                 wide_ref, d_ref, r_ref, s_ref, wa_ref, wb_ref):
    scal = (coef_ref[0], coef_ref[1])
    widen(wide_ref, mask_ref, low_ref, high_ref)
    pad_in((wa_ref, wb_ref), (low_ref, own_ref, high_ref))
    refs = (coef_ref, lm_ref, table_ref, wide_ref, d_ref, r_ref, s_ref)
    begin = starter(scal, fu_ref, low_ref, high_ref)

    def last(z64, s):
        wb_ref[pl.ds(z64 + BU, BU), :] = s.astype(bf16)
        du_ref[pl.ds(z64, BU), :] = s[:, LANES : 2 * LANES]

    sweep(0, FULL, begin, None, scal, refs, wa_ref, wb_ref)
    sweep(1, FULL, None, None, scal, refs, wb_ref, wa_ref)
    sweep(2, FULL, None, last, scal, refs, wa_ref, wb_ref)
    couple(lambda z64: du_ref[pl.ds(z64, BU), :], lm_ref, coup_ref, wide_ref, fp_ref, -1.0, q_ref)
    dp_ref[...] = bands(schur_ref, q_ref)

    def finish(g, carry):
        at = [pl.multiple_of(z * BU, BU) for z in layers_of(g)]
        products = []
        for z, z64 in zip(layers_of(g), at):
            here = pl.ds(pl.multiple_of(z * PB, PB), PB)
            dp = dp_ref[here, :] * wide_ref[z, pl.ds(0, 1), OWN]
            dp_ref[here, :] = dp
            stack = operands(z64, wb_ref, (1,)) + thirds(dp)
            products.append(
                jnp.dot(table_ref[lm_ref[z]][:, : 7 * BU + 3 * PB],
                        jnp.concatenate(stack, axis=0), preferred_element_type=f32)
            )
        for z, z64, product in zip(layers_of(g), at, products):
            rows = pl.ds(z64, BU)
            ru = fu_ref[rows, :] - product * wide_ref[z, pl.ds(0, 1), OWN]
            ru_ref[rows, :] = ru
            send_ref[rows, :] = (ru * scal[0]).astype(bf16)
        return carry

    lax.fori_loop(0, NZ // UNROLL, finish, 0)


def second_kernel(coef_ref, lm_ref, table_ref, coup_ref, schur_ref,
                  fu_ref, mask_ref, ru_ref, du_ref, dp_ref, q_ref, own_ref, low_ref,
                  high_ref, mlow_ref, mhigh_ref, out_ref,
                  wide_ref, d_ref, r_ref, s_ref, wa_ref, wb_ref, p_ref, rows_ref, sort_ref):
    scal = (coef_ref[0], coef_ref[1])
    widen(wide_ref, mask_ref, mlow_ref, mhigh_ref)
    pad_in((wa_ref, wb_ref), (low_ref, own_ref, high_ref))
    refs = (coef_ref, lm_ref, table_ref, wide_ref, d_ref, r_ref, s_ref)
    begin = starter(scal, ru_ref, low_ref, high_ref)

    def last(z64, s):
        s_ref[pl.ds(z64, BU), OWN] = s

    sweep(0, FULL, begin, None, scal, refs, wa_ref, wb_ref)
    sweep(1, FULL, None, None, scal, refs, wb_ref, wa_ref)
    sweep(2, (1,), None, last, scal, refs, wa_ref, wb_ref)
    couple(lambda z64: s_ref[pl.ds(z64, BU), OWN], lm_ref, coup_ref, wide_ref, q_ref, 1.0, p_ref)
    p_ref[...] = bands(schur_ref, p_ref)
    own = OWN
    for half in range(2):
        for b in range(BLOCKS):
            if b < BLOCKS - 1:
                rows = pl.ds(half * HU + b * LANES, LANES)
                flat = s_ref[rows, own] + du_ref[rows, :] - fu_ref[rows, :]
            else:
                pressure = []
                for z in range(half * ZL, half * ZL + ZL):
                    here = pl.ds(z * PB, PB)
                    dp = p_ref[here, :] * mask_ref[pl.ds(z, 1), :]
                    pressure.append(dp + dp_ref[here, :])
                flat = jnp.concatenate(pressure, axis=0)
            rows_ref[b] = flat.T
            for x in range(XL):
                for yl in range(YL):
                    sort_ref[
                        pl.ds((half * BLOCKS + b) * 8 + yl * XL + x, CH // 2, stride=STEP), :
                    ] = rows_ref[b, pl.ds(x * NY + yl, CH // 2, stride=YL), :]
    out_ref[...] = sort_ref[...].astype(bf16)


def unpack_kernel(var_ref, got_ref, fu_ref, mask_ref, disp_ref, pres_ref, rows_ref):
    variant = var_ref[0]
    for k in range(CH):
        src = slot_of(variant, k) * BLOCKS
        for b in range(BLOCKS):
            piece = got_ref[src + b].astype(f32)
            for yl in range(YL):
                rows_ref[yl, b, pl.ds(XL * k, XL), :] = piece[yl * XL : yl * XL + XL]
    for yl in range(YL):
        for b in range(BLOCKS - 1):
            flat = rows_ref[yl, b].T
            for i in range(2):
                z = 2 * b + i
                weight = (mask_ref[pl.ds(z * YL + yl, 1), :] != 0).astype(f32)
                at = pl.ds(z * BU * YL + yl, BU, stride=YL)
                disp_ref[at, :] = flat[i * BU : i * BU + BU] + fu_ref[at, :] * weight
        pres_ref[pl.ds(yl, HP, stride=YL), :] = rows_ref[yl, BLOCKS - 1].T


VM = pl.BlockSpec(memory_space=pltpu.VMEM)
SM = pl.BlockSpec(memory_space=pltpu.SMEM)


def call(kernel, scalars, arrays, outs, scratch, limit=24):
    return pl.pallas_call(
        kernel,
        out_shape=[jax.ShapeDtypeStruct(*o) for o in outs],
        in_specs=[SM] * len(scalars) + [VM] * len(arrays),
        out_specs=[VM] * len(outs),
        scratch_shapes=[pltpu.VMEM(*s) for s in scratch],
        compiler_params=pltpu.CompilerParams(vmem_limit_bytes=limit << 20),
    )(*scalars, *arrays)


def coefficients(spectrum):
    lower, upper = spectrum[0], spectrum[1]
    theta = (upper + lower) / 2.0
    delta = (upper - lower) / 2.0
    sigma = theta / delta
    rho = 1.0 / sigma
    values = [1.0 / theta, theta]
    for _ in range(SWEEPS - 1):
        rho_next = 1.0 / (2.0 * sigma - rho)
        values += [rho_next * rho, 2.0 * rho_next / delta]
        rho = rho_next
    return jnp.stack(values)


def schur_matrix(sinv, band_offsets):
    depth = jnp.arange(NZ, dtype=jnp.int32)
    hit = (depth[None, :, None] + band_offsets[:, None, None] == depth[None, None, :])
    picked = jnp.where(hit[:, :, None, :, None], sinv[:, :, :, None, :], 0.0)
    return jnp.sum(picked, axis=0).reshape(RP, RP)


def body(force_u, force_p, cellmask, layer_mats, kblocks, bcoup, sinv, band_offsets, spectrum):
    up, down = chain()
    other = lax.ppermute(layer_mats, "gz", [(0, 1), (1, 0)])
    gz = lax.axis_index("gz")
    layers = jnp.where(
        gz == 0, jnp.concatenate([layer_mats, other]), jnp.concatenate([other, layer_mats])
    )
    variant = (lax.axis_index("gx") % 4).astype(jnp.int32)[None]
    fu_in = force_u.reshape(ZL * BU * YL, LANES)
    fp_in = force_p.reshape(ZL * PB * YL, LANES)
    mask_in = cellmask.reshape(ZL * YL, LANES)
    coefs = coefficients(spectrum)
    table, pair, matrix = call(
        prep_kernel, [], [kblocks, bcoup, schur_matrix(sinv, band_offsets)],
        [((4, BU, 8 * BU), bf16), ((4, PB, 3 * BU), bf16), ((RP, 3 * RP), bf16)], [],
    )

    (packed,) = call(
        pack_kernel, [variant], [fu_in, fp_in, mask_in],
        [((CH * BLOCKS, 8, LANES), f32)],
        [((YL, BLOCKS, LANES, LANES), f32)],
    )
    got = lax.all_to_all(packed, PLANE, 0, 0, tiled=True)
    got, table, pair, matrix, coefs, layers = lax.optimization_barrier(
        (got, table, pair, matrix, coefs, layers)
    )
    fu, fp, mask, send = call(
        spread_kernel, [coefs], [got.reshape(CH * BLOCKS * 8, LANES)],
        [((RU, LANES), f32), ((RP, LANES), f32), ((NZ, LANES), f32), ((RU + NZ, LANES), bf16)],
        [((BLOCKS, LANES, LANES), f32)],
    )
    low = lax.ppermute(send, ALL, up)
    high = lax.ppermute(send, ALL, down)
    wide = [((NZ, 8, 3 * LANES), f32)] + [((RU, 3 * LANES), f32)] * 3 + [
        ((RU + 2 * BU, 3 * LANES), bf16)
    ] * 2
    ru, du, dp, q, send2 = call(
        first_kernel, [coefs, layers],
        [table, pair, matrix, fu, fp, mask, send, low, high],
        [((RU, LANES), f32), ((RU, LANES), f32), ((RP, LANES), f32), ((RP, LANES), f32),
         ((RU, LANES), bf16)],
        wide,
    )
    low2 = lax.ppermute(send2, ALL, up)
    high2 = lax.ppermute(send2, ALL, down)
    (back,) = call(
        second_kernel, [coefs, layers],
        [table, pair, matrix, fu, mask, ru, du, dp, q, send2, low2, high2, low, high],
        [((CH * BLOCKS * 8, LANES), bf16)],
        wide + [((RP, LANES), f32), ((BLOCKS, LANES, LANES), f32),
                ((CH * BLOCKS * 8, LANES), f32)],
    )
    home = lax.all_to_all(back.reshape(CH * BLOCKS, 8, LANES), PLANE, 0, 0, tiled=True)
    disp, pres = call(
        unpack_kernel, [variant], [home, fu_in, mask_in],
        [((ZL * BU * YL, LANES), f32), ((ZL * PB * YL, LANES), f32)],
        [((YL, BLOCKS, LANES, LANES), f32)],
    )
    return (disp.reshape(ZL, BU, YL, LANES), pres.reshape(ZL, PB, YL, LANES))


def solution(mesh):
    in_specs = (
        P("gz", None, "gy", "gx"),
        P("gz", None, "gy", "gx"),
        P("gz", "gy", "gx"),
        P("gz"),
        P(),
        P(),
        P(),
        P(),
        P(),
    )
    out_specs = (P("gz", None, "gy", "gx"), P("gz", None, "gy", "gx"))
    return jax.shard_map(body, mesh=mesh, in_specs=in_specs, out_specs=out_specs, check_vma=False)
```

```python
import jax
import jax.numpy as jnp
from jax import lax
from jax.experimental import pallas as pl
from jax.experimental.pallas import tpu as pltpu
from jax.sharding import PartitionSpec as P

SWEEPS = 4
ALL = ("gx", "gy", "gz")
PLANE = ("gy", "gz")
HIGHEST = lax.Precision.HIGHEST
NZ, BU, PB, NY = 16, 64, 16, 32
ZL, YL, XL, CH = 8, 2, 4, 32
RU, RP = NZ * BU, NZ * PB
HU, HP = ZL * BU, ZL * PB
WIDE = HU + HP
LANES = 128
BLOCKS = WIDE // LANES
STEP = 2 * BLOCKS * 8
UNROLL = 8
f32, bf16 = jnp.float32, jnp.bfloat16


def place(variant, k):
    if variant == 0:
        cx, r = k // 8, k % 8
        cz = r if cx % 2 == 0 else 7 - r
    elif variant == 1:
        cz, r = k // 4, k % 4
        cx = 3 - r if cz % 2 == 0 else r
    elif variant == 2:
        q, r = k // 8, k % 8
        cx = 3 - q
        cz = 7 - r if q % 2 == 0 else r
    else:
        q, r = k // 4, k % 4
        cz = 7 - q
        cx = r if q % 2 == 0 else 3 - r
    return cx * 8 + cz


def slot_of(variant, k):
    a, b, c, d = (place(v, k) for v in range(4))
    return jnp.where(
        variant < 2, jnp.where(variant == 0, a, b), jnp.where(variant == 2, c, d)
    )


def chain():
    order = [g * CH + place(g % 4, k) for g in range(8) for k in range(CH)]
    up = [(order[i], order[i + 1]) for i in range(len(order) - 1)]
    return up, [(b, a) for a, b in up]


def pack_kernel(var_ref, fu_ref, fp_ref, mask_ref, out_ref, flip_ref):
    for yl in range(YL):
        pressure = []
        for z in range(ZL):
            live = mask_ref[pl.ds(z * YL + yl, 1), :] != 0
            weight = live.astype(f32)
            fp = fp_ref[pl.ds(z * PB * YL + yl, PB, stride=YL), :] * weight
            last = lax.broadcasted_iota(jnp.int32, (PB, LANES), 0) == PB - 1
            dead = jnp.broadcast_to(weight, (PB, LANES)) == 0.0
            pressure.append(jnp.where(jnp.logical_and(last, dead), jnp.inf, fp))
        for b in range(BLOCKS - 1):
            pair = []
            for z in (2 * b, 2 * b + 1):
                weight = (mask_ref[pl.ds(z * YL + yl, 1), :] != 0).astype(f32)
                pair.append(fu_ref[pl.ds(z * BU * YL + yl, BU, stride=YL), :] * weight)
            flip_ref[yl, b] = jnp.concatenate(pair, axis=0).T
        flip_ref[yl, BLOCKS - 1] = jnp.concatenate(pressure, axis=0).T
    variant = var_ref[0]
    for k in range(CH):
        dest = slot_of(variant, k) * BLOCKS
        for b in range(BLOCKS):
            out_ref[dest + b] = jnp.concatenate(
                [flip_ref[yl, b, pl.ds(XL * k, XL), :] for yl in range(YL)], axis=0
            )


def spread_kernel(coef_ref, got_ref, fu_ref, fp_ref, mask_ref, send_ref, rows_ref):
    theta_inv = coef_ref[pl.ds(0, 1), pl.ds(0, LANES)]
    for half in range(2):
        for b in range(BLOCKS):
            for x in range(XL):
                for yl in range(YL):
                    rows_ref[b, pl.ds(x * NY + yl, CH // 2, stride=YL), :] = got_ref[
                        pl.ds((half * BLOCKS + b) * 8 + yl * XL + x, CH // 2, stride=STEP), :
                    ]
            flat = rows_ref[b].T
            if b < BLOCKS - 1:
                at = pl.ds(half * HU + b * LANES, LANES)
                fu_ref[at, :] = flat
                send_ref[at, :] = (flat * theta_inv).astype(bf16)
            else:
                fp_ref[pl.ds(half * HP, HP), :] = flat
    marks = fp_ref[pl.ds(PB - 1, NZ, stride=PB), :]
    weight = jnp.where(marks == jnp.inf, 0.0, 1.0)
    mask_ref[...] = weight
    send_ref[pl.ds(RU, NZ), :] = weight.astype(bf16)
    fp_ref[...] = jnp.where(fp_ref[...] == jnp.inf, 0.0, fp_ref[...])


LOW, HIGH, OWN, EDGE = 0, 1, 2, 3
WIDTH = 4 * LANES


def block(b, count=1):
    return pl.ds(b * LANES, count * LANES)


def lane_of(rows):
    return lax.broadcasted_iota(jnp.int32, (rows, LANES), 1)


def edge_of(low, high):
    return jnp.where(lane_of(low.shape[0]) < LANES // 2, high, low)


def stack_of(z64, w_ref, mode):
    lane = lane_of(BU)
    y = lane % NY
    ins = {"wide": (LOW, HIGH, OWN), "shrink": (LOW, HIGH, OWN), "ring": (OWN, EDGE),
           "own": (OWN, EDGE)}[mode]
    outs = {"wide": (LOW, HIGH, OWN), "shrink": (OWN, EDGE), "ring": (OWN, EDGE),
            "own": (OWN,)}[mode]
    rows = pl.ds(z64 + BU, BU)
    part = {b: w_ref[rows, block(b)] for b in sorted(set(ins) | set(outs))}
    up = {b: pltpu.roll(part[b], NY, 1) for b in ins}
    down = {b: pltpu.roll(part[b], LANES - NY, 1) for b in ins}
    zero = jnp.zeros_like(part[OWN])
    first, half, tail = lane < NY, lane < LANES // 2, lane >= LANES - NY
    if mode in ("wide", "shrink"):
        below = {LOW: up[LOW], OWN: jnp.where(first, up[LOW], up[OWN])}
        above = {HIGH: down[HIGH], OWN: jnp.where(tail, down[HIGH], down[OWN])}
        if mode == "wide":
            below[HIGH] = jnp.where(first, up[OWN], up[HIGH])
            above[LOW] = jnp.where(tail, down[OWN], down[LOW])
        else:
            below[EDGE] = jnp.where(first, up[OWN], jnp.where(half, up[HIGH], up[LOW]))
            above[EDGE] = jnp.where(tail, down[OWN], jnp.where(half, down[HIGH], down[LOW]))
    else:
        below = {OWN: jnp.where(first, up[EDGE], up[OWN]), EDGE: jnp.where(first, up[OWN], up[EDGE])}
        above = {OWN: jnp.where(tail, down[EDGE], down[OWN]),
                 EDGE: jnp.where(tail, down[OWN], down[EDGE])}
    columns = []
    for b in outs:
        below_y = jnp.where(y == 0, zero, pltpu.roll(part[b], 1, 1))
        above_y = jnp.where(y == NY - 1, zero, pltpu.roll(part[b], LANES - 1, 1))
        columns.append(jnp.concatenate([below_y, above_y, below[b], above[b]], axis=0))
    depth = w_ref[pl.ds(z64, 3 * BU), block(outs[0], len(outs))]
    return [jnp.concatenate(columns, axis=1), depth]


def layers_of(group):
    return [group * UNROLL + i for i in range(UNROLL)]


def sweep(k, mode, begin, last, refs, old, new):
    coef_ref, lm_ref, table_ref, mask_ref, state = refs
    count = {"wide": 3, "own": 1}.get(mode, 2)
    lanes = block(LOW if mode == "wide" else OWN, count)
    inner = block(0, min(count, 2))
    keep = coef_ref[pl.ds(2 + 2 * k, 1), block(0, count)]
    scale = coef_ref[pl.ds(3 + 2 * k, 1), block(0, count)]

    def group(g, carry):
        for z in layers_of(g):
            z64 = pl.multiple_of(z * BU, BU)
            table = table_ref[lm_ref[z]]
            stack = jnp.concatenate(stack_of(z64, old, mode), axis=0)
            product = jnp.dot(table[:, : 7 * BU], stack, preferred_element_type=f32)
            rows = pl.ds(z64, BU)
            if begin is None:
                r, d, s = [ref[rows, inner] for ref in state]
            else:
                r, d = begin(rows)
                s = d
            r = r - product * mask_ref[z, pl.ds(0, 1), lanes]
            d = keep * d + scale * r
            s = s + d
            if last is not None:
                last(z64, s)
                continue
            here = pl.ds(z64 + BU, BU)
            if mode == "wide":
                w = d.astype(bf16)
                new[here, block(LOW, 3)] = w
                new[here, block(EDGE)] = edge_of(w[:, :LANES], w[:, LANES : 2 * LANES])
                for ref, v in zip(state, (r, d, s)):
                    ref[rows, block(0)] = v[:, 2 * LANES :]
                    ref[rows, block(1)] = edge_of(v[:, :LANES], v[:, LANES : 2 * LANES])
            else:
                new[here, lanes] = d.astype(bf16)
                for ref, v in zip(state, (r, d, s)):
                    ref[rows, inner] = v
        return carry

    lax.fori_loop(0, NZ // UNROLL, group, 0)


def starter(coef_ref, own_ref, low_ref, high_ref, wide):
    theta_inv = coef_ref[pl.ds(0, 1), block(0)]
    theta = coef_ref[pl.ds(1, 1), block(0)]

    def begin(rows):
        r = own_ref[rows, :]
        d = r * theta_inv
        low = low_ref[rows, :].astype(f32)
        high = high_ref[rows, :].astype(f32)
        if wide:
            return (
                jnp.concatenate([low * theta, high * theta, r], axis=1),
                jnp.concatenate([low, high, d], axis=1),
            )
        edge = edge_of(low, high)
        return (
            jnp.concatenate([r, edge * theta], axis=1),
            jnp.concatenate([d, edge], axis=1),
        )

    return begin


def widen(wide_ref, mask_ref, low_ref, high_ref):
    low = low_ref[pl.ds(RU, NZ), :].astype(f32)
    high = high_ref[pl.ds(RU, NZ), :].astype(f32)
    whole = jnp.concatenate([low, high, mask_ref[...], edge_of(low, high)], axis=1)
    for z in range(NZ):
        wide_ref[z] = jnp.broadcast_to(whole[z : z + 1], (8, WIDTH))


def pad_in(w_refs, low_ref, high_ref, own_ref, with_edge):
    edge = jnp.zeros((BU, WIDTH), bf16)
    for w_ref in w_refs:
        w_ref[pl.ds(0, BU), :] = edge
        w_ref[pl.ds(RU + BU, BU), :] = edge
    for b, src in ((LOW, low_ref), (HIGH, high_ref), (OWN, own_ref)):
        w_refs[0][pl.ds(BU, RU), block(b)] = src[pl.ds(0, RU), :]
    if with_edge:
        w_refs[0][pl.ds(BU, RU), block(EDGE)] = edge_of(
            low_ref[pl.ds(0, RU), :], high_ref[pl.ds(0, RU), :]
        )


def thirds(v):
    high = v.astype(bf16)
    low = (v - high.astype(f32)).astype(bf16)
    return [high, low, high]


def halves(v):
    high = v.astype(bf16)
    return high, (v - high.astype(f32)).astype(bf16)


def couple(get, lm_ref, coup_ref, mask_ref, rest_ref, sign, q_ref):
    def group(g, carry):
        for z in layers_of(g):
            here = pl.ds(pl.multiple_of(z * PB, PB), PB)
            du = get(pl.multiple_of(z * BU, BU))
            q = jnp.dot(coup_ref[lm_ref[z]], jnp.concatenate(thirds(du), axis=0),
                        preferred_element_type=f32)
            q_ref[here, :] = q * mask_ref[z, pl.ds(0, 1), block(OWN)] + sign * rest_ref[here, :]
        return carry

    lax.fori_loop(0, NZ // UNROLL, group, 0)


def bands(schur_ref, q_ref):
    return jnp.dot(schur_ref[...], jnp.concatenate(thirds(q_ref[...]), axis=0),
                   preferred_element_type=f32)


def prep_kernel(spec_ref, off_ref, kb_ref, coup_ref, sinv_ref,
                coef_ref, table_ref, pair_ref, band_ref):
    lower = jnp.full((1, WIDTH), spec_ref[0], f32)
    upper = jnp.full((1, WIDTH), spec_ref[1], f32)
    theta = (upper + lower) / 2.0
    delta = (upper - lower) / 2.0
    sigma = theta / delta
    rho = 1.0 / sigma
    coef_ref[pl.ds(0, 1), :] = 1.0 / theta
    coef_ref[pl.ds(1, 1), :] = theta
    for k in range(SWEEPS - 1):
        rho_next = 1.0 / (2.0 * sigma - rho)
        coef_ref[pl.ds(2 + 2 * k, 1), :] = rho_next * rho
        coef_ref[pl.ds(3 + 2 * k, 1), :] = 2.0 * rho_next / delta
        rho = rho_next
    for m in range(4):
        high, low = halves(coup_ref[m])
        pair_ref[m] = jnp.concatenate([high, high, low], axis=1)
        high, low = halves(coup_ref[m].T)
        blocks = [kb_ref[m, d] for d in (3, 4, 5, 6, 1, 0, 2)]
        pad = jnp.zeros((BU, PB), bf16)
        table_ref[m] = jnp.concatenate(blocks + [high, high, low, pad], axis=1)
    row = lax.broadcasted_iota(jnp.int32, (PB, RP), 0)
    col = lax.broadcasted_iota(jnp.int32, (PB, RP), 1)
    spread = (col % PB == row).astype(f32).astype(bf16)
    gap = (lax.broadcasted_iota(jnp.int32, (RP, RP), 1) // PB
           - lax.broadcasted_iota(jnp.int32, (RP, RP), 0) // PB)
    total = [jnp.zeros((RP, RP), f32)] * 2
    for k in range(8):
        hit = gap == off_ref[k]
        for i, part in enumerate(halves(sinv_ref[k].reshape(RP, PB))):
            wide = jnp.dot(part, spread, preferred_element_type=f32)
            total[i] = total[i] + jnp.where(hit, wide, 0.0)
    high, low = total[0].astype(bf16), total[1].astype(bf16)
    band_ref[...] = jnp.concatenate([high, high, low], axis=1)


def first_kernel(lm_ref, coef_ref, table_ref, coup_ref, schur_ref,
                 fu_ref, fp_ref, mask_ref, own_ref, low_ref, high_ref,
                 ru_ref, du_ref, dp_ref, q_ref, send_ref,
                 wide_ref, d_ref, r_ref, s_ref, wa_ref, wb_ref):
    widen(wide_ref, mask_ref, low_ref, high_ref)
    pad_in((wa_ref, wb_ref), low_ref, high_ref, own_ref, False)
    refs = (coef_ref, lm_ref, table_ref, wide_ref, (r_ref, d_ref, s_ref))
    begin = starter(coef_ref, fu_ref, low_ref, high_ref, True)

    def last(z64, s):
        wb_ref[pl.ds(z64 + BU, BU), block(OWN, 2)] = s.astype(bf16)
        du_ref[pl.ds(z64, BU), :] = s[:, :LANES]

    sweep(0, "wide", begin, None, refs, wa_ref, wb_ref)
    sweep(1, "shrink", None, None, refs, wb_ref, wa_ref)
    sweep(2, "ring", None, last, refs, wa_ref, wb_ref)
    couple(lambda z64: du_ref[pl.ds(z64, BU), :], lm_ref, coup_ref, wide_ref, fp_ref, -1.0, q_ref)
    dp_ref[...] = bands(schur_ref, q_ref)
    theta_inv = coef_ref[pl.ds(0, 1), block(0)]

    def finish(g, carry):
        for z in layers_of(g):
            z64 = pl.multiple_of(z * BU, BU)
            here = pl.ds(pl.multiple_of(z * PB, PB), PB)
            weight = wide_ref[z, pl.ds(0, 1), block(OWN)]
            dp = dp_ref[here, :] * weight
            dp_ref[here, :] = dp
            stack = stack_of(z64, wb_ref, "own") + thirds(dp)
            product = jnp.dot(table_ref[lm_ref[z]][:, : 7 * BU + 3 * PB],
                              jnp.concatenate(stack, axis=0), preferred_element_type=f32)
            rows = pl.ds(z64, BU)
            ru = fu_ref[rows, :] - product * weight
            ru_ref[rows, :] = ru
            send_ref[rows, :] = (ru * theta_inv).astype(bf16)
        return carry

    lax.fori_loop(0, NZ // UNROLL, finish, 0)


def second_kernel(lm_ref, coef_ref, table_ref, coup_ref, schur_ref,
                  fu_ref, mask_ref, ru_ref, du_ref, dp_ref, q_ref, own_ref, low_ref,
                  high_ref, mlow_ref, mhigh_ref, out_ref,
                  wide_ref, d_ref, r_ref, s_ref, wa_ref, wb_ref, p_ref, rows_ref, sort_ref):
    widen(wide_ref, mask_ref, mlow_ref, mhigh_ref)
    pad_in((wa_ref, wb_ref), low_ref, high_ref, own_ref, True)
    refs = (coef_ref, lm_ref, table_ref, wide_ref, (r_ref, d_ref, s_ref))
    begin = starter(coef_ref, ru_ref, low_ref, high_ref, False)
    own = block(0)

    def last(z64, s):
        s_ref[pl.ds(z64, BU), own] = s

    sweep(0, "shrink", begin, None, refs, wa_ref, wb_ref)
    sweep(1, "ring", None, None, refs, wb_ref, wa_ref)
    sweep(2, "own", None, last, refs, wa_ref, wb_ref)
    couple(lambda z64: s_ref[pl.ds(z64, BU), own], lm_ref, coup_ref, wide_ref, q_ref, 1.0, p_ref)
    p_ref[...] = bands(schur_ref, p_ref)
    for half in range(2):
        for b in range(BLOCKS):
            if b < BLOCKS - 1:
                rows = pl.ds(half * HU + b * LANES, LANES)
                flat = s_ref[rows, own] + du_ref[rows, :] - fu_ref[rows, :]
            else:
                pressure = []
                for z in range(half * ZL, half * ZL + ZL):
                    here = pl.ds(z * PB, PB)
                    dp = p_ref[here, :] * mask_ref[pl.ds(z, 1), :]
                    pressure.append(dp + dp_ref[here, :])
                flat = jnp.concatenate(pressure, axis=0)
            rows_ref[b] = flat.T
            for x in range(XL):
                for yl in range(YL):
                    sort_ref[
                        pl.ds((half * BLOCKS + b) * 8 + yl * XL + x, CH // 2, stride=STEP), :
                    ] = rows_ref[b, pl.ds(x * NY + yl, CH // 2, stride=YL), :]
    out_ref[...] = sort_ref[...].astype(bf16)


def unpack_kernel(var_ref, got_ref, fu_ref, mask_ref, disp_ref, pres_ref, rows_ref):
    variant = var_ref[0]
    for k in range(CH):
        src = slot_of(variant, k) * BLOCKS
        for b in range(BLOCKS):
            piece = got_ref[src + b].astype(f32)
            for yl in range(YL):
                rows_ref[yl, b, pl.ds(XL * k, XL), :] = piece[yl * XL : yl * XL + XL]
    for yl in range(YL):
        for b in range(BLOCKS - 1):
            flat = rows_ref[yl, b].T
            for i in range(2):
                z = 2 * b + i
                weight = (mask_ref[pl.ds(z * YL + yl, 1), :] != 0).astype(f32)
                at = pl.ds(z * BU * YL + yl, BU, stride=YL)
                disp_ref[at, :] = flat[i * BU : i * BU + BU] + fu_ref[at, :] * weight
        pres_ref[pl.ds(yl, HP, stride=YL), :] = rows_ref[yl, BLOCKS - 1].T


VM = pl.BlockSpec(memory_space=pltpu.VMEM)
SM = pl.BlockSpec(memory_space=pltpu.SMEM)


def call(kernel, scalars, arrays, outs, scratch, limit=24):
    return pl.pallas_call(
        kernel,
        out_shape=[jax.ShapeDtypeStruct(*o) for o in outs],
        in_specs=[SM] * len(scalars) + [VM] * len(arrays),
        out_specs=[VM] * len(outs),
        scratch_shapes=[pltpu.VMEM(*s) for s in scratch],
        compiler_params=pltpu.CompilerParams(vmem_limit_bytes=limit << 20),
    )(*scalars, *arrays)


def body(force_u, force_p, cellmask, layer_mats, kblocks, bcoup, sinv, band_offsets, spectrum):
    up, down = chain()
    other = lax.ppermute(layer_mats, "gz", [(0, 1), (1, 0)])
    gz = lax.axis_index("gz")
    layers = jnp.where(
        gz == 0, jnp.concatenate([layer_mats, other]), jnp.concatenate([other, layer_mats])
    )
    variant = (lax.axis_index("gx") % 4).astype(jnp.int32)[None]
    fu_in = force_u.reshape(ZL * BU * YL, LANES)
    fp_in = force_p.reshape(ZL * PB * YL, LANES)
    mask_in = cellmask.reshape(ZL * YL, LANES)
    coefs, table, pair, matrix = call(
        prep_kernel, [spectrum, band_offsets], [kblocks, bcoup, sinv],
        [((8, WIDTH), f32), ((4, BU, 8 * BU), bf16), ((4, PB, 3 * BU), bf16),
         ((RP, 3 * RP), bf16)], [],
    )

    (packed,) = call(
        pack_kernel, [variant], [fu_in, fp_in, mask_in],
        [((CH * BLOCKS, 8, LANES), f32)],
        [((YL, BLOCKS, LANES, LANES), f32)],
        limit=60,
    )
    got = lax.all_to_all(packed, PLANE, 0, 0, tiled=True)
    got, table, pair, matrix, coefs = lax.optimization_barrier(
        (got, table, pair, matrix, coefs)
    )
    fu, fp, mask, send = call(
        spread_kernel, [], [coefs, got.reshape(CH * BLOCKS * 8, LANES)],
        [((RU, LANES), f32), ((RP, LANES), f32), ((NZ, LANES), f32), ((RU + NZ, LANES), bf16)],
        [((BLOCKS, LANES, LANES), f32)],
    )
    low = lax.ppermute(send, ALL, up)
    high = lax.ppermute(send, ALL, down)
    wide = [((NZ, 8, WIDTH), f32)] + [((RU, 2 * LANES), f32)] * 3 + [
        ((RU + 2 * BU, WIDTH), bf16)
    ] * 2
    ru, du, dp, q, send2 = call(
        first_kernel, [layers],
        [coefs, table, pair, matrix, fu, fp, mask, send, low, high],
        [((RU, LANES), f32), ((RU, LANES), f32), ((RP, LANES), f32), ((RP, LANES), f32),
         ((RU, LANES), bf16)],
        wide,
    )
    low2 = lax.ppermute(send2, ALL, up)
    high2 = lax.ppermute(send2, ALL, down)
    (back,) = call(
        second_kernel, [layers],
        [coefs, table, pair, matrix, fu, mask, ru, du, dp, q, send2, low2, high2, low, high],
        [((CH * BLOCKS * 8, LANES), bf16)],
        wide + [((RP, LANES), f32), ((BLOCKS, LANES, LANES), f32),
                ((CH * BLOCKS * 8, LANES), f32)],
    )
    home = lax.all_to_all(back.reshape(CH * BLOCKS, 8, LANES), PLANE, 0, 0, tiled=True)
    disp, pres = call(
        unpack_kernel, [variant], [home, fu_in, mask_in],
        [((ZL * BU * YL, LANES), f32), ((ZL * PB * YL, LANES), f32)],
        [((YL, BLOCKS, LANES, LANES), f32)],
    )
    return (disp.reshape(ZL, BU, YL, LANES), pres.reshape(ZL, PB, YL, LANES))


def solution(mesh):
    in_specs = (
        P("gz", None, "gy", "gx"),
        P("gz", None, "gy", "gx"),
        P("gz", "gy", "gx"),
        P("gz"),
        P(),
        P(),
        P(),
        P(),
        P(),
    )
    out_specs = (P("gz", None, "gy", "gx"), P("gz", None, "gy", "gx"))
    return jax.shard_map(body, mesh=mesh, in_specs=in_specs, out_specs=out_specs, check_vma=False)
```

```python
import jax
import jax.numpy as jnp
from jax import lax
from jax.experimental import pallas as pl
from jax.experimental.pallas import tpu as pltpu
from jax.sharding import PartitionSpec as P

SWEEPS = 4
ALL = ("gx", "gy", "gz")
PLANE = ("gy", "gz")
HIGHEST = lax.Precision.HIGHEST
NZ, BU, PB, NY = 16, 64, 16, 32
ZL, YL, XL, CH = 8, 2, 4, 32
RU, RP = NZ * BU, NZ * PB
HU, HP = ZL * BU, ZL * PB
WIDE = HU + HP
LANES = 128
BLOCKS = WIDE // LANES
STEP = 2 * BLOCKS * 8
UNROLL = 8
f32, bf16 = jnp.float32, jnp.bfloat16


def place(variant, k):
    if variant == 0:
        cx, r = k // 8, k % 8
        cz = r if cx % 2 == 0 else 7 - r
    elif variant == 1:
        cz, r = k // 4, k % 4
        cx = 3 - r if cz % 2 == 0 else r
    elif variant == 2:
        q, r = k // 8, k % 8
        cx = 3 - q
        cz = 7 - r if q % 2 == 0 else r
    else:
        q, r = k // 4, k % 4
        cz = 7 - q
        cx = r if q % 2 == 0 else 3 - r
    return cx * 8 + cz


def slot_of(variant, k):
    a, b, c, d = (place(v, k) for v in range(4))
    return jnp.where(
        variant < 2, jnp.where(variant == 0, a, b), jnp.where(variant == 2, c, d)
    )


def ring():
    order = [g * CH + place(g % 4, k) for g in range(8) for k in range(CH)]
    up = [(order[i - 1], order[i]) for i in range(len(order))]
    return up, [(b, a) for a, b in up]


def at_end(group):
    plane = lax.axis_index("gy") + lax.axis_index("gz")
    return jnp.logical_and(lax.axis_index("gx") == group, plane == 0)


def pack_kernel(fu_hbm, fp_hbm, mask_hbm, out_ref, fu_ref, fp_ref, mask_ref, flip_ref, sem):
    part = 2 * BU * YL
    copies = [pltpu.make_async_copy(mask_hbm, mask_ref, sem.at[0])]
    for b in range(BLOCKS - 1):
        rows = pl.ds(b * part, part)
        copies.append(pltpu.make_async_copy(fu_hbm.at[rows], fu_ref.at[rows], sem.at[1 + b]))
    copies.append(pltpu.make_async_copy(fp_hbm, fp_ref, sem.at[BLOCKS]))
    for copy in copies:
        copy.start()
    copies[0].wait()
    variant = lax.axis_index("gx") % 4
    dests = [slot_of(variant, k) * BLOCKS for k in range(CH)]
    for b in range(BLOCKS):
        copies[1 + b].wait()
        for yl in range(YL):
            rows = []
            if b < BLOCKS - 1:
                for z in (2 * b, 2 * b + 1):
                    weight = (mask_ref[pl.ds(z * YL + yl, 1), :] != 0).astype(f32)
                    rows.append(fu_ref[pl.ds(z * BU * YL + yl, BU, stride=YL), :] * weight)
            else:
                last = lax.broadcasted_iota(jnp.int32, (PB, LANES), 0) == PB - 1
                for z in range(ZL):
                    weight = (mask_ref[pl.ds(z * YL + yl, 1), :] != 0).astype(f32)
                    fp = fp_ref[pl.ds(z * PB * YL + yl, PB, stride=YL), :] * weight
                    dead = jnp.broadcast_to(weight, (PB, LANES)) == 0.0
                    rows.append(jnp.where(jnp.logical_and(last, dead), jnp.inf, fp))
            flip_ref[yl, b] = jnp.concatenate(rows, axis=0).T
        for k in range(CH):
            out_ref[dests[k] + b] = jnp.concatenate(
                [flip_ref[yl, b, pl.ds(XL * k, XL), :] for yl in range(YL)], axis=0
            )


def spread_kernel(coef_ref, got_ref, fu_ref, fp_ref, mask_ref, send_ref, rows_ref):
    theta_inv = coef_ref[pl.ds(0, 1), pl.ds(0, LANES)]
    for half in range(2):
        for b in range(BLOCKS):
            for x in range(XL):
                for yl in range(YL):
                    rows_ref[b, pl.ds(x * NY + yl, CH // 2, stride=YL), :] = got_ref[
                        pl.ds((half * BLOCKS + b) * 8 + yl * XL + x, CH // 2, stride=STEP), :
                    ]
            flat = rows_ref[b].T
            if b < BLOCKS - 1:
                at = pl.ds(half * HU + b * LANES, LANES)
                fu_ref[at, :] = flat
                send_ref[at, :] = (flat * theta_inv).astype(bf16)
            else:
                fp_ref[pl.ds(half * HP, HP), :] = flat
    marks = fp_ref[pl.ds(PB - 1, NZ, stride=PB), :]
    weight = jnp.where(marks == jnp.inf, 0.0, 1.0)
    mask_ref[...] = weight
    send_ref[pl.ds(RU, NZ), :] = weight.astype(bf16)
    fp_ref[...] = jnp.where(fp_ref[...] == jnp.inf, 0.0, fp_ref[...])


LOW, HIGH, OWN, EDGE = 0, 1, 2, 3
WIDTH = 4 * LANES


def block(b, count=1):
    return pl.ds(b * LANES, count * LANES)


def lane_of(rows):
    return lax.broadcasted_iota(jnp.int32, (rows, LANES), 1)


def edge_of(low, high):
    return jnp.where(lane_of(low.shape[0]) < LANES // 2, high, low)


def stack_of(z64, w_ref, mode):
    lane = lane_of(BU)
    y = lane % NY
    ins = {"wide": (LOW, HIGH, OWN), "shrink": (LOW, HIGH, OWN), "ring": (OWN, EDGE),
           "own": (OWN, EDGE)}[mode]
    outs = {"wide": (LOW, HIGH, OWN), "shrink": (OWN, EDGE), "ring": (OWN, EDGE),
            "own": (OWN,)}[mode]
    rows = pl.ds(z64 + BU, BU)
    part = {b: w_ref[rows, block(b)] for b in sorted(set(ins) | set(outs))}
    up = {b: pltpu.roll(part[b], NY, 1) for b in ins}
    down = {b: pltpu.roll(part[b], LANES - NY, 1) for b in ins}
    zero = jnp.zeros_like(part[OWN])
    first, half, tail = lane < NY, lane < LANES // 2, lane >= LANES - NY
    if mode in ("wide", "shrink"):
        below = {LOW: up[LOW], OWN: jnp.where(first, up[LOW], up[OWN])}
        above = {HIGH: down[HIGH], OWN: jnp.where(tail, down[HIGH], down[OWN])}
        if mode == "wide":
            below[HIGH] = jnp.where(first, up[OWN], up[HIGH])
            above[LOW] = jnp.where(tail, down[OWN], down[LOW])
        else:
            below[EDGE] = jnp.where(first, up[OWN], jnp.where(half, up[HIGH], up[LOW]))
            above[EDGE] = jnp.where(tail, down[OWN], jnp.where(half, down[HIGH], down[LOW]))
    else:
        below = {OWN: jnp.where(first, up[EDGE], up[OWN]), EDGE: jnp.where(first, up[OWN], up[EDGE])}
        above = {OWN: jnp.where(tail, down[EDGE], down[OWN]),
                 EDGE: jnp.where(tail, down[OWN], down[EDGE])}
    columns = []
    for b in outs:
        below_y = jnp.where(y == 0, zero, pltpu.roll(part[b], 1, 1))
        above_y = jnp.where(y == NY - 1, zero, pltpu.roll(part[b], LANES - 1, 1))
        columns.append(jnp.concatenate([below_y, above_y, below[b], above[b]], axis=0))
    depth = w_ref[pl.ds(z64, 3 * BU), block(outs[0], len(outs))]
    return [jnp.concatenate(columns, axis=1), depth]


def layers_of(group):
    return [group * UNROLL + i for i in range(UNROLL)]


def sweep(k, mode, begin, last, refs, old, new):
    coef_ref, lm_ref, table_ref, mask_ref, state = refs
    count = {"wide": 3, "own": 1}.get(mode, 2)
    lanes = block(LOW if mode == "wide" else OWN, count)
    inner = block(0, min(count, 2))
    keep = coef_ref[pl.ds(2 + 2 * k, 1), block(0, count)]
    scale = coef_ref[pl.ds(3 + 2 * k, 1), block(0, count)]

    def group(g, carry):
        for z in layers_of(g):
            z64 = pl.multiple_of(z * BU, BU)
            table = table_ref[lm_ref[z]]
            stack = jnp.concatenate(stack_of(z64, old, mode), axis=0)
            product = jnp.dot(table[:, : 7 * BU], stack, preferred_element_type=f32)
            rows = pl.ds(z64, BU)
            if begin is None:
                r, d, s = [ref[rows, inner] for ref in state]
            else:
                r, d = begin(rows)
                s = d
            r = r - product * mask_ref[z, pl.ds(0, 1), lanes]
            d = keep * d + scale * r
            s = s + d
            if last is not None:
                last(z64, s)
                continue
            here = pl.ds(z64 + BU, BU)
            if mode == "wide":
                w = d.astype(bf16)
                new[here, block(LOW, 3)] = w
                new[here, block(EDGE)] = edge_of(w[:, :LANES], w[:, LANES : 2 * LANES])
                for ref, v in zip(state, (r, d, s)):
                    ref[rows, block(0)] = v[:, 2 * LANES :]
                    ref[rows, block(1)] = edge_of(v[:, :LANES], v[:, LANES : 2 * LANES])
            else:
                new[here, lanes] = d.astype(bf16)
                for ref, v in zip(state, (r, d, s)):
                    ref[rows, inner] = v
        return carry

    lax.fori_loop(0, NZ // UNROLL, group, 0)


def starter(coef_ref, own_ref, w_ref, wide):
    theta_inv = coef_ref[pl.ds(0, 1), block(0)]
    theta = coef_ref[pl.ds(1, 1), block(0)]

    def begin(rows):
        r = own_ref[rows, :]
        d = r * theta_inv
        here = pl.ds(rows.start + BU, BU)
        if wide:
            low = w_ref[here, block(LOW)].astype(f32)
            high = w_ref[here, block(HIGH)].astype(f32)
            return (
                jnp.concatenate([low * theta, high * theta, r], axis=1),
                jnp.concatenate([low, high, d], axis=1),
            )
        edge = w_ref[here, block(EDGE)].astype(f32)
        return (
            jnp.concatenate([r, edge * theta], axis=1),
            jnp.concatenate([d, edge], axis=1),
        )

    return begin


def widen(wide_ref, mask_ref, low_ref, high_ref):
    low = low_ref[pl.ds(RU, NZ), :].astype(f32) * jnp.where(at_end(0), 0.0, 1.0)
    high = high_ref[pl.ds(RU, NZ), :].astype(f32) * jnp.where(at_end(7), 0.0, 1.0)
    whole = jnp.concatenate([low, high, mask_ref[...], edge_of(low, high)], axis=1)
    for z in range(NZ):
        wide_ref[z] = jnp.broadcast_to(whole[z : z + 1], (8, WIDTH))


def pad_in(w_refs, low_ref, high_ref, own_ref, with_edge):
    edge = jnp.zeros((BU, WIDTH), bf16)
    for w_ref in w_refs:
        w_ref[pl.ds(0, BU), :] = edge
        w_ref[pl.ds(RU + BU, BU), :] = edge
    for b, src in ((LOW, low_ref), (HIGH, high_ref), (OWN, own_ref)):
        w_refs[0][pl.ds(BU, RU), block(b)] = src[pl.ds(0, RU), :]
    inner = pl.ds(BU, RU)
    for b, group in ((LOW, 0), (HIGH, 7)):

        @pl.when(at_end(group))
        def _():
            w_refs[0][inner, block(b)] = jnp.zeros((RU, LANES), bf16)

    if with_edge:
        w_refs[0][inner, block(EDGE)] = edge_of(
            w_refs[0][inner, block(LOW)], w_refs[0][inner, block(HIGH)]
        )


def thirds(v):
    high = v.astype(bf16)
    low = (v - high.astype(f32)).astype(bf16)
    return [high, low, high]


def halves(v):
    high = v.astype(bf16)
    return high, (v - high.astype(f32)).astype(bf16)


def couple(get, lm_ref, coup_ref, mask_ref, rest_ref, sign, q_ref):
    def group(g, carry):
        for z in layers_of(g):
            here = pl.ds(pl.multiple_of(z * PB, PB), PB)
            du = get(pl.multiple_of(z * BU, BU))
            q = jnp.dot(coup_ref[lm_ref[z]], jnp.concatenate(thirds(du), axis=0),
                        preferred_element_type=f32)
            q_ref[here, :] = q * mask_ref[z, pl.ds(0, 1), block(OWN)] + sign * rest_ref[here, :]
        return carry

    lax.fori_loop(0, NZ // UNROLL, group, 0)


def bands(schur_ref, q_ref):
    return jnp.dot(schur_ref[...], jnp.concatenate(thirds(q_ref[...]), axis=0),
                   preferred_element_type=f32)


def prep_kernel(spec_ref, off_ref, kb_ref, coup_ref, sinv_ref,
                coef_ref, table_ref, pair_ref, band_ref):
    lower = jnp.full((1, WIDTH), spec_ref[0], f32)
    upper = jnp.full((1, WIDTH), spec_ref[1], f32)
    theta = (upper + lower) / 2.0
    delta = (upper - lower) / 2.0
    sigma = theta / delta
    rho = 1.0 / sigma
    coef_ref[pl.ds(0, 1), :] = 1.0 / theta
    coef_ref[pl.ds(1, 1), :] = theta
    for k in range(SWEEPS - 1):
        rho_next = 1.0 / (2.0 * sigma - rho)
        coef_ref[pl.ds(2 + 2 * k, 1), :] = rho_next * rho
        coef_ref[pl.ds(3 + 2 * k, 1), :] = 2.0 * rho_next / delta
        rho = rho_next
    for m in range(4):
        high, low = halves(coup_ref[m])
        pair_ref[m] = jnp.concatenate([high, high, low], axis=1)
        high, low = halves(coup_ref[m].T)
        blocks = [kb_ref[m, d] for d in (3, 4, 5, 6, 1, 0, 2)]
        pad = jnp.zeros((BU, PB), bf16)
        table_ref[m] = jnp.concatenate(blocks + [high, high, low, pad], axis=1)
    row = lax.broadcasted_iota(jnp.int32, (PB, RP), 0)
    col = lax.broadcasted_iota(jnp.int32, (PB, RP), 1)
    spread = (col % PB == row).astype(f32).astype(bf16)
    gap = (lax.broadcasted_iota(jnp.int32, (RP, RP), 1) // PB
           - lax.broadcasted_iota(jnp.int32, (RP, RP), 0) // PB)
    total = [jnp.zeros((RP, RP), f32)] * 2
    for k in range(8):
        hit = gap == off_ref[k]
        for i, part in enumerate(halves(sinv_ref[k].reshape(RP, PB))):
            wide = jnp.dot(part, spread, preferred_element_type=f32)
            total[i] = total[i] + jnp.where(hit, wide, 0.0)
    high, low = total[0].astype(bf16), total[1].astype(bf16)
    band_ref[...] = jnp.concatenate([high, high, low], axis=1)


def first_kernel(lm_ref, coef_ref, table_ref, coup_ref, schur_ref,
                 fu_ref, fp_ref, mask_ref, own_ref, low_ref, high_ref,
                 ru_ref, du_ref, dp_ref, q_ref, send_ref,
                 wide_ref, d_ref, r_ref, s_ref, wa_ref, wb_ref):
    widen(wide_ref, mask_ref, low_ref, high_ref)
    pad_in((wa_ref, wb_ref), low_ref, high_ref, own_ref, False)
    refs = (coef_ref, lm_ref, table_ref, wide_ref, (r_ref, d_ref, s_ref))
    begin = starter(coef_ref, fu_ref, wa_ref, True)

    def last(z64, s):
        wb_ref[pl.ds(z64 + BU, BU), block(OWN, 2)] = s.astype(bf16)
        du_ref[pl.ds(z64, BU), :] = s[:, :LANES]

    sweep(0, "wide", begin, None, refs, wa_ref, wb_ref)
    sweep(1, "shrink", None, None, refs, wb_ref, wa_ref)
    sweep(2, "ring", None, last, refs, wa_ref, wb_ref)
    couple(lambda z64: du_ref[pl.ds(z64, BU), :], lm_ref, coup_ref, wide_ref, fp_ref, -1.0, q_ref)
    dp_ref[...] = bands(schur_ref, q_ref)
    theta_inv = coef_ref[pl.ds(0, 1), block(0)]

    def finish(g, carry):
        for z in layers_of(g):
            z64 = pl.multiple_of(z * BU, BU)
            here = pl.ds(pl.multiple_of(z * PB, PB), PB)
            weight = wide_ref[z, pl.ds(0, 1), block(OWN)]
            dp = dp_ref[here, :] * weight
            dp_ref[here, :] = dp
            stack = stack_of(z64, wb_ref, "own") + thirds(dp)
            product = jnp.dot(table_ref[lm_ref[z]][:, : 7 * BU + 3 * PB],
                              jnp.concatenate(stack, axis=0), preferred_element_type=f32)
            rows = pl.ds(z64, BU)
            ru = fu_ref[rows, :] - product * weight
            ru_ref[rows, :] = ru
            send_ref[rows, :] = (ru * theta_inv).astype(bf16)
        return carry

    lax.fori_loop(0, NZ // UNROLL, finish, 0)


def second_kernel(lm_ref, coef_ref, table_ref, coup_ref, schur_ref,
                  fu_ref, mask_ref, ru_ref, du_ref, dp_ref, q_ref, own_ref, low_ref,
                  high_ref, mlow_ref, mhigh_ref, out_ref,
                  wide_ref, d_ref, r_ref, s_ref, wa_ref, wb_ref, p_ref, rows_ref, sort_ref):
    widen(wide_ref, mask_ref, mlow_ref, mhigh_ref)
    pad_in((wa_ref, wb_ref), low_ref, high_ref, own_ref, True)
    refs = (coef_ref, lm_ref, table_ref, wide_ref, (r_ref, d_ref, s_ref))
    begin = starter(coef_ref, ru_ref, wa_ref, False)
    own = block(0)

    def last(z64, s):
        s_ref[pl.ds(z64, BU), own] = s

    sweep(0, "shrink", begin, None, refs, wa_ref, wb_ref)
    sweep(1, "ring", None, None, refs, wb_ref, wa_ref)
    sweep(2, "own", None, last, refs, wa_ref, wb_ref)
    couple(lambda z64: s_ref[pl.ds(z64, BU), own], lm_ref, coup_ref, wide_ref, q_ref, 1.0, p_ref)
    p_ref[...] = bands(schur_ref, p_ref)
    for half in range(2):
        for b in range(BLOCKS):
            if b < BLOCKS - 1:
                rows = pl.ds(half * HU + b * LANES, LANES)
                flat = s_ref[rows, own] + du_ref[rows, :] - fu_ref[rows, :]
            else:
                pressure = []
                for z in range(half * ZL, half * ZL + ZL):
                    here = pl.ds(z * PB, PB)
                    dp = p_ref[here, :] * mask_ref[pl.ds(z, 1), :]
                    pressure.append(dp + dp_ref[here, :])
                flat = jnp.concatenate(pressure, axis=0)
            rows_ref[b] = flat.T
            for x in range(XL):
                for yl in range(YL):
                    sort_ref[
                        pl.ds((half * BLOCKS + b) * 8 + yl * XL + x, CH // 2, stride=STEP), :
                    ] = rows_ref[b, pl.ds(x * NY + yl, CH // 2, stride=YL), :]
    out_ref[...] = sort_ref[...].astype(bf16)


def unpack_kernel(got_ref, fu_ref, mask_ref, disp_ref, pres_ref, rows_ref):
    variant = lax.axis_index("gx") % 4
    for k in range(CH):
        src = slot_of(variant, k) * BLOCKS
        for b in range(BLOCKS):
            piece = got_ref[src + b].astype(f32)
            for yl in range(YL):
                rows_ref[yl, b, pl.ds(XL * k, XL), :] = piece[yl * XL : yl * XL + XL]
    for yl in range(YL):
        for b in range(BLOCKS - 1):
            flat = rows_ref[yl, b].T
            for i in range(2):
                z = 2 * b + i
                weight = (mask_ref[pl.ds(z * YL + yl, 1), :] != 0).astype(f32)
                at = pl.ds(z * BU * YL + yl, BU, stride=YL)
                disp_ref[at, :] = flat[i * BU : i * BU + BU] + fu_ref[at, :] * weight
        pres_ref[pl.ds(yl, HP, stride=YL), :] = rows_ref[yl, BLOCKS - 1].T


VM = pl.BlockSpec(memory_space=pltpu.VMEM)
SM = pl.BlockSpec(memory_space=pltpu.SMEM)


def call(kernel, scalars, arrays, outs, scratch, limit=24):
    return pl.pallas_call(
        kernel,
        out_shape=[jax.ShapeDtypeStruct(*o) for o in outs],
        in_specs=[SM] * len(scalars) + [VM] * len(arrays),
        out_specs=[VM] * len(outs),
        scratch_shapes=[pltpu.VMEM(*s) for s in scratch],
        compiler_params=pltpu.CompilerParams(vmem_limit_bytes=limit << 20),
    )(*scalars, *arrays)


def body(force_u, force_p, cellmask, layer_mats, kblocks, bcoup, sinv, band_offsets, spectrum):
    up, down = ring()
    other = lax.ppermute(layer_mats, "gz", [(0, 1), (1, 0)])
    fu_in = force_u.reshape(ZL * BU * YL, LANES)
    fp_in = force_p.reshape(ZL * PB * YL, LANES)
    mask_in = cellmask.reshape(ZL * YL, LANES)
    coefs, table, pair, matrix = call(
        prep_kernel, [spectrum, band_offsets], [kblocks, bcoup, sinv],
        [((8, WIDTH), f32), ((4, BU, 8 * BU), bf16), ((4, PB, 3 * BU), bf16),
         ((RP, 3 * RP), bf16)], [],
    )

    packed = pl.pallas_call(
        pack_kernel,
        out_shape=jax.ShapeDtypeStruct((CH * BLOCKS, 8, LANES), f32),
        in_specs=[pl.BlockSpec(memory_space=pltpu.HBM)] * 3,
        out_specs=VM,
        scratch_shapes=[
            pltpu.VMEM(fu_in.shape, f32), pltpu.VMEM(fp_in.shape, f32),
            pltpu.VMEM(mask_in.shape, jnp.int32),
            pltpu.VMEM((YL, BLOCKS, LANES, LANES), f32), pltpu.SemaphoreType.DMA((BLOCKS + 1,)),
        ],
        compiler_params=pltpu.CompilerParams(vmem_limit_bytes=60 << 20),
    )(fu_in, fp_in, mask_in)
    packed, other = lax.optimization_barrier((packed, other))
    gz = lax.axis_index("gz")
    layers = jnp.where(
        gz == 0, jnp.concatenate([layer_mats, other]), jnp.concatenate([other, layer_mats])
    )
    got = lax.all_to_all(packed, PLANE, 0, 0, tiled=True)
    got, table, pair, matrix, coefs = lax.optimization_barrier(
        (got, table, pair, matrix, coefs)
    )
    fu, fp, mask, send = call(
        spread_kernel, [], [coefs, got.reshape(CH * BLOCKS * 8, LANES)],
        [((RU, LANES), f32), ((RP, LANES), f32), ((NZ, LANES), f32), ((RU + NZ, LANES), bf16)],
        [((BLOCKS, LANES, LANES), f32)],
    )
    low = lax.ppermute(send, ALL, up)
    high = lax.ppermute(send, ALL, down)
    wide = [((NZ, 8, WIDTH), f32)] + [((RU, 2 * LANES), f32)] * 3 + [
        ((RU + 2 * BU, WIDTH), bf16)
    ] * 2
    ru, du, dp, q, send2 = call(
        first_kernel, [layers],
        [coefs, table, pair, matrix, fu, fp, mask, send, low, high],
        [((RU, LANES), f32), ((RU, LANES), f32), ((RP, LANES), f32), ((RP, LANES), f32),
         ((RU, LANES), bf16)],
        wide,
    )
    low2 = lax.ppermute(send2, ALL, up)
    high2 = lax.ppermute(send2, ALL, down)
    (back,) = call(
        second_kernel, [layers],
        [coefs, table, pair, matrix, fu, mask, ru, du, dp, q, send2, low2, high2, low, high],
        [((CH * BLOCKS * 8, LANES), bf16)],
        wide + [((RP, LANES), f32), ((BLOCKS, LANES, LANES), f32),
                ((CH * BLOCKS * 8, LANES), f32)],
    )
    home = lax.all_to_all(back.reshape(CH * BLOCKS, 8, LANES), PLANE, 0, 0, tiled=True)
    disp, pres = call(
        unpack_kernel, [], [home, fu_in, mask_in],
        [((ZL * BU * YL, LANES), f32), ((ZL * PB * YL, LANES), f32)],
        [((YL, BLOCKS, LANES, LANES), f32)],
    )
    return (disp.reshape(ZL, BU, YL, LANES), pres.reshape(ZL, PB, YL, LANES))


def solution(mesh):
    in_specs = (
        P("gz", None, "gy", "gx"),
        P("gz", None, "gy", "gx"),
        P("gz", "gy", "gx"),
        P("gz"),
        P(),
        P(),
        P(),
        P(),
        P(),
    )
    out_specs = (P("gz", None, "gy", "gx"), P("gz", None, "gy", "gx"))
    return jax.shard_map(body, mesh=mesh, in_specs=in_specs, out_specs=out_specs, check_vma=False)
```

```python
import jax
import jax.numpy as jnp
from jax import lax
from jax.experimental import pallas as pl
from jax.experimental.pallas import tpu as pltpu
from jax.sharding import PartitionSpec as P

SWEEPS = 4
ALL = ("gx", "gy", "gz")
PLANE = ("gy", "gz")
HIGHEST = lax.Precision.HIGHEST
NZ, BU, PB, NY = 16, 64, 16, 32
ZL, YL, XL, CH = 8, 2, 4, 32
RU, RP = NZ * BU, NZ * PB
HU, HP = ZL * BU, ZL * PB
WIDE = HU + HP
LANES = 128
BLOCKS = WIDE // LANES
STEP = 2 * BLOCKS * 8
UNROLL = {"wide": 16, "shrink": 16, "ring": 16, "own": 16}
f32, bf16 = jnp.float32, jnp.bfloat16


def place(variant, k):
    if variant == 0:
        cx, r = k // 8, k % 8
        cz = r if cx % 2 == 0 else 7 - r
    elif variant == 1:
        cz, r = k // 4, k % 4
        cx = 3 - r if cz % 2 == 0 else r
    elif variant == 2:
        q, r = k // 8, k % 8
        cx = 3 - q
        cz = 7 - r if q % 2 == 0 else r
    else:
        q, r = k // 4, k % 4
        cz = 7 - q
        cx = r if q % 2 == 0 else 3 - r
    return cx * 8 + cz


def slot_of(variant, k):
    a, b, c, d = (place(v, k) for v in range(4))
    return jnp.where(
        variant < 2, jnp.where(variant == 0, a, b), jnp.where(variant == 2, c, d)
    )


def ring():
    order = [g * CH + place(g % 4, k) for g in range(8) for k in range(CH)]
    up = [(order[i - 1], order[i]) for i in range(len(order))]
    return up, [(b, a) for a, b in up]


def at_end(group):
    plane = lax.axis_index("gy") + lax.axis_index("gz")
    return jnp.logical_and(lax.axis_index("gx") == group, plane == 0)


def pack_kernel(fu_hbm, fp_hbm, mask_hbm, out_ref, fu_ref, fp_ref, mask_ref, flip_ref, sem):
    part = 2 * BU * YL
    copies = [pltpu.make_async_copy(mask_hbm, mask_ref, sem.at[0])]
    for b in range(BLOCKS - 1):
        rows = pl.ds(b * part, part)
        copies.append(pltpu.make_async_copy(fu_hbm.at[rows], fu_ref.at[rows], sem.at[1 + b]))
    copies.append(pltpu.make_async_copy(fp_hbm, fp_ref, sem.at[BLOCKS]))
    for copy in copies:
        copy.start()
    copies[0].wait()
    variant = lax.axis_index("gx") % 4
    dests = [slot_of(variant, k) * BLOCKS for k in range(CH)]
    for b in range(BLOCKS):
        copies[1 + b].wait()
        for yl in range(YL):
            rows = []
            if b < BLOCKS - 1:
                for z in (2 * b, 2 * b + 1):
                    weight = (mask_ref[pl.ds(z * YL + yl, 1), :] != 0).astype(f32)
                    rows.append(fu_ref[pl.ds(z * BU * YL + yl, BU, stride=YL), :] * weight)
            else:
                last = lax.broadcasted_iota(jnp.int32, (PB, LANES), 0) == PB - 1
                for z in range(ZL):
                    weight = (mask_ref[pl.ds(z * YL + yl, 1), :] != 0).astype(f32)
                    fp = fp_ref[pl.ds(z * PB * YL + yl, PB, stride=YL), :] * weight
                    dead = jnp.broadcast_to(weight, (PB, LANES)) == 0.0
                    rows.append(jnp.where(jnp.logical_and(last, dead), jnp.inf, fp))
            flip_ref[yl, b] = jnp.concatenate(rows, axis=0).T
        for k in range(CH):
            out_ref[dests[k] + b] = jnp.concatenate(
                [flip_ref[yl, b, pl.ds(XL * k, XL), :] for yl in range(YL)], axis=0
            )


def spread_kernel(spec_ref, got_ref, fu_ref, fp_ref, mask_ref, send_ref, rows_ref):
    theta_inv = 1.0 / (jnp.full((1, LANES), spec_ref[1] + spec_ref[0], f32) / 2.0)
    for half in range(2):
        for b in range(BLOCKS):
            for x in range(XL):
                for yl in range(YL):
                    rows_ref[b, pl.ds(x * NY + yl, CH // 2, stride=YL), :] = got_ref[
                        pl.ds((half * BLOCKS + b) * 8 + yl * XL + x, CH // 2, stride=STEP), :
                    ]
            flat = rows_ref[b].T
            if b < BLOCKS - 1:
                at = pl.ds(half * HU + b * LANES, LANES)
                fu_ref[at, :] = flat
                send_ref[at, :] = (flat * theta_inv).astype(bf16)
            else:
                fp_ref[pl.ds(half * HP, HP), :] = flat
    marks = fp_ref[pl.ds(PB - 1, NZ, stride=PB), :]
    weight = jnp.where(marks == jnp.inf, 0.0, 1.0)
    mask_ref[...] = weight
    send_ref[pl.ds(RU, NZ), :] = weight.astype(bf16)
    fp_ref[...] = jnp.where(fp_ref[...] == jnp.inf, 0.0, fp_ref[...])


LOW, HIGH, OWN, EDGE = 0, 1, 2, 3
WIDTH = 4 * LANES


def block(b, count=1):
    return pl.ds(b * LANES, count * LANES)


def lane_of(rows):
    return lax.broadcasted_iota(jnp.int32, (rows, LANES), 1)


def edge_of(low, high):
    return jnp.where(lane_of(low.shape[0]) < LANES // 2, high, low)


def stack_of(z64, w_ref, mode):
    lane = lane_of(BU)
    y = lane % NY
    ins = {"wide": (LOW, HIGH, OWN), "shrink": (LOW, HIGH, OWN), "ring": (OWN, EDGE),
           "own": (OWN, EDGE)}[mode]
    outs = {"wide": (LOW, HIGH, OWN), "shrink": (OWN, EDGE), "ring": (OWN, EDGE),
            "own": (OWN,)}[mode]
    rows = pl.ds(z64 + BU, BU)
    part = {b: w_ref[rows, block(b)] for b in sorted(set(ins) | set(outs))}
    up = {b: pltpu.roll(part[b], NY, 1) for b in ins}
    down = {b: pltpu.roll(part[b], LANES - NY, 1) for b in ins}
    zero = jnp.zeros_like(part[OWN])
    first, half, tail = lane < NY, lane < LANES // 2, lane >= LANES - NY
    if mode in ("wide", "shrink"):
        below = {LOW: up[LOW], OWN: jnp.where(first, up[LOW], up[OWN])}
        above = {HIGH: down[HIGH], OWN: jnp.where(tail, down[HIGH], down[OWN])}
        if mode == "wide":
            below[HIGH] = jnp.where(first, up[OWN], up[HIGH])
            above[LOW] = jnp.where(tail, down[OWN], down[LOW])
        else:
            below[EDGE] = jnp.where(first, up[OWN], jnp.where(half, up[HIGH], up[LOW]))
            above[EDGE] = jnp.where(tail, down[OWN], jnp.where(half, down[HIGH], down[LOW]))
    else:
        below = {OWN: jnp.where(first, up[EDGE], up[OWN]), EDGE: jnp.where(first, up[OWN], up[EDGE])}
        above = {OWN: jnp.where(tail, down[EDGE], down[OWN]),
                 EDGE: jnp.where(tail, down[OWN], down[EDGE])}
    columns = []
    for b in outs:
        below_y = jnp.where(y == 0, zero, pltpu.roll(part[b], 1, 1))
        above_y = jnp.where(y == NY - 1, zero, pltpu.roll(part[b], LANES - 1, 1))
        columns.append(jnp.concatenate([below_y, above_y, below[b], above[b]], axis=0))
    depth = w_ref[pl.ds(z64, 3 * BU), block(outs[0], len(outs))]
    return [jnp.concatenate(columns, axis=1), depth]


def layers_of(group, unroll):
    return [group * unroll + i for i in range(unroll)]


def sweep(k, mode, begin, last, refs, old, new):
    unroll = UNROLL[mode]
    coef_ref, lm_ref, table_ref, mask_ref, state = refs
    count = {"wide": 3, "own": 1}.get(mode, 2)
    lanes = block(LOW if mode == "wide" else OWN, count)
    inner = block(0, min(count, 2))
    keep = coef_ref[pl.ds(2 + 2 * k, 1), block(0, count)]
    scale = coef_ref[pl.ds(3 + 2 * k, 1), block(0, count)]

    def group(g, carry):
        for z in layers_of(g, unroll):
            z64 = pl.multiple_of(z * BU, BU)
            table = table_ref[lm_ref[z]]
            stack = jnp.concatenate(stack_of(z64, old, mode), axis=0)
            product = jnp.dot(table[:, : 7 * BU], stack, preferred_element_type=f32)
            rows = pl.ds(z64, BU)
            if begin is None:
                r, d, s = [ref[rows, inner] for ref in state]
            else:
                r, d = begin(rows)
                s = d
            r = r - product * mask_ref[z, pl.ds(0, 1), lanes]
            d = keep * d + scale * r
            s = s + d
            if last is not None:
                last(z64, s)
                continue
            here = pl.ds(z64 + BU, BU)
            if mode == "wide":
                w = d.astype(bf16)
                new[here, block(LOW, 3)] = w
                new[here, block(EDGE)] = edge_of(w[:, :LANES], w[:, LANES : 2 * LANES])
                for ref, v in zip(state, (r, d, s)):
                    ref[rows, block(0)] = v[:, 2 * LANES :]
                    ref[rows, block(1)] = edge_of(v[:, :LANES], v[:, LANES : 2 * LANES])
            else:
                new[here, lanes] = d.astype(bf16)
                for ref, v in zip(state, (r, d, s)):
                    ref[rows, inner] = v
        return carry

    lax.fori_loop(0, NZ // unroll, group, 0)


def starter(coef_ref, own_ref, w_ref, wide):
    theta_inv = coef_ref[pl.ds(0, 1), block(0)]
    theta = coef_ref[pl.ds(1, 1), block(0)]

    def begin(rows):
        r = own_ref[rows, :]
        d = r * theta_inv
        here = pl.ds(rows.start + BU, BU)
        if wide:
            low = w_ref[here, block(LOW)].astype(f32)
            high = w_ref[here, block(HIGH)].astype(f32)
            return (
                jnp.concatenate([low * theta, high * theta, r], axis=1),
                jnp.concatenate([low, high, d], axis=1),
            )
        edge = w_ref[here, block(EDGE)].astype(f32)
        return (
            jnp.concatenate([r, edge * theta], axis=1),
            jnp.concatenate([d, edge], axis=1),
        )

    return begin


def widen(wide_ref, mask_ref, low_ref, high_ref):
    low = low_ref[pl.ds(RU, NZ), :].astype(f32) * jnp.where(at_end(0), 0.0, 1.0)
    high = high_ref[pl.ds(RU, NZ), :].astype(f32) * jnp.where(at_end(7), 0.0, 1.0)
    whole = jnp.concatenate([low, high, mask_ref[...], edge_of(low, high)], axis=1)
    for z in range(NZ):
        wide_ref[z] = jnp.broadcast_to(whole[z : z + 1], (8, WIDTH))


def pad_in(w_refs, low_ref, high_ref, own_ref, with_edge):
    edge = jnp.zeros((BU, WIDTH), bf16)
    for w_ref in w_refs:
        w_ref[pl.ds(0, BU), :] = edge
        w_ref[pl.ds(RU + BU, BU), :] = edge
    for b, src in ((LOW, low_ref), (HIGH, high_ref), (OWN, own_ref)):
        w_refs[0][pl.ds(BU, RU), block(b)] = src[pl.ds(0, RU), :]
    inner = pl.ds(BU, RU)
    for b, group in ((LOW, 0), (HIGH, 7)):

        @pl.when(at_end(group))
        def _():
            w_refs[0][inner, block(b)] = jnp.zeros((RU, LANES), bf16)

    if with_edge:
        w_refs[0][inner, block(EDGE)] = edge_of(
            w_refs[0][inner, block(LOW)], w_refs[0][inner, block(HIGH)]
        )


def thirds(v):
    high = v.astype(bf16)
    low = (v - high.astype(f32)).astype(bf16)
    return [high, low, high]


def halves(v):
    high = v.astype(bf16)
    return high, (v - high.astype(f32)).astype(bf16)


def couple(get, lm_ref, coup_ref, mask_ref, rest_ref, sign, q_ref):
    def group(g, carry):
        for z in layers_of(g, NZ):
            here = pl.ds(pl.multiple_of(z * PB, PB), PB)
            du = get(pl.multiple_of(z * BU, BU))
            q = jnp.dot(coup_ref[lm_ref[z]], jnp.concatenate(thirds(du), axis=0),
                        preferred_element_type=f32)
            q_ref[here, :] = q * mask_ref[z, pl.ds(0, 1), block(OWN)] + sign * rest_ref[here, :]
        return carry

    lax.fori_loop(0, 1, group, 0)


def bands(schur_ref, q_ref):
    return jnp.dot(schur_ref[...], jnp.concatenate(thirds(q_ref[...]), axis=0),
                   preferred_element_type=f32)


def prep_kernel(spec_ref, off_ref, kb_ref, coup_ref, sinv_ref,
                coef_ref, table_ref, pair_ref, band_ref):
    lower = jnp.full((1, WIDTH), spec_ref[0], f32)
    upper = jnp.full((1, WIDTH), spec_ref[1], f32)
    theta = (upper + lower) / 2.0
    delta = (upper - lower) / 2.0
    sigma = theta / delta
    rho = 1.0 / sigma
    coef_ref[pl.ds(0, 1), :] = 1.0 / theta
    coef_ref[pl.ds(1, 1), :] = theta
    for k in range(SWEEPS - 1):
        rho_next = 1.0 / (2.0 * sigma - rho)
        coef_ref[pl.ds(2 + 2 * k, 1), :] = rho_next * rho
        coef_ref[pl.ds(3 + 2 * k, 1), :] = 2.0 * rho_next / delta
        rho = rho_next
    for m in range(4):
        high, low = halves(coup_ref[m])
        pair_ref[m] = jnp.concatenate([high, high, low], axis=1)
        high, low = halves(coup_ref[m].T)
        blocks = [kb_ref[m, d] for d in (3, 4, 5, 6, 1, 0, 2)]
        pad = jnp.zeros((BU, PB), bf16)
        table_ref[m] = jnp.concatenate(blocks + [high, high, low, pad], axis=1)
    row = lax.broadcasted_iota(jnp.int32, (PB, RP), 0)
    col = lax.broadcasted_iota(jnp.int32, (PB, RP), 1)
    spread = (col % PB == row).astype(f32).astype(bf16)
    gap = (lax.broadcasted_iota(jnp.int32, (RP, RP), 1) // PB
           - lax.broadcasted_iota(jnp.int32, (RP, RP), 0) // PB)
    total = [jnp.zeros((RP, RP), f32)] * 2
    for k in range(8):
        hit = gap == off_ref[k]
        for i, part in enumerate(halves(sinv_ref[k].reshape(RP, PB))):
            wide = jnp.dot(part, spread, preferred_element_type=f32)
            total[i] = total[i] + jnp.where(hit, wide, 0.0)
    high, low = total[0].astype(bf16), total[1].astype(bf16)
    band_ref[...] = jnp.concatenate([high, high, low], axis=1)


def first_kernel(lm_ref, coef_ref, table_ref, coup_ref, schur_ref,
                 fu_ref, fp_ref, mask_ref, own_ref, low_ref, high_ref,
                 ru_ref, du_ref, dp_ref, q_ref, send_ref,
                 wide_ref, d_ref, r_ref, s_ref, wa_ref, wb_ref):
    widen(wide_ref, mask_ref, low_ref, high_ref)
    pad_in((wa_ref, wb_ref), low_ref, high_ref, own_ref, False)
    refs = (coef_ref, lm_ref, table_ref, wide_ref, (r_ref, d_ref, s_ref))
    begin = starter(coef_ref, fu_ref, wa_ref, True)

    def last(z64, s):
        wb_ref[pl.ds(z64 + BU, BU), block(OWN, 2)] = s.astype(bf16)
        du_ref[pl.ds(z64, BU), :] = s[:, :LANES]

    sweep(0, "wide", begin, None, refs, wa_ref, wb_ref)
    sweep(1, "shrink", None, None, refs, wb_ref, wa_ref)
    sweep(2, "ring", None, last, refs, wa_ref, wb_ref)
    couple(lambda z64: du_ref[pl.ds(z64, BU), :], lm_ref, coup_ref, wide_ref, fp_ref, -1.0, q_ref)
    dp_ref[...] = bands(schur_ref, q_ref)
    theta_inv = coef_ref[pl.ds(0, 1), block(0)]

    def finish(g, carry):
        for z in layers_of(g, 8):
            z64 = pl.multiple_of(z * BU, BU)
            here = pl.ds(pl.multiple_of(z * PB, PB), PB)
            weight = wide_ref[z, pl.ds(0, 1), block(OWN)]
            dp = dp_ref[here, :] * weight
            dp_ref[here, :] = dp
            stack = stack_of(z64, wb_ref, "own") + thirds(dp)
            product = jnp.dot(table_ref[lm_ref[z]][:, : 7 * BU + 3 * PB],
                              jnp.concatenate(stack, axis=0), preferred_element_type=f32)
            rows = pl.ds(z64, BU)
            ru = fu_ref[rows, :] - product * weight
            ru_ref[rows, :] = ru
            send_ref[rows, :] = (ru * theta_inv).astype(bf16)
        return carry

    lax.fori_loop(0, 2, finish, 0)


def second_kernel(lm_ref, coef_ref, table_ref, coup_ref, schur_ref,
                  fu_ref, mask_ref, ru_ref, du_ref, dp_ref, q_ref, own_ref, low_ref,
                  high_ref, mlow_ref, mhigh_ref, out_ref,
                  wide_ref, d_ref, r_ref, s_ref, wa_ref, wb_ref, p_ref, rows_ref, sort_ref):
    widen(wide_ref, mask_ref, mlow_ref, mhigh_ref)
    pad_in((wa_ref, wb_ref), low_ref, high_ref, own_ref, True)
    refs = (coef_ref, lm_ref, table_ref, wide_ref, (r_ref, d_ref, s_ref))
    begin = starter(coef_ref, ru_ref, wa_ref, False)
    own = block(0)

    def last(z64, s):
        s_ref[pl.ds(z64, BU), own] = s

    sweep(0, "shrink", begin, None, refs, wa_ref, wb_ref)
    sweep(1, "ring", None, None, refs, wb_ref, wa_ref)
    sweep(2, "own", None, last, refs, wa_ref, wb_ref)
    couple(lambda z64: s_ref[pl.ds(z64, BU), own], lm_ref, coup_ref, wide_ref, q_ref, 1.0, p_ref)
    p_ref[...] = bands(schur_ref, p_ref)
    for half in range(2):
        for b in range(BLOCKS):
            if b < BLOCKS - 1:
                rows = pl.ds(half * HU + b * LANES, LANES)
                flat = s_ref[rows, own] + du_ref[rows, :] - fu_ref[rows, :]
            else:
                pressure = []
                for z in range(half * ZL, half * ZL + ZL):
                    here = pl.ds(z * PB, PB)
                    dp = p_ref[here, :] * mask_ref[pl.ds(z, 1), :]
                    pressure.append(dp + dp_ref[here, :])
                flat = jnp.concatenate(pressure, axis=0)
            rows_ref[b] = flat.T
            for x in range(XL):
                for yl in range(YL):
                    sort_ref[
                        pl.ds((half * BLOCKS + b) * 8 + yl * XL + x, CH // 2, stride=STEP), :
                    ] = rows_ref[b, pl.ds(x * NY + yl, CH // 2, stride=YL), :]
    out_ref[...] = sort_ref[...].astype(bf16)


def unpack_kernel(got_ref, fu_ref, mask_ref, disp_ref, pres_ref, rows_ref):
    variant = lax.axis_index("gx") % 4
    for k in range(CH):
        src = slot_of(variant, k) * BLOCKS
        for b in range(BLOCKS):
            piece = got_ref[src + b].astype(f32)
            for yl in range(YL):
                rows_ref[yl, b, pl.ds(XL * k, XL), :] = piece[yl * XL : yl * XL + XL]
    for yl in range(YL):
        for b in range(BLOCKS - 1):
            flat = rows_ref[yl, b].T
            for i in range(2):
                z = 2 * b + i
                weight = (mask_ref[pl.ds(z * YL + yl, 1), :] != 0).astype(f32)
                at = pl.ds(z * BU * YL + yl, BU, stride=YL)
                disp_ref[at, :] = flat[i * BU : i * BU + BU] + fu_ref[at, :] * weight
        pres_ref[pl.ds(yl, HP, stride=YL), :] = rows_ref[yl, BLOCKS - 1].T


VM = pl.BlockSpec(memory_space=pltpu.VMEM)
SM = pl.BlockSpec(memory_space=pltpu.SMEM)


def call(kernel, scalars, arrays, outs, scratch, limit=24):
    return pl.pallas_call(
        kernel,
        out_shape=[jax.ShapeDtypeStruct(*o) for o in outs],
        in_specs=[SM] * len(scalars) + [VM] * len(arrays),
        out_specs=[VM] * len(outs),
        scratch_shapes=[pltpu.VMEM(*s) for s in scratch],
        compiler_params=pltpu.CompilerParams(vmem_limit_bytes=limit << 20),
    )(*scalars, *arrays)


def body(force_u, force_p, cellmask, layer_mats, kblocks, bcoup, sinv, band_offsets, spectrum):
    up, down = ring()
    other = lax.ppermute(layer_mats, "gz", [(0, 1), (1, 0)])
    fu_in = force_u.reshape(ZL * BU * YL, LANES)
    fp_in = force_p.reshape(ZL * PB * YL, LANES)
    mask_in = cellmask.reshape(ZL * YL, LANES)
    packed = pl.pallas_call(
        pack_kernel,
        out_shape=jax.ShapeDtypeStruct((CH * BLOCKS, 8, LANES), f32),
        in_specs=[pl.BlockSpec(memory_space=pltpu.HBM)] * 3,
        out_specs=VM,
        scratch_shapes=[
            pltpu.VMEM(fu_in.shape, f32), pltpu.VMEM(fp_in.shape, f32),
            pltpu.VMEM(mask_in.shape, jnp.int32),
            pltpu.VMEM((YL, BLOCKS, LANES, LANES), f32), pltpu.SemaphoreType.DMA((BLOCKS + 1,)),
        ],
        compiler_params=pltpu.CompilerParams(vmem_limit_bytes=24 << 20),
    )(*(pltpu.with_memory_space_constraint(v, pltpu.HBM) for v in (fu_in, fp_in, mask_in)))
    packed, other = lax.optimization_barrier((packed, other))
    gz = lax.axis_index("gz")
    layers = jnp.where(
        gz == 0, jnp.concatenate([layer_mats, other]), jnp.concatenate([other, layer_mats])
    )
    got = lax.all_to_all(packed, PLANE, 0, 0, tiled=True)
    fu, fp, mask, send = call(
        spread_kernel, [spectrum], [got.reshape(CH * BLOCKS * 8, LANES)],
        [((RU, LANES), f32), ((RP, LANES), f32), ((NZ, LANES), f32), ((RU + NZ, LANES), bf16)],
        [((BLOCKS, LANES, LANES), f32)],
    )
    send, spectrum = lax.optimization_barrier((send, spectrum))
    coefs, table, pair, matrix = call(
        prep_kernel, [spectrum, band_offsets], [kblocks, bcoup, sinv],
        [((8, WIDTH), f32), ((4, BU, 8 * BU), bf16), ((4, PB, 3 * BU), bf16),
         ((RP, 3 * RP), bf16)], [],
    )
    low = lax.ppermute(send, ALL, up)
    high = lax.ppermute(send, ALL, down)
    wide = [((NZ, 8, WIDTH), f32)] + [((RU, 2 * LANES), f32)] * 3 + [
        ((RU + 2 * BU, WIDTH), bf16)
    ] * 2
    ru, du, dp, q, send2 = call(
        first_kernel, [layers],
        [coefs, table, pair, matrix, fu, fp, mask, send, low, high],
        [((RU, LANES), f32), ((RU, LANES), f32), ((RP, LANES), f32), ((RP, LANES), f32),
         ((RU, LANES), bf16)],
        wide,
    )
    low2 = lax.ppermute(send2, ALL, up)
    high2 = lax.ppermute(send2, ALL, down)
    (back,) = call(
        second_kernel, [layers],
        [coefs, table, pair, matrix, fu, mask, ru, du, dp, q, send2, low2, high2, low, high],
        [((CH * BLOCKS * 8, LANES), bf16)],
        wide + [((RP, LANES), f32), ((BLOCKS, LANES, LANES), f32),
                ((CH * BLOCKS * 8, LANES), f32)],
    )
    home = lax.all_to_all(back.reshape(CH * BLOCKS, 8, LANES), PLANE, 0, 0, tiled=True)
    disp, pres = call(
        unpack_kernel, [], [home, fu_in, mask_in],
        [((ZL * BU * YL, LANES), f32), ((ZL * PB * YL, LANES), f32)],
        [((YL, BLOCKS, LANES, LANES), f32)],
    )
    return (disp.reshape(ZL, BU, YL, LANES), pres.reshape(ZL, PB, YL, LANES))


def solution(mesh):
    in_specs = (
        P("gz", None, "gy", "gx"),
        P("gz", None, "gy", "gx"),
        P("gz", "gy", "gx"),
        P("gz"),
        P(),
        P(),
        P(),
        P(),
        P(),
    )
    out_specs = (P("gz", None, "gy", "gx"), P("gz", None, "gy", "gx"))
    return jax.shard_map(body, mesh=mesh, in_specs=in_specs, out_specs=out_specs, check_vma=False)
```

```python
import jax
import jax.numpy as jnp
from jax import lax
from jax.experimental import pallas as pl
from jax.experimental.pallas import tpu as pltpu
from jax.sharding import PartitionSpec as P

SWEEPS = 4
ALL = ("gx", "gy", "gz")
PLANE = ("gy", "gz")
HIGHEST = lax.Precision.HIGHEST
NZ, BU, PB, NY = 16, 64, 16, 32
ZL, YL, XL, CH = 8, 2, 4, 32
RU, RP = NZ * BU, NZ * PB
HU, HP = ZL * BU, ZL * PB
WIDE = HU + HP
LANES = 128
BLOCKS = WIDE // LANES
PACKED = NZ * 3 // 4
STEP = 2 * BLOCKS * 8
UNROLL = {"wide": 16, "shrink": 16, "ring": 16, "own": 16}
f32, bf16 = jnp.float32, jnp.bfloat16


def place(variant, k):
    if variant == 0:
        cx, r = k // 8, k % 8
        cz = r if cx % 2 == 0 else 7 - r
    elif variant == 1:
        cz, r = k // 4, k % 4
        cx = 3 - r if cz % 2 == 0 else r
    elif variant == 2:
        q, r = k // 8, k % 8
        cx = 3 - q
        cz = 7 - r if q % 2 == 0 else r
    else:
        q, r = k // 4, k % 4
        cz = 7 - q
        cx = r if q % 2 == 0 else 3 - r
    return cx * 8 + cz


def slot_of(variant, k):
    a, b, c, d = (place(v, k) for v in range(4))
    return jnp.where(
        variant < 2, jnp.where(variant == 0, a, b), jnp.where(variant == 2, c, d)
    )


def ring():
    order = [g * CH + place(g % 4, k) for g in range(8) for k in range(CH)]
    up = [(order[i - 1], order[i]) for i in range(len(order))]
    return up, [(b, a) for a, b in up]


def at_end(group):
    plane = lax.axis_index("gy") + lax.axis_index("gz")
    return jnp.logical_and(lax.axis_index("gx") == group, plane == 0)


def pack_kernel(fu_hbm, fp_hbm, mask_hbm, out_ref, fu_ref, fp_ref, mask_ref, flip_ref, sem):
    part = 2 * BU * YL
    copies = [pltpu.make_async_copy(mask_hbm, mask_ref, sem.at[0])]
    for b in range(BLOCKS - 1):
        rows = pl.ds(b * part, part)
        copies.append(pltpu.make_async_copy(fu_hbm.at[rows], fu_ref.at[rows], sem.at[1 + b]))
    copies.append(pltpu.make_async_copy(fp_hbm, fp_ref, sem.at[BLOCKS]))
    for copy in copies:
        copy.start()
    copies[0].wait()
    variant = lax.axis_index("gx") % 4
    dests = [slot_of(variant, k) * BLOCKS for k in range(CH)]
    for b in range(BLOCKS):
        copies[1 + b].wait()
        for yl in range(YL):
            rows = []
            if b < BLOCKS - 1:
                for z in (2 * b, 2 * b + 1):
                    weight = (mask_ref[pl.ds(z * YL + yl, 1), :] != 0).astype(f32)
                    rows.append(fu_ref[pl.ds(z * BU * YL + yl, BU, stride=YL), :] * weight)
            else:
                last = lax.broadcasted_iota(jnp.int32, (PB, LANES), 0) == PB - 1
                for z in range(ZL):
                    weight = (mask_ref[pl.ds(z * YL + yl, 1), :] != 0).astype(f32)
                    fp = fp_ref[pl.ds(z * PB * YL + yl, PB, stride=YL), :] * weight
                    dead = jnp.broadcast_to(weight, (PB, LANES)) == 0.0
                    rows.append(jnp.where(jnp.logical_and(last, dead), jnp.inf, fp))
            flip_ref[yl, b] = jnp.concatenate(rows, axis=0).T
        for k in range(CH):
            out_ref[dests[k] + b] = jnp.concatenate(
                [flip_ref[yl, b, pl.ds(XL * k, XL), :] for yl in range(YL)], axis=0
            )


def spread_kernel(spec_ref, got_ref, fu_ref, fp_ref, mask_ref, send_ref, rows_ref):
    theta_inv = 1.0 / (jnp.full((1, LANES), spec_ref[1] + spec_ref[0], f32) / 2.0)
    for half in range(2):
        for b in range(BLOCKS):
            for x in range(XL):
                for yl in range(YL):
                    rows_ref[b, pl.ds(x * NY + yl, CH // 2, stride=YL), :] = got_ref[
                        pl.ds((half * BLOCKS + b) * 8 + yl * XL + x, CH // 2, stride=STEP), :
                    ]
            flat = rows_ref[b].T
            if b < BLOCKS - 1:
                at = pl.ds(half * HU + b * LANES, LANES)
                fu_ref[at, :] = flat
                send_ref[at, :] = (flat * theta_inv).astype(bf16)
            else:
                fp_ref[pl.ds(half * HP, HP), :] = flat
    marks = fp_ref[pl.ds(PB - 1, NZ, stride=PB), :]
    weight = jnp.where(marks == jnp.inf, 0.0, 1.0)
    mask_ref[...] = weight
    send_ref[pl.ds(RU, NZ), :] = weight.astype(bf16)
    fp_ref[...] = jnp.where(fp_ref[...] == jnp.inf, 0.0, fp_ref[...])


LOW, HIGH, OWN, EDGE = 0, 1, 2, 3
WIDTH = 4 * LANES


def block(b, count=1):
    return pl.ds(b * LANES, count * LANES)


def lane_of(rows):
    return lax.broadcasted_iota(jnp.int32, (rows, LANES), 1)


def edge_of(low, high):
    return jnp.where(lane_of(low.shape[0]) < LANES // 2, high, low)


def stack_of(z64, w_ref, mode):
    lane = lane_of(BU)
    y = lane % NY
    outs = {"wide": (LOW, HIGH, OWN), "shrink": (OWN, EDGE), "ring": (OWN, EDGE),
            "own": (OWN,)}[mode]
    rows = pl.ds(z64 + BU, BU)
    near = {"wide": (), "shrink": (LOW, HIGH), "ring": (), "own": (EDGE,)}[mode]
    part = {b: w_ref[rows, block(b)] for b in outs + near}
    zero = jnp.zeros_like(part[OWN])
    first, tail = lane < NY, lane >= LANES - NY
    if mode in ("wide", "ring"):
        up = {b: pltpu.roll(part[b], NY, 1) for b in outs}
        down = {b: pltpu.roll(part[b], LANES - NY, 1) for b in outs}
    if mode == "wide":
        below = {LOW: up[LOW], OWN: jnp.where(first, up[LOW], up[OWN]),
                 HIGH: jnp.where(first, up[OWN], up[HIGH])}
        above = {HIGH: down[HIGH], OWN: jnp.where(tail, down[HIGH], down[OWN]),
                 LOW: jnp.where(tail, down[OWN], down[LOW])}
    elif mode == "ring":
        below = {OWN: jnp.where(first, up[EDGE], up[OWN]), EDGE: jnp.where(first, up[OWN], up[EDGE])}
        above = {OWN: jnp.where(tail, down[EDGE], down[OWN]),
                 EDGE: jnp.where(tail, down[OWN], down[EDGE])}
    else:
        if mode == "shrink":
            under = {OWN: jnp.where(tail, part[LOW], part[OWN]),
                     EDGE: jnp.where(first, part[HIGH], jnp.where(tail, part[OWN], part[LOW]))}
            over = {OWN: jnp.where(first, part[HIGH], part[OWN]),
                    EDGE: jnp.where(first, part[OWN], jnp.where(tail, part[LOW], part[HIGH]))}
        else:
            under = {OWN: jnp.where(tail, part[EDGE], part[OWN])}
            over = {OWN: jnp.where(first, part[EDGE], part[OWN])}
        below = {b: pltpu.roll(under[b], NY, 1) for b in outs}
        above = {b: pltpu.roll(over[b], LANES - NY, 1) for b in outs}
    columns = []
    for b in outs:
        below_y = jnp.where(y == 0, zero, pltpu.roll(part[b], 1, 1))
        above_y = jnp.where(y == NY - 1, zero, pltpu.roll(part[b], LANES - 1, 1))
        columns.append(jnp.concatenate([below_y, above_y, below[b], above[b]], axis=0))
    depth = w_ref[pl.ds(z64, 3 * BU), block(outs[0], len(outs))]
    return [jnp.concatenate(columns, axis=1), depth]


def layers_of(group, unroll):
    return [group * unroll + i for i in range(unroll)]


def sweep(k, mode, begin, last, refs, old, new):
    unroll = UNROLL[mode]
    coef_ref, lm_ref, table_ref, mask_ref, state = refs
    count = {"wide": 3, "own": 1}.get(mode, 2)
    lanes = block(LOW if mode == "wide" else OWN, count)
    inner = block(0, min(count, 2))
    keep = coef_ref[pl.ds(2 + 2 * k, 1), block(0, count)]
    scale = coef_ref[pl.ds(3 + 2 * k, 1), block(0, count)]

    def group(g, carry):
        for z in layers_of(g, unroll):
            z64 = pl.multiple_of(z * BU, BU)
            table = table_ref[lm_ref[z]]
            stack = jnp.concatenate(stack_of(z64, old, mode), axis=0)
            product = jnp.dot(table[:, : 7 * BU], stack, preferred_element_type=f32)
            rows = pl.ds(z64, BU)
            if begin is None:
                r, d, s = [ref[rows, inner] for ref in state]
            else:
                r, d = begin(rows)
                s = d
            r = r - product * mask_ref[z, pl.ds(0, 1), lanes]
            d = keep * d + scale * r
            s = s + d
            if last is not None:
                last(z64, s)
                continue
            here = pl.ds(z64 + BU, BU)
            if mode == "wide":
                w = d.astype(bf16)
                new[here, block(LOW, 3)] = w
                new[here, block(EDGE)] = edge_of(w[:, :LANES], w[:, LANES : 2 * LANES])
                for ref, v in zip(state, (r, d, s)):
                    ref[rows, block(0)] = v[:, 2 * LANES :]
                    ref[rows, block(1)] = edge_of(v[:, :LANES], v[:, LANES : 2 * LANES])
            else:
                new[here, lanes] = d.astype(bf16)
                for ref, v in zip(state, (r, d, s)):
                    ref[rows, inner] = v
        return carry

    lax.fori_loop(0, NZ // unroll, group, 0)


def starter(coef_ref, own_ref, w_ref, wide):
    theta_inv = coef_ref[pl.ds(0, 1), block(0)]
    theta = coef_ref[pl.ds(1, 1), block(0)]

    def begin(rows):
        r = own_ref[rows, :]
        d = r * theta_inv
        here = pl.ds(rows.start + BU, BU)
        if wide:
            low = w_ref[here, block(LOW)].astype(f32)
            high = w_ref[here, block(HIGH)].astype(f32)
            return (
                jnp.concatenate([low * theta, high * theta, r], axis=1),
                jnp.concatenate([low, high, d], axis=1),
            )
        edge = w_ref[here, block(EDGE)].astype(f32)
        return (
            jnp.concatenate([r, edge * theta], axis=1),
            jnp.concatenate([d, edge], axis=1),
        )

    return begin


def widen(wide_ref, mask_ref, low_ref, high_ref):
    low = low_ref[pl.ds(RU, NZ), :].astype(f32) * jnp.where(at_end(0), 0.0, 1.0)
    high = high_ref[pl.ds(RU, NZ), :].astype(f32) * jnp.where(at_end(7), 0.0, 1.0)
    whole = jnp.concatenate([low, high, mask_ref[...], edge_of(low, high)], axis=1)
    for z in range(NZ):
        wide_ref[z] = jnp.broadcast_to(whole[z : z + 1], (8, WIDTH))


def unfold(z, src_ref, shifted):
    if z < PACKED:
        return src_ref[pl.ds(z * BU, BU), :]
    pieces = [src_ref[pl.ds((3 * (z - PACKED) + at) * BU, BU), :] for at in range(3)]
    if shifted:
        pieces = [pltpu.roll(p, NY * (at + 1), 1) for at, p in enumerate(pieces)]
        edges = (2 * NY, 3 * NY)
    else:
        pieces = [pltpu.roll(p, LANES - NY * (3 - at), 1) for at, p in enumerate(pieces)]
        edges = (NY, 2 * NY)
    lane = lane_of(BU)
    return jnp.where(lane < edges[0], pieces[0], jnp.where(lane < edges[1], pieces[1], pieces[2]))


def pad_in(w_refs, low_ref, high_ref, own_ref, with_edge):
    edge = jnp.zeros((BU, WIDTH), bf16)
    for w_ref in w_refs:
        w_ref[pl.ds(0, BU), :] = edge
        w_ref[pl.ds(RU + BU, BU), :] = edge
    for b, src in ((LOW, low_ref), (HIGH, high_ref), (OWN, own_ref)):
        if b != OWN and with_edge:
            for z in range(NZ):
                w_refs[0][pl.ds(z * BU + BU, BU), block(b)] = unfold(z, src, b == LOW)
        else:
            w_refs[0][pl.ds(BU, RU), block(b)] = src[pl.ds(0, RU), :]
    inner = pl.ds(BU, RU)
    for b, group in ((LOW, 0), (HIGH, 7)):

        @pl.when(at_end(group))
        def _():
            w_refs[0][inner, block(b)] = jnp.zeros((RU, LANES), bf16)

    if with_edge:
        w_refs[0][inner, block(EDGE)] = edge_of(
            w_refs[0][inner, block(LOW)], w_refs[0][inner, block(HIGH)]
        )


def thirds(v):
    high = v.astype(bf16)
    low = (v - high.astype(f32)).astype(bf16)
    return [high, low, high]


def halves(v):
    high = v.astype(bf16)
    return high, (v - high.astype(f32)).astype(bf16)


def couple(get, lm_ref, coup_ref, mask_ref, rest_ref, sign, q_ref):
    def group(g, carry):
        for z in layers_of(g, NZ):
            here = pl.ds(pl.multiple_of(z * PB, PB), PB)
            du = get(pl.multiple_of(z * BU, BU))
            q = jnp.dot(coup_ref[lm_ref[z]], jnp.concatenate(thirds(du), axis=0),
                        preferred_element_type=f32)
            q_ref[here, :] = q * mask_ref[z, pl.ds(0, 1), block(OWN)] + sign * rest_ref[here, :]
        return carry

    lax.fori_loop(0, 1, group, 0)


def bands(schur_ref, q_ref):
    return jnp.dot(schur_ref[...], jnp.concatenate(thirds(q_ref[...]), axis=0),
                   preferred_element_type=f32)


def prep_kernel(spec_ref, off_ref, kb_ref, coup_ref, sinv_ref,
                coef_ref, table_ref, pair_ref, band_ref):
    lower = jnp.full((1, WIDTH), spec_ref[0], f32)
    upper = jnp.full((1, WIDTH), spec_ref[1], f32)
    theta = (upper + lower) / 2.0
    delta = (upper - lower) / 2.0
    sigma = theta / delta
    rho = 1.0 / sigma
    coef_ref[pl.ds(0, 1), :] = 1.0 / theta
    coef_ref[pl.ds(1, 1), :] = theta
    for k in range(SWEEPS - 1):
        rho_next = 1.0 / (2.0 * sigma - rho)
        coef_ref[pl.ds(2 + 2 * k, 1), :] = rho_next * rho
        coef_ref[pl.ds(3 + 2 * k, 1), :] = 2.0 * rho_next / delta
        rho = rho_next
    for m in range(4):
        high, low = halves(coup_ref[m])
        pair_ref[m] = jnp.concatenate([high, high, low], axis=1)
        high, low = halves(coup_ref[m].T)
        blocks = [kb_ref[m, d] for d in (3, 4, 5, 6, 1, 0, 2)]
        pad = jnp.zeros((BU, PB), bf16)
        table_ref[m] = jnp.concatenate(blocks + [high, high, low, pad], axis=1)
    row = lax.broadcasted_iota(jnp.int32, (PB, RP), 0)
    col = lax.broadcasted_iota(jnp.int32, (PB, RP), 1)
    spread = (col % PB == row).astype(f32).astype(bf16)
    gap = (lax.broadcasted_iota(jnp.int32, (RP, RP), 1) // PB
           - lax.broadcasted_iota(jnp.int32, (RP, RP), 0) // PB)
    total = [jnp.zeros((RP, RP), f32)] * 2
    for k in range(8):
        hit = gap == off_ref[k]
        for i, part in enumerate(halves(sinv_ref[k].reshape(RP, PB))):
            wide = jnp.dot(part, spread, preferred_element_type=f32)
            total[i] = total[i] + jnp.where(hit, wide, 0.0)
    high, low = total[0].astype(bf16), total[1].astype(bf16)
    band_ref[...] = jnp.concatenate([high, high, low], axis=1)


def first_kernel(lm_ref, coef_ref, table_ref, coup_ref, schur_ref,
                 fu_ref, fp_ref, mask_ref, own_ref, low_ref, high_ref,
                 ru_ref, du_ref, dp_ref, q_ref, send_ref, up_ref, down_ref,
                 wide_ref, d_ref, r_ref, s_ref, wa_ref, wb_ref):
    widen(wide_ref, mask_ref, low_ref, high_ref)
    pad_in((wa_ref, wb_ref), low_ref, high_ref, own_ref, False)
    refs = (coef_ref, lm_ref, table_ref, wide_ref, (r_ref, d_ref, s_ref))
    begin = starter(coef_ref, fu_ref, wa_ref, True)

    def last(z64, s):
        wb_ref[pl.ds(z64 + BU, BU), block(OWN, 2)] = s.astype(bf16)
        du_ref[pl.ds(z64, BU), :] = s[:, :LANES]

    sweep(0, "wide", begin, None, refs, wa_ref, wb_ref)
    sweep(1, "shrink", None, None, refs, wb_ref, wa_ref)
    sweep(2, "ring", None, last, refs, wa_ref, wb_ref)
    couple(lambda z64: du_ref[pl.ds(z64, BU), :], lm_ref, coup_ref, wide_ref, fp_ref, -1.0, q_ref)
    dp_ref[...] = bands(schur_ref, q_ref)
    theta_inv = coef_ref[pl.ds(0, 1), block(0)]

    def finish(g, carry):
        for z in layers_of(g, 8):
            z64 = pl.multiple_of(z * BU, BU)
            here = pl.ds(pl.multiple_of(z * PB, PB), PB)
            weight = wide_ref[z, pl.ds(0, 1), block(OWN)]
            dp = dp_ref[here, :] * weight
            dp_ref[here, :] = dp
            stack = stack_of(z64, wb_ref, "own") + thirds(dp)
            product = jnp.dot(table_ref[lm_ref[z]][:, : 7 * BU + 3 * PB],
                              jnp.concatenate(stack, axis=0), preferred_element_type=f32)
            rows = pl.ds(z64, BU)
            ru = fu_ref[rows, :] - product * weight
            ru_ref[rows, :] = ru
            send_ref[rows, :] = (ru * theta_inv).astype(bf16)
        return carry

    lax.fori_loop(0, 2, finish, 0)
    lane = lane_of(BU)
    for z in range(PACKED):
        rows, spare = pl.ds(z * BU, BU), pl.ds((PACKED + z // 3) * BU, BU)
        mine, moved, at = send_ref[rows, :], send_ref[spare, :], z % 3
        up_ref[rows, :] = jnp.where(
            lane < NY, pltpu.roll(moved, LANES - NY * (at + 1), 1), mine
        )
        down_ref[rows, :] = jnp.where(
            lane >= 3 * NY, pltpu.roll(moved, NY * (3 - at), 1), mine
        )


def second_kernel(lm_ref, coef_ref, table_ref, coup_ref, schur_ref,
                  fu_ref, mask_ref, ru_ref, du_ref, dp_ref, q_ref, own_ref, low_ref,
                  high_ref, mlow_ref, mhigh_ref, out_ref,
                  wide_ref, d_ref, r_ref, s_ref, wa_ref, wb_ref, p_ref, rows_ref, sort_ref):
    widen(wide_ref, mask_ref, mlow_ref, mhigh_ref)
    pad_in((wa_ref, wb_ref), low_ref, high_ref, own_ref, True)
    refs = (coef_ref, lm_ref, table_ref, wide_ref, (r_ref, d_ref, s_ref))
    begin = starter(coef_ref, ru_ref, wa_ref, False)
    own = block(0)

    def last(z64, s):
        s_ref[pl.ds(z64, BU), own] = s

    sweep(0, "shrink", begin, None, refs, wa_ref, wb_ref)
    sweep(1, "ring", None, None, refs, wb_ref, wa_ref)
    sweep(2, "own", None, last, refs, wa_ref, wb_ref)
    couple(lambda z64: s_ref[pl.ds(z64, BU), own], lm_ref, coup_ref, wide_ref, q_ref, 1.0, p_ref)
    p_ref[...] = bands(schur_ref, p_ref)
    for half in range(2):
        for b in range(BLOCKS):
            if b < BLOCKS - 1:
                rows = pl.ds(half * HU + b * LANES, LANES)
                flat = s_ref[rows, own] + du_ref[rows, :] - fu_ref[rows, :]
            else:
                pressure = []
                for z in range(half * ZL, half * ZL + ZL):
                    here = pl.ds(z * PB, PB)
                    dp = p_ref[here, :] * mask_ref[pl.ds(z, 1), :]
                    pressure.append(dp + dp_ref[here, :])
                flat = jnp.concatenate(pressure, axis=0)
            rows_ref[b] = flat.T
            for x in range(XL):
                for yl in range(YL):
                    sort_ref[
                        pl.ds((half * BLOCKS + b) * 8 + yl * XL + x, CH // 2, stride=STEP), :
                    ] = rows_ref[b, pl.ds(x * NY + yl, CH // 2, stride=YL), :]
    out_ref[...] = sort_ref[...].astype(bf16)


def unpack_kernel(got_ref, fu_ref, mask_ref, disp_ref, pres_ref, rows_ref):
    variant = lax.axis_index("gx") % 4
    for k in range(CH):
        src = slot_of(variant, k) * BLOCKS
        for b in range(BLOCKS):
            piece = got_ref[src + b].astype(f32)
            for yl in range(YL):
                rows_ref[yl, b, pl.ds(XL * k, XL), :] = piece[yl * XL : yl * XL + XL]
    for yl in range(YL):
        for b in range(BLOCKS - 1):
            flat = rows_ref[yl, b].T
            for i in range(2):
                z = 2 * b + i
                weight = (mask_ref[pl.ds(z * YL + yl, 1), :] != 0).astype(f32)
                at = pl.ds(z * BU * YL + yl, BU, stride=YL)
                disp_ref[at, :] = flat[i * BU : i * BU + BU] + fu_ref[at, :] * weight
        pres_ref[pl.ds(yl, HP, stride=YL), :] = rows_ref[yl, BLOCKS - 1].T


VM = pl.BlockSpec(memory_space=pltpu.VMEM)
SM = pl.BlockSpec(memory_space=pltpu.SMEM)


def call(kernel, scalars, arrays, outs, scratch, limit=24):
    return pl.pallas_call(
        kernel,
        out_shape=[jax.ShapeDtypeStruct(*o) for o in outs],
        in_specs=[SM] * len(scalars) + [VM] * len(arrays),
        out_specs=[VM] * len(outs),
        scratch_shapes=[pltpu.VMEM(*s) for s in scratch],
        compiler_params=pltpu.CompilerParams(vmem_limit_bytes=limit << 20),
    )(*scalars, *arrays)


def body(force_u, force_p, cellmask, layer_mats, kblocks, bcoup, sinv, band_offsets, spectrum):
    up, down = ring()
    other = lax.ppermute(layer_mats, "gz", [(0, 1), (1, 0)])
    fu_in = force_u.reshape(ZL * BU * YL, LANES)
    fp_in = force_p.reshape(ZL * PB * YL, LANES)
    mask_in = cellmask.reshape(ZL * YL, LANES)
    packed = pl.pallas_call(
        pack_kernel,
        out_shape=jax.ShapeDtypeStruct((CH * BLOCKS, 8, LANES), f32),
        in_specs=[pl.BlockSpec(memory_space=pltpu.HBM)] * 3,
        out_specs=VM,
        scratch_shapes=[
            pltpu.VMEM(fu_in.shape, f32), pltpu.VMEM(fp_in.shape, f32),
            pltpu.VMEM(mask_in.shape, jnp.int32),
            pltpu.VMEM((YL, BLOCKS, LANES, LANES), f32), pltpu.SemaphoreType.DMA((BLOCKS + 1,)),
        ],
        compiler_params=pltpu.CompilerParams(vmem_limit_bytes=24 << 20),
    )(*(pltpu.with_memory_space_constraint(v, pltpu.HBM) for v in (fu_in, fp_in, mask_in)))
    packed, other = lax.optimization_barrier((packed, other))
    gz = lax.axis_index("gz")
    layers = jnp.where(
        gz == 0, jnp.concatenate([layer_mats, other]), jnp.concatenate([other, layer_mats])
    )
    got = lax.all_to_all(packed, PLANE, 0, 0, tiled=True)
    fu, fp, mask, send = call(
        spread_kernel, [spectrum], [got.reshape(CH * BLOCKS * 8, LANES)],
        [((RU, LANES), f32), ((RP, LANES), f32), ((NZ, LANES), f32), ((RU + NZ, LANES), bf16)],
        [((BLOCKS, LANES, LANES), f32)],
    )
    send, spectrum = lax.optimization_barrier((send, spectrum))
    coefs, table, pair, matrix = call(
        prep_kernel, [spectrum, band_offsets], [kblocks, bcoup, sinv],
        [((8, WIDTH), f32), ((4, BU, 8 * BU), bf16), ((4, PB, 3 * BU), bf16),
         ((RP, 3 * RP), bf16)], [],
    )
    low = lax.ppermute(send, ALL, up)
    high = lax.ppermute(send, ALL, down)
    wide = [((NZ, 8, WIDTH), f32)] + [((RU, 2 * LANES), f32)] * 3 + [
        ((RU + 2 * BU, WIDTH), bf16)
    ] * 2
    ru, du, dp, q, send2, up2, down2 = call(
        first_kernel, [layers],
        [coefs, table, pair, matrix, fu, fp, mask, send, low, high],
        [((RU, LANES), f32), ((RU, LANES), f32), ((RP, LANES), f32), ((RP, LANES), f32),
         ((RU, LANES), bf16), ((PACKED * BU, LANES), bf16), ((PACKED * BU, LANES), bf16)],
        wide,
    )
    low2 = lax.ppermute(up2, ALL, up)
    high2 = lax.ppermute(down2, ALL, down)
    (back,) = call(
        second_kernel, [layers],
        [coefs, table, pair, matrix, fu, mask, ru, du, dp, q, send2, low2, high2, low, high],
        [((CH * BLOCKS * 8, LANES), bf16)],
        wide + [((RP, LANES), f32), ((BLOCKS, LANES, LANES), f32),
                ((CH * BLOCKS * 8, LANES), f32)],
    )
    home = lax.all_to_all(back.reshape(CH * BLOCKS, 8, LANES), PLANE, 0, 0, tiled=True)
    disp, pres = call(
        unpack_kernel, [], [home, fu_in, mask_in],
        [((ZL * BU * YL, LANES), f32), ((ZL * PB * YL, LANES), f32)],
        [((YL, BLOCKS, LANES, LANES), f32)],
    )
    return (disp.reshape(ZL, BU, YL, LANES), pres.reshape(ZL, PB, YL, LANES))


def solution(mesh):
    in_specs = (
        P("gz", None, "gy", "gx"),
        P("gz", None, "gy", "gx"),
        P("gz", "gy", "gx"),
        P("gz"),
        P(),
        P(),
        P(),
        P(),
        P(),
    )
    out_specs = (P("gz", None, "gy", "gx"), P("gz", None, "gy", "gx"))
    return jax.shard_map(body, mesh=mesh, in_specs=in_specs, out_specs=out_specs, check_vma=False)
```

```python
import jax
import jax.numpy as jnp
from jax import lax
from jax.experimental import pallas as pl
from jax.experimental.pallas import tpu as pltpu
from jax.sharding import PartitionSpec as P

SWEEPS = 4
ALL = ("gx", "gy", "gz")
PLANE = ("gy", "gz")
HIGHEST = lax.Precision.HIGHEST
NZ, BU, PB, NY = 16, 64, 16, 32
ZL, YL, XL, CH = 8, 2, 4, 32
RU, RP = NZ * BU, NZ * PB
HU, HP = ZL * BU, ZL * PB
WIDE = HU + HP
LANES = 128
BLOCKS = WIDE // LANES
PACKED = NZ * 3 // 4
STEP = 2 * BLOCKS * 8
UNROLL = {"wide": 16, "shrink": 16, "ring": 16, "own": 16}
f32, bf16 = jnp.float32, jnp.bfloat16


def place(variant, k):
    if variant == 0:
        cx, r = k // 8, k % 8
        cz = r if cx % 2 == 0 else 7 - r
    elif variant == 1:
        cz, r = k // 4, k % 4
        cx = 3 - r if cz % 2 == 0 else r
    elif variant == 2:
        q, r = k // 8, k % 8
        cx = 3 - q
        cz = 7 - r if q % 2 == 0 else r
    else:
        q, r = k // 4, k % 4
        cz = 7 - q
        cx = r if q % 2 == 0 else 3 - r
    return cx * 8 + cz


def slot_of(variant, k):
    a, b, c, d = (place(v, k) for v in range(4))
    return jnp.where(
        variant < 2, jnp.where(variant == 0, a, b), jnp.where(variant == 2, c, d)
    )


def ring():
    order = [g * CH + place(g % 4, k) for g in range(8) for k in range(CH)]
    up = [(order[i - 1], order[i]) for i in range(len(order))]
    return up, [(b, a) for a, b in up]


def at_end(group):
    plane = lax.axis_index("gy") + lax.axis_index("gz")
    return jnp.logical_and(lax.axis_index("gx") == group, plane == 0)


def pack_kernel(fu_hbm, fp_hbm, mask_hbm, out_ref, fu_ref, fp_ref, mask_ref, flip_ref, sem):
    part = 2 * BU * YL
    copies = [pltpu.make_async_copy(mask_hbm, mask_ref, sem.at[0])]
    for b in range(BLOCKS - 1):
        rows = pl.ds(b * part, part)
        copies.append(pltpu.make_async_copy(fu_hbm.at[rows], fu_ref.at[rows], sem.at[1 + b]))
    copies.append(pltpu.make_async_copy(fp_hbm, fp_ref, sem.at[BLOCKS]))
    for copy in copies:
        copy.start()
    copies[0].wait()
    variant = lax.axis_index("gx") % 4
    dests = [slot_of(variant, k) * BLOCKS for k in range(CH)]
    for b in range(BLOCKS):
        copies[1 + b].wait()
        for yl in range(YL):
            rows = []
            if b < BLOCKS - 1:
                for z in (2 * b, 2 * b + 1):
                    weight = (mask_ref[pl.ds(z * YL + yl, 1), :] != 0).astype(f32)
                    rows.append(fu_ref[pl.ds(z * BU * YL + yl, BU, stride=YL), :] * weight)
            else:
                last = lax.broadcasted_iota(jnp.int32, (PB, LANES), 0) == PB - 1
                for z in range(ZL):
                    weight = (mask_ref[pl.ds(z * YL + yl, 1), :] != 0).astype(f32)
                    fp = fp_ref[pl.ds(z * PB * YL + yl, PB, stride=YL), :] * weight
                    dead = jnp.broadcast_to(weight, (PB, LANES)) == 0.0
                    rows.append(jnp.where(jnp.logical_and(last, dead), jnp.inf, fp))
            flip_ref[yl, b] = jnp.concatenate(rows, axis=0).T
        for k in range(CH):
            out_ref[dests[k] + b] = jnp.concatenate(
                [flip_ref[yl, b, pl.ds(XL * k, XL), :] for yl in range(YL)], axis=0
            )


def spread_kernel(spec_ref, got_ref, fu_ref, fp_ref, mask_ref, send_ref, rows_ref):
    theta = (spec_ref[:, 1:2] + spec_ref[:, 0:1]) / 2.0
    theta_inv = 1.0 / jnp.broadcast_to(theta, (1, LANES))
    for half in range(2):
        for b in range(BLOCKS):
            for x in range(XL):
                for yl in range(YL):
                    rows_ref[b, pl.ds(x * NY + yl, CH // 2, stride=YL), :] = got_ref[
                        pl.ds((half * BLOCKS + b) * 8 + yl * XL + x, CH // 2, stride=STEP), :
                    ]
            flat = rows_ref[b].T
            if b < BLOCKS - 1:
                at = pl.ds(half * HU + b * LANES, LANES)
                fu_ref[at, :] = flat
                send_ref[at, :] = (flat * theta_inv).astype(bf16)
            else:
                fp_ref[pl.ds(half * HP, HP), :] = flat
    marks = fp_ref[pl.ds(PB - 1, NZ, stride=PB), :]
    weight = jnp.where(marks == jnp.inf, 0.0, 1.0)
    mask_ref[...] = weight
    send_ref[pl.ds(RU, NZ), :] = weight.astype(bf16)
    fp_ref[...] = jnp.where(fp_ref[...] == jnp.inf, 0.0, fp_ref[...])


LOW, HIGH, OWN, EDGE = 0, 1, 2, 3
WIDTH = 4 * LANES


def block(b, count=1):
    return pl.ds(b * LANES, count * LANES)


def lane_of(rows):
    return lax.broadcasted_iota(jnp.int32, (rows, LANES), 1)


def edge_of(low, high):
    return jnp.where(lane_of(low.shape[0]) < LANES // 2, high, low)


def stack_of(z64, w_ref, mode):
    lane = lane_of(BU)
    y = lane % NY
    outs = {"wide": (LOW, HIGH, OWN), "shrink": (OWN, EDGE), "ring": (OWN, EDGE),
            "own": (OWN,)}[mode]
    rows = pl.ds(z64 + BU, BU)
    near = {"wide": (), "shrink": (LOW, HIGH), "ring": (), "own": (EDGE,)}[mode]
    part = {b: w_ref[rows, block(b)] for b in outs + near}
    zero = jnp.zeros_like(part[OWN])
    first, tail = lane < NY, lane >= LANES - NY
    if mode in ("wide", "ring"):
        up = {b: pltpu.roll(part[b], NY, 1) for b in outs}
        down = {b: pltpu.roll(part[b], LANES - NY, 1) for b in outs}
    if mode == "wide":
        below = {LOW: up[LOW], OWN: jnp.where(first, up[LOW], up[OWN]),
                 HIGH: jnp.where(first, up[OWN], up[HIGH])}
        above = {HIGH: down[HIGH], OWN: jnp.where(tail, down[HIGH], down[OWN]),
                 LOW: jnp.where(tail, down[OWN], down[LOW])}
    elif mode == "ring":
        below = {OWN: jnp.where(first, up[EDGE], up[OWN]), EDGE: jnp.where(first, up[OWN], up[EDGE])}
        above = {OWN: jnp.where(tail, down[EDGE], down[OWN]),
                 EDGE: jnp.where(tail, down[OWN], down[EDGE])}
    else:
        if mode == "shrink":
            under = {OWN: jnp.where(tail, part[LOW], part[OWN]),
                     EDGE: jnp.where(first, part[HIGH], jnp.where(tail, part[OWN], part[LOW]))}
            over = {OWN: jnp.where(first, part[HIGH], part[OWN]),
                    EDGE: jnp.where(first, part[OWN], jnp.where(tail, part[LOW], part[HIGH]))}
        else:
            under = {OWN: jnp.where(tail, part[EDGE], part[OWN])}
            over = {OWN: jnp.where(first, part[EDGE], part[OWN])}
        below = {b: pltpu.roll(under[b], NY, 1) for b in outs}
        above = {b: pltpu.roll(over[b], LANES - NY, 1) for b in outs}
    columns = []
    for b in outs:
        below_y = jnp.where(y == 0, zero, pltpu.roll(part[b], 1, 1))
        above_y = jnp.where(y == NY - 1, zero, pltpu.roll(part[b], LANES - 1, 1))
        columns.append(jnp.concatenate([below_y, above_y, below[b], above[b]], axis=0))
    depth = w_ref[pl.ds(z64, 3 * BU), block(outs[0], len(outs))]
    return [jnp.concatenate(columns, axis=1), depth]


def layers_of(group, unroll):
    return [group * unroll + i for i in range(unroll)]


def sweep(k, mode, begin, last, refs, old, new):
    unroll = UNROLL[mode]
    coef_ref, table_ref, mask_ref, state = refs
    count = {"wide": 3, "own": 1}.get(mode, 2)
    lanes = block(LOW if mode == "wide" else OWN, count)
    inner = block(0, min(count, 2))
    keep = coef_ref[pl.ds(2 + 2 * k, 1), block(0, count)]
    scale = coef_ref[pl.ds(3 + 2 * k, 1), block(0, count)]

    def group(g, carry):
        for z in layers_of(g, unroll):
            z64 = pl.multiple_of(z * BU, BU)
            table = table_ref[z]
            stack = jnp.concatenate(stack_of(z64, old, mode), axis=0)
            product = jnp.dot(table[:, : 7 * BU], stack, preferred_element_type=f32)
            rows = pl.ds(z64, BU)
            if begin is None:
                r, d, s = [ref[rows, inner] for ref in state]
            else:
                r, d = begin(rows)
                s = d
            r = r - product * mask_ref[z, pl.ds(0, 1), lanes]
            d = keep * d + scale * r
            s = s + d
            if last is not None:
                last(z64, s)
                continue
            here = pl.ds(z64 + BU, BU)
            if mode == "wide":
                w = d.astype(bf16)
                new[here, block(LOW, 3)] = w
                new[here, block(EDGE)] = edge_of(w[:, :LANES], w[:, LANES : 2 * LANES])
                for ref, v in zip(state, (r, d, s)):
                    ref[rows, block(0)] = v[:, 2 * LANES :]
                    ref[rows, block(1)] = edge_of(v[:, :LANES], v[:, LANES : 2 * LANES])
            else:
                new[here, lanes] = d.astype(bf16)
                for ref, v in zip(state, (r, d, s)):
                    ref[rows, inner] = v
        return carry

    lax.fori_loop(0, NZ // unroll, group, 0)


def starter(coef_ref, own_ref, w_ref, wide):
    theta_inv = coef_ref[pl.ds(0, 1), block(0)]
    theta = coef_ref[pl.ds(1, 1), block(0)]

    def begin(rows):
        r = own_ref[rows, :]
        d = r * theta_inv
        here = pl.ds(rows.start + BU, BU)
        if wide:
            low = w_ref[here, block(LOW)].astype(f32)
            high = w_ref[here, block(HIGH)].astype(f32)
            return (
                jnp.concatenate([low * theta, high * theta, r], axis=1),
                jnp.concatenate([low, high, d], axis=1),
            )
        edge = w_ref[here, block(EDGE)].astype(f32)
        return (
            jnp.concatenate([r, edge * theta], axis=1),
            jnp.concatenate([d, edge], axis=1),
        )

    return begin


def widen(wide_ref, mask_ref, low_ref, high_ref):
    low = low_ref[pl.ds(RU, NZ), :].astype(f32) * jnp.where(at_end(0), 0.0, 1.0)
    high = high_ref[pl.ds(RU, NZ), :].astype(f32) * jnp.where(at_end(7), 0.0, 1.0)
    whole = jnp.concatenate([low, high, mask_ref[...], edge_of(low, high)], axis=1)
    for z in range(NZ):
        wide_ref[z] = jnp.broadcast_to(whole[z : z + 1], (8, WIDTH))


def unfold(z, src_ref, shifted):
    if z < PACKED:
        return src_ref[pl.ds(z * BU, BU), :]
    pieces = [src_ref[pl.ds((3 * (z - PACKED) + at) * BU, BU), :] for at in range(3)]
    if shifted:
        pieces = [pltpu.roll(p, NY * (at + 1), 1) for at, p in enumerate(pieces)]
        edges = (2 * NY, 3 * NY)
    else:
        pieces = [pltpu.roll(p, LANES - NY * (3 - at), 1) for at, p in enumerate(pieces)]
        edges = (NY, 2 * NY)
    lane = lane_of(BU)
    return jnp.where(lane < edges[0], pieces[0], jnp.where(lane < edges[1], pieces[1], pieces[2]))


def pad_in(w_refs, low_ref, high_ref, own_ref, with_edge):
    edge = jnp.zeros((BU, WIDTH), bf16)
    for w_ref in w_refs:
        w_ref[pl.ds(0, BU), :] = edge
        w_ref[pl.ds(RU + BU, BU), :] = edge
    for b, src in ((LOW, low_ref), (HIGH, high_ref), (OWN, own_ref)):
        if b != OWN and with_edge:
            for z in range(NZ):
                w_refs[0][pl.ds(z * BU + BU, BU), block(b)] = unfold(z, src, b == LOW)
        else:
            w_refs[0][pl.ds(BU, RU), block(b)] = src[pl.ds(0, RU), :]
    inner = pl.ds(BU, RU)
    for b, group in ((LOW, 0), (HIGH, 7)):

        @pl.when(at_end(group))
        def _():
            w_refs[0][inner, block(b)] = jnp.zeros((RU, LANES), bf16)

    if with_edge:
        w_refs[0][inner, block(EDGE)] = edge_of(
            w_refs[0][inner, block(LOW)], w_refs[0][inner, block(HIGH)]
        )


def thirds(v):
    high = v.astype(bf16)
    low = (v - high.astype(f32)).astype(bf16)
    return [high, low, high]


def halves(v):
    high = v.astype(bf16)
    return high, (v - high.astype(f32)).astype(bf16)


def couple(get, coup_ref, mask_ref, rest_ref, sign, q_ref):
    def group(g, carry):
        for z in layers_of(g, NZ):
            here = pl.ds(pl.multiple_of(z * PB, PB), PB)
            du = get(pl.multiple_of(z * BU, BU))
            q = jnp.dot(coup_ref[z], jnp.concatenate(thirds(du), axis=0),
                        preferred_element_type=f32)
            q_ref[here, :] = q * mask_ref[z, pl.ds(0, 1), block(OWN)] + sign * rest_ref[here, :]
        return carry

    lax.fori_loop(0, 1, group, 0)


def bands(schur_ref, q_ref):
    return jnp.dot(schur_ref[...], jnp.concatenate(thirds(q_ref[...]), axis=0),
                   preferred_element_type=f32)


def prep_kernel(spec_ref, off_ref, lm_ref, kb_ref, coup_ref, sinv_ref,
                coef_ref, table_ref, pair_ref, band_ref, kinds_ref, pairs_ref):
    lower = jnp.full((1, WIDTH), spec_ref[0], f32)
    upper = jnp.full((1, WIDTH), spec_ref[1], f32)
    theta = (upper + lower) / 2.0
    delta = (upper - lower) / 2.0
    sigma = theta / delta
    rho = 1.0 / sigma
    coef_ref[pl.ds(0, 1), :] = 1.0 / theta
    coef_ref[pl.ds(1, 1), :] = theta
    for k in range(SWEEPS - 1):
        rho_next = 1.0 / (2.0 * sigma - rho)
        coef_ref[pl.ds(2 + 2 * k, 1), :] = rho_next * rho
        coef_ref[pl.ds(3 + 2 * k, 1), :] = 2.0 * rho_next / delta
        rho = rho_next
    for m in range(4):
        high, low = halves(coup_ref[m])
        pairs_ref[m] = jnp.concatenate([high, high, low], axis=1)
        high, low = halves(coup_ref[m].T)
        blocks = [kb_ref[m, d] for d in (3, 4, 5, 6, 1, 0, 2)]
        pad = jnp.zeros((BU, PB), bf16)
        kinds_ref[m] = jnp.concatenate(blocks + [high, high, low, pad], axis=1)
    for z in range(NZ):
        table_ref[z] = kinds_ref[lm_ref[z]]
        pair_ref[z] = pairs_ref[lm_ref[z]]
    row = lax.broadcasted_iota(jnp.int32, (PB, RP), 0)
    col = lax.broadcasted_iota(jnp.int32, (PB, RP), 1)
    spread = (col % PB == row).astype(f32).astype(bf16)
    gap = (lax.broadcasted_iota(jnp.int32, (RP, RP), 1) // PB
           - lax.broadcasted_iota(jnp.int32, (RP, RP), 0) // PB)
    total = [jnp.zeros((RP, RP), f32)] * 2
    for k in range(8):
        hit = gap == off_ref[k]
        for i, part in enumerate(halves(sinv_ref[k].reshape(RP, PB))):
            wide = jnp.dot(part, spread, preferred_element_type=f32)
            total[i] = total[i] + jnp.where(hit, wide, 0.0)
    high, low = total[0].astype(bf16), total[1].astype(bf16)
    band_ref[...] = jnp.concatenate([high, high, low], axis=1)


def first_kernel(coef_ref, table_ref, coup_ref, schur_ref,
                 fu_ref, fp_ref, mask_ref, own_ref, low_ref, high_ref,
                 ru_ref, du_ref, dp_ref, q_ref, send_ref, up_ref, down_ref,
                 wide_ref, d_ref, r_ref, s_ref, wa_ref, wb_ref):
    widen(wide_ref, mask_ref, low_ref, high_ref)
    pad_in((wa_ref, wb_ref), low_ref, high_ref, own_ref, False)
    refs = (coef_ref, table_ref, wide_ref, (r_ref, d_ref, s_ref))
    begin = starter(coef_ref, fu_ref, wa_ref, True)

    def last(z64, s):
        wb_ref[pl.ds(z64 + BU, BU), block(OWN, 2)] = s.astype(bf16)
        du_ref[pl.ds(z64, BU), :] = s[:, :LANES]

    sweep(0, "wide", begin, None, refs, wa_ref, wb_ref)
    sweep(1, "shrink", None, None, refs, wb_ref, wa_ref)
    sweep(2, "ring", None, last, refs, wa_ref, wb_ref)
    couple(lambda z64: du_ref[pl.ds(z64, BU), :], coup_ref, wide_ref, fp_ref, -1.0, q_ref)
    dp_ref[...] = bands(schur_ref, q_ref)
    theta_inv = coef_ref[pl.ds(0, 1), block(0)]

    def finish(g, carry):
        for z in layers_of(g, 8):
            z64 = pl.multiple_of(z * BU, BU)
            here = pl.ds(pl.multiple_of(z * PB, PB), PB)
            weight = wide_ref[z, pl.ds(0, 1), block(OWN)]
            dp = dp_ref[here, :] * weight
            dp_ref[here, :] = dp
            stack = stack_of(z64, wb_ref, "own") + thirds(dp)
            product = jnp.dot(table_ref[z][:, : 7 * BU + 3 * PB],
                              jnp.concatenate(stack, axis=0), preferred_element_type=f32)
            rows = pl.ds(z64, BU)
            ru = fu_ref[rows, :] - product * weight
            ru_ref[rows, :] = ru
            send_ref[rows, :] = (ru * theta_inv).astype(bf16)
        return carry

    lax.fori_loop(0, 2, finish, 0)
    lane = lane_of(BU)
    for z in range(PACKED):
        rows, spare = pl.ds(z * BU, BU), pl.ds((PACKED + z // 3) * BU, BU)
        mine, moved, at = send_ref[rows, :], send_ref[spare, :], z % 3
        up_ref[rows, :] = jnp.where(
            lane < NY, pltpu.roll(moved, LANES - NY * (at + 1), 1), mine
        )
        down_ref[rows, :] = jnp.where(
            lane >= 3 * NY, pltpu.roll(moved, NY * (3 - at), 1), mine
        )


def second_kernel(coef_ref, table_ref, coup_ref, schur_ref,
                  fu_ref, mask_ref, ru_ref, du_ref, dp_ref, q_ref, own_ref, low_ref,
                  high_ref, mlow_ref, mhigh_ref, out_ref,
                  wide_ref, d_ref, r_ref, s_ref, wa_ref, wb_ref, p_ref, rows_ref, sort_ref):
    widen(wide_ref, mask_ref, mlow_ref, mhigh_ref)
    pad_in((wa_ref, wb_ref), low_ref, high_ref, own_ref, True)
    refs = (coef_ref, table_ref, wide_ref, (r_ref, d_ref, s_ref))
    begin = starter(coef_ref, ru_ref, wa_ref, False)
    own = block(0)

    def last(z64, s):
        s_ref[pl.ds(z64, BU), own] = s

    sweep(0, "shrink", begin, None, refs, wa_ref, wb_ref)
    sweep(1, "ring", None, None, refs, wb_ref, wa_ref)
    sweep(2, "own", None, last, refs, wa_ref, wb_ref)
    couple(lambda z64: s_ref[pl.ds(z64, BU), own], coup_ref, wide_ref, q_ref, 1.0, p_ref)
    p_ref[...] = bands(schur_ref, p_ref)
    for half in range(2):
        for b in range(BLOCKS):
            if b < BLOCKS - 1:
                rows = pl.ds(half * HU + b * LANES, LANES)
                flat = s_ref[rows, own] + du_ref[rows, :] - fu_ref[rows, :]
            else:
                pressure = []
                for z in range(half * ZL, half * ZL + ZL):
                    here = pl.ds(z * PB, PB)
                    dp = p_ref[here, :] * mask_ref[pl.ds(z, 1), :]
                    pressure.append(dp + dp_ref[here, :])
                flat = jnp.concatenate(pressure, axis=0)
            rows_ref[b] = flat.T
            for x in range(XL):
                for yl in range(YL):
                    sort_ref[
                        pl.ds((half * BLOCKS + b) * 8 + yl * XL + x, CH // 2, stride=STEP), :
                    ] = rows_ref[b, pl.ds(x * NY + yl, CH // 2, stride=YL), :]
    out_ref[...] = sort_ref[...].astype(bf16)


def unpack_kernel(got_ref, fu_ref, mask_ref, disp_ref, pres_ref, rows_ref):
    variant = lax.axis_index("gx") % 4
    for k in range(CH):
        src = slot_of(variant, k) * BLOCKS
        for b in range(BLOCKS):
            piece = got_ref[src + b].astype(f32)
            for yl in range(YL):
                rows_ref[yl, b, pl.ds(XL * k, XL), :] = piece[yl * XL : yl * XL + XL]
    for yl in range(YL):
        for b in range(BLOCKS - 1):
            flat = rows_ref[yl, b].T
            for i in range(2):
                z = 2 * b + i
                weight = (mask_ref[pl.ds(z * YL + yl, 1), :] != 0).astype(f32)
                at = pl.ds(z * BU * YL + yl, BU, stride=YL)
                disp_ref[at, :] = flat[i * BU : i * BU + BU] + fu_ref[at, :] * weight
        pres_ref[pl.ds(yl, HP, stride=YL), :] = rows_ref[yl, BLOCKS - 1].T


VM = pl.BlockSpec(memory_space=pltpu.VMEM)
SM = pl.BlockSpec(memory_space=pltpu.SMEM)


def call(kernel, scalars, arrays, outs, scratch, limit=24):
    return pl.pallas_call(
        kernel,
        out_shape=[jax.ShapeDtypeStruct(*o) for o in outs],
        in_specs=[SM] * len(scalars) + [VM] * len(arrays),
        out_specs=[VM] * len(outs),
        scratch_shapes=[pltpu.VMEM(*s) for s in scratch],
        compiler_params=pltpu.CompilerParams(vmem_limit_bytes=limit << 20),
    )(*scalars, *arrays)


def body(force_u, force_p, cellmask, layer_mats, kblocks, bcoup, sinv, band_offsets, spectrum):
    up, down = ring()
    other = lax.ppermute(layer_mats, "gz", [(0, 1), (1, 0)])
    fu_in = force_u.reshape(ZL * BU * YL, LANES)
    fp_in = force_p.reshape(ZL * PB * YL, LANES)
    mask_in = cellmask.reshape(ZL * YL, LANES)
    packed = pl.pallas_call(
        pack_kernel,
        out_shape=jax.ShapeDtypeStruct((CH * BLOCKS, 8, LANES), f32),
        in_specs=[pl.BlockSpec(memory_space=pltpu.HBM)] * 3,
        out_specs=VM,
        scratch_shapes=[
            pltpu.VMEM(fu_in.shape, f32), pltpu.VMEM(fp_in.shape, f32),
            pltpu.VMEM(mask_in.shape, jnp.int32),
            pltpu.VMEM((YL, BLOCKS, LANES, LANES), f32), pltpu.SemaphoreType.DMA((BLOCKS + 1,)),
        ],
        compiler_params=pltpu.CompilerParams(vmem_limit_bytes=24 << 20),
    )(*(pltpu.with_memory_space_constraint(v, pltpu.HBM) for v in (fu_in, fp_in, mask_in)))
    packed, other = lax.optimization_barrier((packed, other))
    gz = lax.axis_index("gz")
    layers = jnp.where(
        gz == 0, jnp.concatenate([layer_mats, other]), jnp.concatenate([other, layer_mats])
    )
    got = lax.all_to_all(packed, PLANE, 0, 0, tiled=True)
    fu, fp, mask, send = call(
        spread_kernel, [], [spectrum.reshape(1, 2), got.reshape(CH * BLOCKS * 8, LANES)],
        [((RU, LANES), f32), ((RP, LANES), f32), ((NZ, LANES), f32), ((RU + NZ, LANES), bf16)],
        [((BLOCKS, LANES, LANES), f32)],
    )
    send, spectrum = lax.optimization_barrier((send, spectrum))
    coefs, table, pair, matrix = call(
        prep_kernel, [spectrum, band_offsets, layers], [kblocks, bcoup, sinv],
        [((8, WIDTH), f32), ((NZ, BU, 8 * BU), bf16), ((NZ, PB, 3 * BU), bf16),
         ((RP, 3 * RP), bf16)],
        [((4, BU, 8 * BU), bf16), ((4, PB, 3 * BU), bf16)],
    )
    low = lax.ppermute(send, ALL, up)
    high = lax.ppermute(send, ALL, down)
    wide = [((NZ, 8, WIDTH), f32)] + [((RU, 2 * LANES), f32)] * 3 + [
        ((RU + 2 * BU, WIDTH), bf16)
    ] * 2
    ru, du, dp, q, send2, up2, down2 = call(
        first_kernel, [],
        [coefs, table, pair, matrix, fu, fp, mask, send, low, high],
        [((RU, LANES), f32), ((RU, LANES), f32), ((RP, LANES), f32), ((RP, LANES), f32),
         ((RU, LANES), bf16), ((PACKED * BU, LANES), bf16), ((PACKED * BU, LANES), bf16)],
        wide,
    )
    low2 = lax.ppermute(up2, ALL, up)
    high2 = lax.ppermute(down2, ALL, down)
    (back,) = call(
        second_kernel, [],
        [coefs, table, pair, matrix, fu, mask, ru, du, dp, q, send2, low2, high2, low, high],
        [((CH * BLOCKS * 8, LANES), bf16)],
        wide + [((RP, LANES), f32), ((BLOCKS, LANES, LANES), f32),
                ((CH * BLOCKS * 8, LANES), f32)],
    )
    home = lax.all_to_all(back.reshape(CH * BLOCKS, 8, LANES), PLANE, 0, 0, tiled=True)
    disp, pres = call(
        unpack_kernel, [], [home, fu_in, mask_in],
        [((ZL * BU * YL, LANES), f32), ((ZL * PB * YL, LANES), f32)],
        [((YL, BLOCKS, LANES, LANES), f32)],
    )
    return (disp.reshape(ZL, BU, YL, LANES), pres.reshape(ZL, PB, YL, LANES))


def solution(mesh):
    in_specs = (
        P("gz", None, "gy", "gx"),
        P("gz", None, "gy", "gx"),
        P("gz", "gy", "gx"),
        P("gz"),
        P(),
        P(),
        P(),
        P(),
        P(),
    )
    out_specs = (P("gz", None, "gy", "gx"), P("gz", None, "gy", "gx"))
    return jax.shard_map(body, mesh=mesh, in_specs=in_specs, out_specs=out_specs, check_vma=False)
```

```python
import jax
import jax.numpy as jnp
from jax import lax
from jax.experimental import pallas as pl
from jax.experimental.pallas import tpu as pltpu
from jax.sharding import PartitionSpec as P

SWEEPS = 4
ALL = ("gx", "gy", "gz")
PLANE = ("gy", "gz")
HIGHEST = lax.Precision.HIGHEST
NZ, BU, PB, NY = 16, 64, 16, 32
ZL, YL, XL, CH = 8, 2, 4, 32
RU, RP = NZ * BU, NZ * PB
HU, HP = ZL * BU, ZL * PB
WIDE = HU + HP
LANES = 128
BLOCKS = WIDE // LANES
PACKED = NZ * 3 // 4
STEP = 2 * BLOCKS * 8
UNROLL = {"wide": 16, "shrink": 16, "ring": 16, "own": 16}
f32, bf16 = jnp.float32, jnp.bfloat16


def place(variant, k):
    if variant == 0:
        cx, r = k // 8, k % 8
        cz = r if cx % 2 == 0 else 7 - r
    elif variant == 1:
        cz, r = k // 4, k % 4
        cx = 3 - r if cz % 2 == 0 else r
    elif variant == 2:
        q, r = k // 8, k % 8
        cx = 3 - q
        cz = 7 - r if q % 2 == 0 else r
    else:
        q, r = k // 4, k % 4
        cz = 7 - q
        cx = r if q % 2 == 0 else 3 - r
    return cx * 8 + cz


def slot_of(variant, k):
    a, b, c, d = (place(v, k) for v in range(4))
    return jnp.where(
        variant < 2, jnp.where(variant == 0, a, b), jnp.where(variant == 2, c, d)
    )


def ring():
    order = [g * CH + place(g % 4, k) for g in range(8) for k in range(CH)]
    up = [(order[i - 1], order[i]) for i in range(len(order))]
    return up, [(b, a) for a, b in up]


def at_end(group):
    plane = lax.axis_index("gy") + lax.axis_index("gz")
    return jnp.logical_and(lax.axis_index("gx") == group, plane == 0)


def pack_kernel(fu_hbm, fp_hbm, mask_hbm, out_ref, fu_ref, fp_ref, mask_ref, flip_ref, sem):
    part = 2 * BU * YL
    copies = [pltpu.make_async_copy(mask_hbm, mask_ref, sem.at[0])]
    for b in range(BLOCKS - 1):
        rows = pl.ds(b * part, part)
        copies.append(pltpu.make_async_copy(fu_hbm.at[rows], fu_ref.at[rows], sem.at[1 + b]))
    copies.append(pltpu.make_async_copy(fp_hbm, fp_ref, sem.at[BLOCKS]))
    for copy in copies:
        copy.start()
    copies[0].wait()
    variant = lax.axis_index("gx") % 4
    dests = [slot_of(variant, k) * BLOCKS for k in range(CH)]
    for b in range(BLOCKS):
        copies[1 + b].wait()
        for yl in range(YL):
            rows = []
            if b < BLOCKS - 1:
                for z in (2 * b, 2 * b + 1):
                    weight = (mask_ref[pl.ds(z * YL + yl, 1), :] != 0).astype(f32)
                    rows.append(fu_ref[pl.ds(z * BU * YL + yl, BU, stride=YL), :] * weight)
            else:
                last = lax.broadcasted_iota(jnp.int32, (PB, LANES), 0) == PB - 1
                for z in range(ZL):
                    weight = (mask_ref[pl.ds(z * YL + yl, 1), :] != 0).astype(f32)
                    fp = fp_ref[pl.ds(z * PB * YL + yl, PB, stride=YL), :] * weight
                    dead = jnp.broadcast_to(weight, (PB, LANES)) == 0.0
                    rows.append(jnp.where(jnp.logical_and(last, dead), jnp.inf, fp))
            flip_ref[yl, b] = jnp.concatenate(rows, axis=0).T
        for k in range(CH):
            out_ref[dests[k] + b] = jnp.concatenate(
                [flip_ref[yl, b, pl.ds(XL * k, XL), :] for yl in range(YL)], axis=0
            )


def spread_kernel(spec_ref, got_ref, fu_ref, fp_ref, mask_ref, send_ref, rows_ref):
    theta = (spec_ref[:, 1:2] + spec_ref[:, 0:1]) / 2.0
    theta_inv = 1.0 / jnp.broadcast_to(theta, (1, LANES))
    for half in range(2):
        for b in range(BLOCKS):
            for x in range(XL):
                for yl in range(YL):
                    rows_ref[b, pl.ds(x * NY + yl, CH // 2, stride=YL), :] = got_ref[
                        pl.ds((half * BLOCKS + b) * 8 + yl * XL + x, CH // 2, stride=STEP), :
                    ]
            flat = rows_ref[b].T
            if b < BLOCKS - 1:
                at = pl.ds(half * HU + b * LANES, LANES)
                fu_ref[at, :] = flat
                send_ref[at, :] = (flat * theta_inv).astype(bf16)
            else:
                fp_ref[pl.ds(half * HP, HP), :] = flat
    marks = fp_ref[pl.ds(PB - 1, NZ, stride=PB), :]
    weight = jnp.where(marks == jnp.inf, 0.0, 1.0)
    mask_ref[...] = weight
    send_ref[pl.ds(RU, NZ), :] = weight.astype(bf16)
    fp_ref[...] = jnp.where(fp_ref[...] == jnp.inf, 0.0, fp_ref[...])


LOW, HIGH, OWN, EDGE = 0, 1, 2, 3
WIDTH = 4 * LANES


def block(b, count=1):
    return pl.ds(b * LANES, count * LANES)


def lane_of(rows):
    return lax.broadcasted_iota(jnp.int32, (rows, LANES), 1)


def edge_of(low, high):
    return jnp.where(lane_of(low.shape[0]) < LANES // 2, high, low)


def stack_of(z64, w_ref, mode):
    lane = lane_of(BU)
    y = lane % NY
    outs = {"wide": (LOW, HIGH, OWN), "shrink": (OWN, EDGE), "ring": (OWN, EDGE),
            "own": (OWN,)}[mode]
    rows = pl.ds(z64 + BU, BU)
    near = {"wide": (), "shrink": (LOW, HIGH), "ring": (), "own": (EDGE,)}[mode]
    part = {b: w_ref[rows, block(b)] for b in outs + near}
    zero = jnp.zeros_like(part[OWN])
    first, tail = lane < NY, lane >= LANES - NY
    if mode in ("wide", "ring"):
        up = {b: pltpu.roll(part[b], NY, 1) for b in outs}
        down = {b: pltpu.roll(part[b], LANES - NY, 1) for b in outs}
    if mode == "wide":
        below = {LOW: up[LOW], OWN: jnp.where(first, up[LOW], up[OWN]),
                 HIGH: jnp.where(first, up[OWN], up[HIGH])}
        above = {HIGH: down[HIGH], OWN: jnp.where(tail, down[HIGH], down[OWN]),
                 LOW: jnp.where(tail, down[OWN], down[LOW])}
    elif mode == "ring":
        below = {OWN: jnp.where(first, up[EDGE], up[OWN]), EDGE: jnp.where(first, up[OWN], up[EDGE])}
        above = {OWN: jnp.where(tail, down[EDGE], down[OWN]),
                 EDGE: jnp.where(tail, down[OWN], down[EDGE])}
    else:
        if mode == "shrink":
            under = {OWN: jnp.where(tail, part[LOW], part[OWN]),
                     EDGE: jnp.where(first, part[HIGH], jnp.where(tail, part[OWN], part[LOW]))}
            over = {OWN: jnp.where(first, part[HIGH], part[OWN]),
                    EDGE: jnp.where(first, part[OWN], jnp.where(tail, part[LOW], part[HIGH]))}
        else:
            under = {OWN: jnp.where(tail, part[EDGE], part[OWN])}
            over = {OWN: jnp.where(first, part[EDGE], part[OWN])}
        below = {b: pltpu.roll(under[b], NY, 1) for b in outs}
        above = {b: pltpu.roll(over[b], LANES - NY, 1) for b in outs}
    columns = []
    for b in outs:
        below_y = jnp.where(y == 0, zero, pltpu.roll(part[b], 1, 1))
        above_y = jnp.where(y == NY - 1, zero, pltpu.roll(part[b], LANES - 1, 1))
        columns.append(jnp.concatenate([below_y, above_y, below[b], above[b]], axis=0))
    depth = w_ref[pl.ds(z64, 3 * BU), block(outs[0], len(outs))]
    return [jnp.concatenate(columns, axis=1), depth]


def layers_of(group, unroll):
    return [group * unroll + i for i in range(unroll)]


def sweep(k, mode, begin, last, refs, old, new):
    unroll = UNROLL[mode]
    coef_ref, table_ref, mask_ref, state = refs
    count = {"wide": 3, "own": 1}.get(mode, 2)
    lanes = block(LOW if mode == "wide" else OWN, count)
    inner = block(0, min(count, 2))
    keep = coef_ref[pl.ds(2 + 2 * k, 1), block(0, count)]
    scale = coef_ref[pl.ds(3 + 2 * k, 1), block(0, count)]

    def group(g, carry):
        for z in layers_of(g, unroll):
            z64 = pl.multiple_of(z * BU, BU)
            table = table_ref[z]
            stack = jnp.concatenate(stack_of(z64, old, mode), axis=0)
            product = jnp.dot(table[:, : 7 * BU], stack, preferred_element_type=f32)
            rows = pl.ds(z64, BU)
            if begin is None:
                r, d, s = [ref[rows, inner] for ref in state]
            else:
                r, d = begin(rows)
                s = d
            r = r - product * mask_ref[z, pl.ds(0, 1), lanes]
            d = keep * d + scale * r
            s = s + d
            if last is not None:
                last(z64, s)
                continue
            here = pl.ds(z64 + BU, BU)
            if mode == "wide":
                w = d.astype(bf16)
                new[here, block(LOW, 3)] = w
                new[here, block(EDGE)] = edge_of(w[:, :LANES], w[:, LANES : 2 * LANES])
                for ref, v in zip(state, (r, d, s)):
                    ref[rows, block(0)] = v[:, 2 * LANES :]
                    ref[rows, block(1)] = edge_of(v[:, :LANES], v[:, LANES : 2 * LANES])
            else:
                new[here, lanes] = d.astype(bf16)
                for ref, v in zip(state, (r, d, s)):
                    ref[rows, inner] = v
        return carry

    lax.fori_loop(0, NZ // unroll, group, 0)


def starter(coef_ref, own_ref, w_ref, wide):
    theta_inv = coef_ref[pl.ds(0, 1), block(0)]
    theta = coef_ref[pl.ds(1, 1), block(0)]

    def begin(rows):
        r = own_ref[rows, :]
        d = r * theta_inv
        here = pl.ds(rows.start + BU, BU)
        if wide:
            low = w_ref[here, block(LOW)].astype(f32)
            high = w_ref[here, block(HIGH)].astype(f32)
            return (
                jnp.concatenate([low * theta, high * theta, r], axis=1),
                jnp.concatenate([low, high, d], axis=1),
            )
        edge = w_ref[here, block(EDGE)].astype(f32)
        return (
            jnp.concatenate([r, edge * theta], axis=1),
            jnp.concatenate([d, edge], axis=1),
        )

    return begin


def widen(wide_ref, mask_ref, low_ref, high_ref):
    low = low_ref[pl.ds(RU, NZ), :].astype(f32) * jnp.where(at_end(0), 0.0, 1.0)
    high = high_ref[pl.ds(RU, NZ), :].astype(f32) * jnp.where(at_end(7), 0.0, 1.0)
    whole = jnp.concatenate([low, high, mask_ref[...], edge_of(low, high)], axis=1)
    for z in range(NZ):
        wide_ref[z] = jnp.broadcast_to(whole[z : z + 1], (8, WIDTH))


def unfold(z, src_ref, shifted):
    if z < PACKED:
        return src_ref[pl.ds(z * BU, BU), :]
    pieces = [src_ref[pl.ds((3 * (z - PACKED) + at) * BU, BU), :] for at in range(3)]
    if shifted:
        pieces = [pltpu.roll(p, NY * (at + 1), 1) for at, p in enumerate(pieces)]
        edges = (2 * NY, 3 * NY)
    else:
        pieces = [pltpu.roll(p, LANES - NY * (3 - at), 1) for at, p in enumerate(pieces)]
        edges = (NY, 2 * NY)
    lane = lane_of(BU)
    return jnp.where(lane < edges[0], pieces[0], jnp.where(lane < edges[1], pieces[1], pieces[2]))


def pad_in(w_refs, low_ref, high_ref, own_ref, with_edge):
    edge = jnp.zeros((BU, WIDTH), bf16)
    for w_ref in w_refs:
        w_ref[pl.ds(0, BU), :] = edge
        w_ref[pl.ds(RU + BU, BU), :] = edge
    for b, src in ((LOW, low_ref), (HIGH, high_ref), (OWN, own_ref)):
        if b != OWN and with_edge:
            for z in range(NZ):
                w_refs[0][pl.ds(z * BU + BU, BU), block(b)] = unfold(z, src, b == LOW)
        else:
            w_refs[0][pl.ds(BU, RU), block(b)] = src[pl.ds(0, RU), :]
    inner = pl.ds(BU, RU)
    for b, group in ((LOW, 0), (HIGH, 7)):

        @pl.when(at_end(group))
        def _():
            w_refs[0][inner, block(b)] = jnp.zeros((RU, LANES), bf16)

    if with_edge:
        w_refs[0][inner, block(EDGE)] = edge_of(
            w_refs[0][inner, block(LOW)], w_refs[0][inner, block(HIGH)]
        )


def thirds(v):
    high = v.astype(bf16)
    low = (v - high.astype(f32)).astype(bf16)
    return [high, low, high]


def halves(v):
    high = v.astype(bf16)
    return high, (v - high.astype(f32)).astype(bf16)


def couple(get, coup_ref, mask_ref, rest_ref, sign, q_ref):
    def group(g, carry):
        for z in layers_of(g, NZ):
            here = pl.ds(pl.multiple_of(z * PB, PB), PB)
            du = get(pl.multiple_of(z * BU, BU))
            q = jnp.dot(coup_ref[z], jnp.concatenate(thirds(du), axis=0),
                        preferred_element_type=f32)
            q_ref[here, :] = q * mask_ref[z, pl.ds(0, 1), block(OWN)] + sign * rest_ref[here, :]
        return carry

    lax.fori_loop(0, 1, group, 0)


def bands(schur_ref, q_ref):
    return jnp.dot(schur_ref[...], jnp.concatenate(thirds(q_ref[...]), axis=0),
                   preferred_element_type=f32)


def prep_kernel(spec_ref, off_ref, lm_ref, kb_ref, coup_ref, sinv_ref,
                coef_ref, table_ref, pair_ref, band_ref, kinds_ref, pairs_ref):
    lower = jnp.full((1, WIDTH), spec_ref[0], f32)
    upper = jnp.full((1, WIDTH), spec_ref[1], f32)
    theta = (upper + lower) / 2.0
    delta = (upper - lower) / 2.0
    sigma = theta / delta
    rho = 1.0 / sigma
    coef_ref[pl.ds(0, 1), :] = 1.0 / theta
    coef_ref[pl.ds(1, 1), :] = theta
    for k in range(SWEEPS - 1):
        rho_next = 1.0 / (2.0 * sigma - rho)
        coef_ref[pl.ds(2 + 2 * k, 1), :] = rho_next * rho
        coef_ref[pl.ds(3 + 2 * k, 1), :] = 2.0 * rho_next / delta
        rho = rho_next
    for m in range(4):
        high, low = halves(coup_ref[m])
        pairs_ref[m] = jnp.concatenate([high, high, low], axis=1)
        high, low = halves(coup_ref[m].T)
        blocks = [kb_ref[m, d] for d in (3, 4, 5, 6, 1, 0, 2)]
        pad = jnp.zeros((BU, PB), bf16)
        kinds_ref[m] = jnp.concatenate(blocks + [high, high, low, pad], axis=1)
    for z in range(NZ):
        table_ref[z] = kinds_ref[lm_ref[z]]
        pair_ref[z] = pairs_ref[lm_ref[z]]
    row = lax.broadcasted_iota(jnp.int32, (PB, RP), 0)
    col = lax.broadcasted_iota(jnp.int32, (PB, RP), 1)
    spread = (col % PB == row).astype(f32).astype(bf16)
    gap = (lax.broadcasted_iota(jnp.int32, (RP, RP), 1) // PB
           - lax.broadcasted_iota(jnp.int32, (RP, RP), 0) // PB)
    total = [jnp.zeros((RP, RP), f32)] * 2
    for k in range(8):
        hit = gap == off_ref[k]
        for i, part in enumerate(halves(sinv_ref[k].reshape(RP, PB))):
            wide = jnp.dot(part, spread, preferred_element_type=f32)
            total[i] = total[i] + jnp.where(hit, wide, 0.0)
    high, low = total[0].astype(bf16), total[1].astype(bf16)
    band_ref[...] = jnp.concatenate([high, high, low], axis=1)


def first_kernel(coef_ref, table_ref, coup_ref, schur_ref,
                 fu_ref, fp_ref, mask_ref, own_ref, low_ref, high_ref,
                 ru_ref, du_ref, dp_ref, q_ref, send_ref, up_ref, down_ref, wide_ref,
                 d_ref, r_ref, s_ref, wa_ref, wb_ref):
    widen(wide_ref, mask_ref, low_ref, high_ref)
    pad_in((wa_ref, wb_ref), low_ref, high_ref, own_ref, False)
    refs = (coef_ref, table_ref, wide_ref, (r_ref, d_ref, s_ref))
    begin = starter(coef_ref, fu_ref, wa_ref, True)

    def last(z64, s):
        wb_ref[pl.ds(z64 + BU, BU), block(OWN, 2)] = s.astype(bf16)
        du_ref[pl.ds(z64, BU), :] = s[:, :LANES]

    sweep(0, "wide", begin, None, refs, wa_ref, wb_ref)
    sweep(1, "shrink", None, None, refs, wb_ref, wa_ref)
    sweep(2, "ring", None, last, refs, wa_ref, wb_ref)
    couple(lambda z64: du_ref[pl.ds(z64, BU), :], coup_ref, wide_ref, fp_ref, -1.0, q_ref)
    dp_ref[...] = bands(schur_ref, q_ref)
    theta_inv = coef_ref[pl.ds(0, 1), block(0)]

    def finish(g, carry):
        for z in layers_of(g, 8):
            z64 = pl.multiple_of(z * BU, BU)
            here = pl.ds(pl.multiple_of(z * PB, PB), PB)
            weight = wide_ref[z, pl.ds(0, 1), block(OWN)]
            dp = dp_ref[here, :] * weight
            dp_ref[here, :] = dp
            stack = stack_of(z64, wb_ref, "own") + thirds(dp)
            product = jnp.dot(table_ref[z][:, : 7 * BU + 3 * PB],
                              jnp.concatenate(stack, axis=0), preferred_element_type=f32)
            rows = pl.ds(z64, BU)
            ru = fu_ref[rows, :] - product * weight
            ru_ref[rows, :] = ru
            send_ref[rows, :] = (ru * theta_inv).astype(bf16)
        return carry

    lax.fori_loop(0, 2, finish, 0)
    lane = lane_of(BU)
    for z in range(PACKED):
        rows, spare = pl.ds(z * BU, BU), pl.ds((PACKED + z // 3) * BU, BU)
        mine, moved, at = send_ref[rows, :], send_ref[spare, :], z % 3
        up_ref[rows, :] = jnp.where(
            lane < NY, pltpu.roll(moved, LANES - NY * (at + 1), 1), mine
        )
        down_ref[rows, :] = jnp.where(
            lane >= 3 * NY, pltpu.roll(moved, NY * (3 - at), 1), mine
        )


def second_kernel(coef_ref, table_ref, coup_ref, schur_ref,
                  fu_ref, wide_ref, ru_ref, du_ref, dp_ref, q_ref, own_ref, low_ref,
                  high_ref, out_ref,
                  d_ref, r_ref, s_ref, wa_ref, wb_ref, p_ref, rows_ref, sort_ref):
    pad_in((wa_ref, wb_ref), low_ref, high_ref, own_ref, True)
    refs = (coef_ref, table_ref, wide_ref, (r_ref, d_ref, s_ref))
    begin = starter(coef_ref, ru_ref, wa_ref, False)
    own = block(0)

    def last(z64, s):
        s_ref[pl.ds(z64, BU), own] = s

    sweep(0, "shrink", begin, None, refs, wa_ref, wb_ref)
    sweep(1, "ring", None, None, refs, wb_ref, wa_ref)
    sweep(2, "own", None, last, refs, wa_ref, wb_ref)
    couple(lambda z64: s_ref[pl.ds(z64, BU), own], coup_ref, wide_ref, q_ref, 1.0, p_ref)
    p_ref[...] = bands(schur_ref, p_ref)
    for half in range(2):
        for b in range(BLOCKS):
            if b < BLOCKS - 1:
                rows = pl.ds(half * HU + b * LANES, LANES)
                flat = s_ref[rows, own] + du_ref[rows, :] - fu_ref[rows, :]
            else:
                pressure = []
                for z in range(half * ZL, half * ZL + ZL):
                    here = pl.ds(z * PB, PB)
                    dp = p_ref[here, :] * wide_ref[z, pl.ds(0, 1), block(OWN)]
                    pressure.append(dp + dp_ref[here, :])
                flat = jnp.concatenate(pressure, axis=0)
            rows_ref[b] = flat.T
            for x in range(XL):
                for yl in range(YL):
                    sort_ref[
                        pl.ds((half * BLOCKS + b) * 8 + yl * XL + x, CH // 2, stride=STEP), :
                    ] = rows_ref[b, pl.ds(x * NY + yl, CH // 2, stride=YL), :]
    out_ref[...] = sort_ref[...].astype(bf16)


def unpack_kernel(got_ref, fu_ref, mask_ref, disp_ref, pres_ref, rows_ref):
    variant = lax.axis_index("gx") % 4
    for k in range(CH):
        src = slot_of(variant, k) * BLOCKS
        for b in range(BLOCKS):
            piece = got_ref[src + b].astype(f32)
            for yl in range(YL):
                rows_ref[yl, b, pl.ds(XL * k, XL), :] = piece[yl * XL : yl * XL + XL]
    for yl in range(YL):
        for b in range(BLOCKS - 1):
            flat = rows_ref[yl, b].T
            for i in range(2):
                z = 2 * b + i
                weight = (mask_ref[pl.ds(z * YL + yl, 1), :] != 0).astype(f32)
                at = pl.ds(z * BU * YL + yl, BU, stride=YL)
                disp_ref[at, :] = flat[i * BU : i * BU + BU] + fu_ref[at, :] * weight
        pres_ref[pl.ds(yl, HP, stride=YL), :] = rows_ref[yl, BLOCKS - 1].T


VM = pl.BlockSpec(memory_space=pltpu.VMEM)
SM = pl.BlockSpec(memory_space=pltpu.SMEM)


def call(kernel, scalars, arrays, outs, scratch, limit=24):
    return pl.pallas_call(
        kernel,
        out_shape=[jax.ShapeDtypeStruct(*o) for o in outs],
        in_specs=[SM] * len(scalars) + [VM] * len(arrays),
        out_specs=[VM] * len(outs),
        scratch_shapes=[pltpu.VMEM(*s) for s in scratch],
        compiler_params=pltpu.CompilerParams(vmem_limit_bytes=limit << 20),
    )(*scalars, *arrays)


def body(force_u, force_p, cellmask, layer_mats, kblocks, bcoup, sinv, band_offsets, spectrum):
    up, down = ring()
    other = lax.ppermute(layer_mats, "gz", [(0, 1), (1, 0)])
    fu_in = force_u.reshape(ZL * BU * YL, LANES)
    fp_in = force_p.reshape(ZL * PB * YL, LANES)
    mask_in = cellmask.reshape(ZL * YL, LANES)
    packed = pl.pallas_call(
        pack_kernel,
        out_shape=jax.ShapeDtypeStruct((CH * BLOCKS, 8, LANES), f32),
        in_specs=[pl.BlockSpec(memory_space=pltpu.HBM)] * 3,
        out_specs=VM,
        scratch_shapes=[
            pltpu.VMEM(fu_in.shape, f32), pltpu.VMEM(fp_in.shape, f32),
            pltpu.VMEM(mask_in.shape, jnp.int32),
            pltpu.VMEM((YL, BLOCKS, LANES, LANES), f32), pltpu.SemaphoreType.DMA((BLOCKS + 1,)),
        ],
        compiler_params=pltpu.CompilerParams(vmem_limit_bytes=24 << 20),
    )(*(pltpu.with_memory_space_constraint(v, pltpu.HBM) for v in (fu_in, fp_in, mask_in)))
    packed, other = lax.optimization_barrier((packed, other))
    gz = lax.axis_index("gz")
    layers = jnp.where(
        gz == 0, jnp.concatenate([layer_mats, other]), jnp.concatenate([other, layer_mats])
    )
    got = lax.all_to_all(packed, PLANE, 0, 0, tiled=True)
    fu, fp, mask, send = call(
        spread_kernel, [], [spectrum.reshape(1, 2), got.reshape(CH * BLOCKS * 8, LANES)],
        [((RU, LANES), f32), ((RP, LANES), f32), ((NZ, LANES), f32), ((RU + NZ, LANES), bf16)],
        [((BLOCKS, LANES, LANES), f32)],
    )
    send, spectrum = lax.optimization_barrier((send, spectrum))
    coefs, table, pair, matrix = call(
        prep_kernel, [spectrum, band_offsets, layers], [kblocks, bcoup, sinv],
        [((8, WIDTH), f32), ((NZ, BU, 8 * BU), bf16), ((NZ, PB, 3 * BU), bf16),
         ((RP, 3 * RP), bf16)],
        [((4, BU, 8 * BU), bf16), ((4, PB, 3 * BU), bf16)],
    )
    low = lax.ppermute(send, ALL, up)
    high = lax.ppermute(send, ALL, down)
    wide = [((RU, 2 * LANES), f32)] * 3 + [
        ((RU + 2 * BU, WIDTH), bf16)
    ] * 2
    ru, du, dp, q, send2, up2, down2, live = call(
        first_kernel, [],
        [coefs, table, pair, matrix, fu, fp, mask, send, low, high],
        [((RU, LANES), f32), ((RU, LANES), f32), ((RP, LANES), f32), ((RP, LANES), f32),
         ((RU, LANES), bf16), ((PACKED * BU, LANES), bf16), ((PACKED * BU, LANES), bf16),
         ((NZ, 8, WIDTH), f32)],
        wide,
    )
    low2 = lax.ppermute(up2, ALL, up)
    high2 = lax.ppermute(down2, ALL, down)
    (back,) = call(
        second_kernel, [],
        [coefs, table, pair, matrix, fu, live, ru, du, dp, q, send2, low2, high2],
        [((CH * BLOCKS * 8, LANES), bf16)],
        wide + [((RP, LANES), f32), ((BLOCKS, LANES, LANES), f32),
                ((CH * BLOCKS * 8, LANES), f32)],
    )
    home = lax.all_to_all(back.reshape(CH * BLOCKS, 8, LANES), PLANE, 0, 0, tiled=True)
    disp, pres = call(
        unpack_kernel, [], [home, fu_in, mask_in],
        [((ZL * BU * YL, LANES), f32), ((ZL * PB * YL, LANES), f32)],
        [((YL, BLOCKS, LANES, LANES), f32)],
    )
    return (disp.reshape(ZL, BU, YL, LANES), pres.reshape(ZL, PB, YL, LANES))


def solution(mesh):
    in_specs = (
        P("gz", None, "gy", "gx"),
        P("gz", None, "gy", "gx"),
        P("gz", "gy", "gx"),
        P("gz"),
        P(),
        P(),
        P(),
        P(),
        P(),
    )
    out_specs = (P("gz", None, "gy", "gx"), P("gz", None, "gy", "gx"))
    return jax.shard_map(body, mesh=mesh, in_specs=in_specs, out_specs=out_specs, check_vma=False)
```
